256 devices in a mesh: atoms: 32 (over z_lo, x, core), waves: 8 (over z_hi, y).
Axes of the slice: x: 4, y: 4, z: 8 (z_hi: 2, z_lo: 4; z = z_hi * 4 + z_lo), core: 2. Of those that a mesh axis runs over, the one named last changes fastest.
Arguments:
- features: bfloat16 [64, 65536], P(None, 'atoms'), may hold values from -6 to 6
- coords: float32 [3, 65536], P(None, 'atoms'), may hold values from 0 to 1
- neighbours: int32 [27, 512], P(None, 'atoms'), may hold values from 0 to 511, as said below
- live_slots: int32 [27, 512], P(None, 'atoms'), may hold values 0 or 1
- block_count: int32 [32], P('atoms'), may hold values from 8 to 16, as said below
- kvec: int32 [3, 4096], P(None, 'waves'), may hold values from -64 to 64, as said below
- msg_weight: bfloat16 [1, 64, 64], replicated, may hold values from -0.75 to 0.75
- filter_weight: float32 [1, 64, 64], replicated, may hold values from -0.75 to 0.75
- mlp_in: bfloat16 [1, 128, 192], replicated, may hold values from -0.4375 to 0.4375
- mlp_out: bfloat16 [1, 64, 128], replicated, may hold values from -0.5 to 0.5
Outputs:
- updated: bfloat16 [64, 65536], P(None, 'atoms')
The draws below stay inside these ranges and needn't reach their ends.
Inputs may be any that keep to these rules, and one draw needn't show every extreme that they name: `neighbours`: entry [s, b] names a block slot whose index of atoms, slot // 16, equals b // 16 or lies one before or one after it, cyclically, and which is live. `block_count`: some index of atoms has all 16 of its slots live in every draw. `kvec`: rows 1 and 2 lie in -5 to 5; no column is zero in all three rows.
All inputs are finite; a program needn't handle non-finite values. No bound on the sum of `live_slots` on one device may be relied on, other than what follows from the above.
Results may differ from the reference program's by a relative error of at most 0.0062.
Values may be sent and summed in bfloat16 or wider, within the bound.
No kernel may reach another device: no remote copies, remote signals or barrier semaphores. Data moves between devices by JAX's collectives and lax.ppermute only.
A program may use at most 64 MiB of HBM per device.

```python
import math
import jax
import jax.numpy as jnp
from jax import lax

C = 64
K = 4096
HID = 128
BLOCK = 128
SLOTS = 27
LAYERS = 1
BCAP = 16
NBLOCKS = 512
NATOMS = 65536
N_ATOMS = 32


def counts_of(key):
    first, second = jax.random.split(jax.random.fold_in(key, 11))
    counts = jax.random.randint(first, (N_ATOMS,), BCAP // 2, BCAP + 1)
    fullest = jax.random.randint(second, (), 0, N_ATOMS)
    return jnp.where(jnp.arange(N_ATOMS) == fullest, BCAP, counts).astype(jnp.int32)


def draw_block_count(key, part):
    return counts_of(key)


def draw_neighbours(key, part):
    counts = counts_of(key)
    first, second = jax.random.split(jax.random.fold_in(key, 23))
    home = jnp.arange(N_ATOMS * BCAP, dtype=jnp.int32) // BCAP
    step = jax.random.randint(first, (SLOTS, N_ATOMS * BCAP), -1, 2)
    source = (home[None, :] + step) % N_ATOMS
    local = jax.random.randint(second, (SLOTS, N_ATOMS * BCAP), 0, counts[source])
    return (source * BCAP + local).astype(jnp.int32)


def draw_kvec(key, part):
    first, second, third = jax.random.split(jax.random.fold_in(key, 37), 3)
    along = jax.random.randint(first, (K,), -2 * N_ATOMS, 2 * N_ATOMS + 1)
    across = jax.random.randint(second, (K,), -5, 6)
    upward = jax.random.randint(third, (K,), -5, 6)
    zero = (along == 0) & (across == 0) & (upward == 0)
    upward = jnp.where(zero, 1, upward)
    return jnp.stack([along, across, upward]).astype(jnp.int32)


def draw_coords(key, part):
    total = N_ATOMS * BCAP * BLOCK
    unit = jax.random.uniform(jax.random.fold_in(key, 41), (3, total), jnp.float32)
    region = (jnp.arange(total) // (BCAP * BLOCK)).astype(jnp.float32)
    along = jnp.mod((region - 0.5 + 2.0 * unit[0]) / N_ATOMS, 1.0)
    along = jnp.minimum(along, 0.9999)
    return jnp.stack([along, unit[1], unit[2]]).astype(jnp.float32)


def place_ends(array, key, least, largest):
    longest = array.shape.index(max(array.shape))
    spots = []
    for shift in (0, 1):
        where = [jax.random.randint(jax.random.fold_in(key, axis), (), 0, length) for axis, length in enumerate(array.shape)]
        where[longest] = (where[longest] + shift) % array.shape[longest]
        spots.append(tuple(where))
    return array.at[spots[0]].set(least).at[spots[1]].set(largest)


def block_scale(own_key, extent, cuts, least, high):
    level = 1.0
    for dim, parts in cuts:
        steps = jax.random.uniform(jax.random.fold_in(jax.random.fold_in(own_key, 6), dim), (parts,), jnp.float32, least / len(cuts), high / len(cuts))
        level = level * jnp.repeat(jnp.exp(steps), extent[dim] // parts).reshape((-1,) + (1,) * (len(extent) - 1 - dim))
    return level


def normal_values(key, shape, scale, most, cuts=(), kind=jnp.bfloat16):
    array = scale * jax.random.normal(key, shape, jnp.float32)
    if cuts:
        array = array * block_scale(key, shape, cuts, -0.22, 0.18)
    return jnp.clip(array, -most, most).astype(kind)


def setup_inputs(seed: int = 0) -> dict:
    splits = jax.random.split(jax.random.key(seed), 11)
    features = normal_values(splits[0], (C, NATOMS), 1.0, 6.0, ((1, 32),))
    coords = draw_coords(jax.random.fold_in(splits[10], 71), 0)
    neighbours = draw_neighbours(jax.random.fold_in(splits[10], 71), 0)
    live_slots = place_ends((jax.random.randint(splits[3], (SLOTS, NBLOCKS), 0, 5) < 4).astype(jnp.int32), jax.random.fold_in(splits[3], 1), 0, 1)
    block_count = draw_block_count(jax.random.fold_in(splits[10], 71), 0)
    kvec = draw_kvec(jax.random.fold_in(splits[10], 71), 0)
    msg_weight = normal_values(splits[6], (LAYERS, C, C), C ** -0.5, 0.75)
    filter_weight = normal_values(splits[7], (LAYERS, C, C), C ** -0.5, 0.75, (), jnp.float32)
    mlp_in = normal_values(splits[8], (LAYERS, HID, 3 * C), (3 * C) ** -0.5, 0.4375)
    mlp_out = normal_values(splits[9], (LAYERS, C, HID), HID ** -0.5, 0.5)
    return dict(features=features, coords=coords, neighbours=neighbours, live_slots=live_slots, block_count=block_count, kvec=kvec, msg_weight=msg_weight, filter_weight=filter_weight, mlp_in=mlp_in, mlp_out=mlp_out)


TWO_PI = 6.283185307179586
MSG_SCALE = 0.125
GAIN_TOP = 20.0

def pair_weights(own, near, scale_x, live):
    total = None
    for axis in range(3):
        diff = own[axis][None, :, :, None] - near[axis][:, :, None, :]
        diff = diff - jnp.floor(diff + 0.5)
        if axis == 0:
            diff = diff * scale_x
        total = diff * diff if total is None else total + diff * diff
    return (jnp.exp(-2.0 * total) * live[:, :, None, None]).astype(jnp.bfloat16)

def phase_tables(kf_rows, coords_group):
    theta = TWO_PI * (kf_rows[0][:, None] * coords_group[0][None, :] + kf_rows[1][:, None] * coords_group[1][None, :] + kf_rows[2][:, None] * coords_group[2][None, :])
    return (jnp.cos(theta).astype(jnp.bfloat16), jnp.sin(theta).astype(jnp.bfloat16))

def short_range(hm, coords, neighbours, live_slots):
    chans = hm.shape[0]
    nbl = neighbours.shape[1]
    hm3 = hm.reshape(chans, nbl, BLOCK)
    pos3 = coords.reshape(3, nbl, BLOCK)

    def group(index):
        blocks = index * 2 + jnp.arange(2, dtype=jnp.int32)
        idx = neighbours[:, blocks]
        live = live_slots[:, blocks].astype(jnp.float32)
        weights = pair_weights(pos3[:, blocks], pos3[:, idx], N_ATOMS, live)
        near = hm3[:, idx]
        msg = jnp.einsum('csbj,sbij->cbi', near.astype(jnp.float32), weights.astype(jnp.float32))
        return (msg * MSG_SCALE).astype(jnp.bfloat16)
    out = lax.map(group, jnp.arange(nbl // 2, dtype=jnp.int32))
    return out.transpose(1, 0, 2, 3).reshape(chans, nbl * BLOCK)

def structure(kf, coords, masked):
    size = 4 * BLOCK
    groups = masked.shape[1] // size
    chans = masked.shape[0]
    dims = (((1,), (1,)), ((), ()))

    def step(acc, index):
        start = index * size
        pos = lax.dynamic_slice_in_dim(coords, start, size, 1)
        part = lax.dynamic_slice_in_dim(masked, start, size, 1)
        cosb, sinb = phase_tables(kf, pos)
        term = jnp.concatenate([lax.dot_general(cosb, part, dims, preferred_element_type=jnp.float32), lax.dot_general(sinb, part, dims, preferred_element_type=jnp.float32)], axis=1)
        return (acc + term, None)
    acc, _ = lax.scan(step, jnp.zeros((kf.shape[1], 2 * chans), jnp.float32), jnp.arange(groups, dtype=jnp.int32))
    return acc

def spectral(factor, gain, mixing, total):
    chans = mixing.shape[0]
    scaled = factor * (1.0 / math.sqrt(total))
    cos_part = jnp.dot(scaled[:, :chans], mixing, precision=lax.Precision.HIGHEST)
    sin_part = jnp.dot(scaled[:, chans:], mixing, precision=lax.Precision.HIGHEST)
    return (jnp.concatenate([cos_part, sin_part], axis=1) * gain[:, None]).astype(jnp.bfloat16)

def potentials(filtered, kf, coords):
    size = 4 * BLOCK
    chans = filtered.shape[1] // 2
    groups = coords.shape[1] // size
    dims = (((0,), (0,)), ((), ()))

    def step(carry, index):
        pos = lax.dynamic_slice_in_dim(coords, index * size, size, 1)
        cosb, sinb = phase_tables(kf, pos)
        term = lax.dot_general(filtered[:, :chans], cosb, dims, preferred_element_type=jnp.float32) + lax.dot_general(filtered[:, chans:], sinb, dims, preferred_element_type=jnp.float32)
        return (carry, term * (1.0 / math.sqrt(K)))
    _, out = lax.scan(step, 0, jnp.arange(groups, dtype=jnp.int32))
    return out.transpose(1, 0, 2).reshape(chans, groups * size)

def update(h, msg, potential, live, first_layer, second_layer):
    stacked = jnp.concatenate([h, msg, potential.astype(jnp.bfloat16)], axis=0)
    hidden = jax.nn.silu(jnp.dot(first_layer, stacked, preferred_element_type=jnp.float32)).astype(jnp.bfloat16)
    out = h.astype(jnp.float32) + jnp.dot(second_layer, hidden, preferred_element_type=jnp.float32)
    return jnp.where(live[None, :], out, jnp.zeros_like(out)).astype(jnp.bfloat16)

def reference(features, coords, neighbours, live_slots, block_count, kvec, msg_weight, filter_weight, mlp_in, mlp_out):
    nbl = BCAP * N_ATOMS
    total = nbl * BLOCK
    slot = jnp.arange(nbl, dtype=jnp.int32)
    live_block = slot % BCAP < block_count[slot // BCAP]
    live = jnp.repeat(live_block, BLOCK)
    kf = kvec.astype(jnp.float32)
    kx = kf[0] / N_ATOMS
    gain = GAIN_TOP / (4.0 + kx * kx + kf[1] * kf[1] + kf[2] * kf[2])
    h = features
    for layer in range(LAYERS):
        hm = jnp.dot(msg_weight[layer], h, preferred_element_type=jnp.float32).astype(jnp.bfloat16)
        msg = short_range(hm, coords, neighbours, live_slots)
        masked = jnp.where(live[None, :], h, jnp.zeros_like(h))
        factor = structure(kf, coords, masked)
        filtered = spectral(factor, gain, filter_weight[layer], total)
        potential = potentials(filtered, kf, coords)
        h = update(h, msg, potential, live, mlp_in[layer], mlp_out[layer])
    return h
```

```python
import functools
import math

import jax
import jax.numpy as jnp
from jax import lax
from jax.experimental import pallas as pl
from jax.experimental.pallas import tpu as pltpu
from jax.sharding import PartitionSpec as P

K = 4096
BLOCK = 128


TWO_PI = 6.283185307179586
MSG_SCALE = 0.125
GAIN_TOP = 20.0


def with_halo(cells, sides, width):
    for axis, dim in sides:
        count = lax.axis_size(axis)
        head = lax.slice_in_dim(cells, 0, width, axis=dim)
        tail = lax.slice_in_dim(cells, cells.shape[dim] - width, cells.shape[dim], axis=dim)
        cells = jnp.concatenate(
            [
                lax.ppermute(tail, axis, [(i, (i + 1) % count) for i in range(count)]),
                cells,
                lax.ppermute(head, axis, [((i + 1) % count, i) for i in range(count)]),
            ],
            axis=dim,
        )
    return cells


def laid_out(pieces, dim):
    lengths = list(pieces.shape[1:])
    lengths[dim] *= pieces.shape[0]
    return jnp.moveaxis(pieces, 0, dim).reshape(lengths)


def from_everyone(shard, axis):
    count = lax.axis_size(axis)
    return lax.all_to_all(
        jnp.broadcast_to(shard[None], (count, *shard.shape)), axis, 0, 0, tiled=True
    )


def gather_directly(shard, axis, dim):
    return laid_out(from_everyone(shard, axis), dim)


def pair_weights(own, near, scale_x, live):
    total = None
    for axis in range(3):
        diff = own[axis][None, :, :, None] - near[axis][:, :, None, :]
        diff = diff - jnp.floor(diff + 0.5)
        if axis == 0:
            diff = diff * scale_x
        total = diff * diff if total is None else total + diff * diff
    return (jnp.exp(-2.0 * total) * live[:, :, None, None]).astype(jnp.bfloat16)


def short_range(hm_ext, pos_ext, coords, ext_index, live_slots, first, count, scale_x):
    chans = hm_ext.shape[0]
    hm3 = hm_ext.reshape(chans, -1, BLOCK)
    pos3 = pos_ext.reshape(3, -1, BLOCK)
    own3 = coords.reshape(3, -1, BLOCK)

    def short_step(index, buffer):
        blocks = first + index * 2 + jnp.arange(2, dtype=jnp.int32)
        idx = jnp.take(ext_index, blocks, axis=1)
        live = jnp.take(live_slots, blocks, axis=1).astype(jnp.float32)
        weights = pair_weights(jnp.take(own3, blocks, axis=1), pos3[:, idx], scale_x, live)
        near = hm3[:, idx]
        msg = jnp.einsum("csbj,sbij->cbi", near, weights, preferred_element_type=jnp.float32)
        msg = (msg * MSG_SCALE).astype(jnp.bfloat16).reshape(chans, 2 * BLOCK)
        return msg

    return lax.fori_loop(0, count // 2, short_step, jnp.zeros((chans, count * BLOCK), jnp.bfloat16))


SIN_COEFS = (3.1415926401307073, -5.167710083507923, 2.5500775232148563, -0.5982912856211671, 0.07765766030589402)
COS_COEFS = (0.9999999532476085, -4.934792830619664, 4.058411352862771, -1.3318765680813944, 0.21968961109803095)
ROOT2 = math.sqrt(2.0)
VMEM_SPEC = pl.BlockSpec(memory_space=pltpu.VMEM)


def horner(coefs, scale, u):
    value = coefs[-1] * scale
    for coef in coefs[-2::-1]:
        value = value * u + coef * scale
    return value


def phases_of(turns):
    r = turns - jnp.round(turns)
    u = r * r
    s = r * horner(SIN_COEFS, ROOT2, u)
    c = horner(COS_COEFS, ROOT2, u)
    return 1.0 - s * s, s * c


def three_pieces(values):
    first = values.astype(jnp.bfloat16)
    rest = values - first.astype(jnp.float32)
    second = rest.astype(jnp.bfloat16)
    third = (rest - second.astype(jnp.float32)).astype(jnp.bfloat16)
    return first.astype(jnp.float32), second.astype(jnp.float32), third.astype(jnp.float32)


def structure_kernel(tile, kf_ref, coords_ref, h_ref, count_ref, table_ref, out_ref, ka_ref, xs_ref):
    waves = kf_ref.shape[1]
    atoms = coords_ref.shape[1]
    chans = h_ref.shape[0]
    kf = kf_ref[...].astype(jnp.float32)
    pad_k = jnp.zeros((7, waves), jnp.float32)
    ka = jnp.concatenate([kf, kf, kf, pad_k], axis=0)
    ka_ref[...] = ka.T.astype(jnp.bfloat16)
    first, second, third = three_pieces(coords_ref[...])
    xs = jnp.concatenate([first, second, third, jnp.zeros((7, atoms), jnp.float32)], axis=0)
    xs_ref[...] = xs.astype(jnp.bfloat16)
    live_atoms = count_ref[0] * BLOCK
    rows = 64
    acc = jnp.zeros((waves, 2 * chans), jnp.float32)
    nt = (((1,), (1,)), ((), ()))
    for start in range(0, atoms, tile):
        xt = xs_ref[:, start : start + tile]
        for k in range(0, waves, rows):
            turns = jnp.dot(ka_ref[k : k + rows, :], xt, preferred_element_type=jnp.float32)
            cosv, sinv = phases_of(turns)
            table_ref[k : k + rows, start : start + tile] = cosv.astype(jnp.bfloat16)
            table_ref[k : k + rows, atoms + start : atoms + start + tile] = sinv.astype(jnp.bfloat16)
        lane = lax.broadcasted_iota(jnp.int32, (chans, tile), 1) + start
        ht = jnp.where(lane < live_atoms, h_ref[:, start : start + tile].astype(jnp.float32), 0.0)
        zero = jnp.zeros_like(ht)
        hc = jnp.concatenate([ht, zero], axis=0).astype(jnp.bfloat16)
        hs = jnp.concatenate([zero, ht], axis=0).astype(jnp.bfloat16)
        acc = acc + lax.dot_general(table_ref[:, start : start + tile], hc, nt, preferred_element_type=jnp.float32)
        acc = acc + lax.dot_general(
            table_ref[:, atoms + start : atoms + start + tile], hs, nt, preferred_element_type=jnp.float32
        )
    out_ref[...] = acc.astype(jnp.bfloat16).reshape(out_ref.shape)


def structure(kvec, coords, h, count, pieces):
    waves, atoms, chans = kvec.shape[1], coords.shape[1], h.shape[0]
    return pl.pallas_call(
        functools.partial(structure_kernel, 256),
        out_shape=(
            jax.ShapeDtypeStruct((waves, 2 * atoms), jnp.bfloat16),
            jax.ShapeDtypeStruct((pieces, waves // pieces, 2 * chans), jnp.bfloat16),
        ),
        in_specs=[VMEM_SPEC, VMEM_SPEC, VMEM_SPEC, pl.BlockSpec(memory_space=pltpu.SMEM)],
        out_specs=(VMEM_SPEC, VMEM_SPEC),
        scratch_shapes=[pltpu.VMEM((waves, 16), jnp.bfloat16), pltpu.VMEM((16, atoms), jnp.bfloat16)],
        name="structure",
    )(kvec, coords, h, count)


def potentials_kernel(filtered_ref, table_ref, out_ref):
    chans = out_ref.shape[1]
    pieces, _, width = out_ref.shape
    atoms = pieces * width
    tn = (((0,), (0,)), ((), ()))
    fc = filtered_ref[:, :chans]
    fs = filtered_ref[:, chans:]
    for piece in range(pieces):
        start = piece * width
        term = lax.dot_general(
            fc, table_ref[:, start : start + width], tn, preferred_element_type=jnp.float32
        ) + lax.dot_general(
            fs, table_ref[:, atoms + start : atoms + start + width], tn, preferred_element_type=jnp.float32
        )
        out_ref[piece] = (term * (1.0 / math.sqrt(K))).astype(jnp.bfloat16)


def potentials(filtered, table, pieces):
    chans = filtered.shape[1] // 2
    atoms = table.shape[1] // 2
    return pl.pallas_call(
        potentials_kernel,
        out_shape=jax.ShapeDtypeStruct((pieces, chans, atoms // pieces), jnp.bfloat16),
        in_specs=[VMEM_SPEC, VMEM_SPEC],
        out_specs=VMEM_SPEC,
        name="potentials",
    )(filtered, table)


def spectral(factor, gain, mixing, total):
    chans = mixing.shape[0]
    scaled = factor * (1.0 / math.sqrt(total))
    cos_part = jnp.dot(scaled[:, :chans], mixing, precision=lax.Precision.HIGHEST)
    sin_part = jnp.dot(scaled[:, chans:], mixing, precision=lax.Precision.HIGHEST)
    return (jnp.concatenate([cos_part, sin_part], axis=1) * gain[:, None]).astype(jnp.bfloat16)


def update(h, msg, potential, live, first_layer, second_layer):
    stacked = jnp.concatenate([h, msg, potential.astype(jnp.bfloat16)], axis=0)
    hidden = jax.nn.silu(jnp.dot(first_layer, stacked, preferred_element_type=jnp.float32)).astype(
        jnp.bfloat16
    )
    out = h.astype(jnp.float32) + jnp.dot(second_layer, hidden, preferred_element_type=jnp.float32)
    return jnp.where(live[None, :], out, jnp.zeros_like(out)).astype(jnp.bfloat16)


def local(
    features,
    coords,
    neighbours,
    live_slots,
    block_count,
    kvec,
    msg_weight,
    filter_weight,
    mlp_in,
    mlp_out,
):
    width = features.shape[1]
    nblocks = width // BLOCK
    regions = lax.axis_size("atoms")
    groups_waves = lax.axis_size("waves")
    here = lax.axis_index("atoms")
    total = regions * width
    source = neighbours // nblocks
    offset = (source - here) % regions
    which = jnp.where(offset == 0, 1, jnp.where(offset == 1, 2, 0))
    ext_index = which * nblocks + neighbours % nblocks
    live_block = jnp.arange(nblocks, dtype=jnp.int32) < block_count[0]
    live = jnp.repeat(live_block, BLOCK)
    kf = kvec.astype(jnp.float32)
    kx = kf[0] / regions
    gain = GAIN_TOP / (4.0 + kx * kx + kf[1] * kf[1] + kf[2] * kf[2])
    wave_rows = kf.shape[1]
    pos_ext = with_halo(coords, (("atoms", 1),), width)
    h = features
    hm = jnp.dot(msg_weight[0], h, preferred_element_type=jnp.float32).astype(jnp.bfloat16)
    hm_ext = with_halo(hm, (("atoms", 1),), width)
    owned = wave_rows // regions
    table, partial_factor = structure(kvec, coords, h, block_count, regions)
    arrived = lax.all_to_all(partial_factor, "atoms", 0, 0, tiled=True)
    share = arrived.astype(jnp.float32).sum(axis=0)
    gain_share = lax.dynamic_slice_in_dim(gain, here * owned, owned, 0)
    filtered_share = spectral(share, gain_share, filter_weight[0], total)
    filtered = gather_directly(filtered_share, "atoms", 0)
    partial_potential = potentials(filtered, table, groups_waves)
    per_group = nblocks // groups_waves
    first = lax.axis_index("waves") * per_group
    potential = lax.all_to_all(partial_potential, "waves", 0, 0, tiled=True).astype(jnp.float32).sum(axis=0)
    msg = short_range(hm_ext, pos_ext, coords, ext_index, live_slots, first, per_group, regions)
    h_share = lax.dynamic_slice_in_dim(h, first * BLOCK, per_group * BLOCK, 1)
    live_share = lax.dynamic_slice_in_dim(live, first * BLOCK, per_group * BLOCK, 0)
    new_share = update(h_share, msg, potential, live_share, mlp_in[0], mlp_out[0])
    h = gather_directly(new_share, "waves", 1)
    return h


def solution(mesh):
    in_specs = (
        P(None, "atoms"),
        P(None, "atoms"),
        P(None, "atoms"),
        P(None, "atoms"),
        P("atoms"),
        P(None, "waves"),
        P(),
        P(),
        P(),
        P(),
    )
    out_specs = P(None, "atoms")
    return jax.shard_map(local, mesh=mesh, in_specs=in_specs, out_specs=out_specs, check_vma=False)
```

```python
import functools
import math

import jax
import jax.numpy as jnp
from jax import lax
from jax.experimental import pallas as pl
from jax.experimental.pallas import tpu as pltpu
from jax.sharding import PartitionSpec as P


K = 4096
BLOCK = 128


MSG_SCALE = 0.125
GAIN_TOP = 20.0


def with_halo(cells, sides, width):
    for axis, dim in sides:
        count = lax.axis_size(axis)
        head = lax.slice_in_dim(cells, 0, width, axis=dim)
        tail = lax.slice_in_dim(cells, cells.shape[dim] - width, cells.shape[dim], axis=dim)
        cells = jnp.concatenate(
            [
                lax.ppermute(tail, axis, [(i, (i + 1) % count) for i in range(count)]),
                cells,
                lax.ppermute(head, axis, [((i + 1) % count, i) for i in range(count)]),
            ],
            axis=dim,
        )
    return cells


def laid_out(pieces, dim):
    lengths = list(pieces.shape[1:])
    lengths[dim] *= pieces.shape[0]
    return jnp.moveaxis(pieces, 0, dim).reshape(lengths)


def pair_weights(own, near, scale_x, live):
    total = None
    for axis in range(3):
        diff = own[axis][None, :, :, None] - near[axis][:, :, None, :]
        diff = diff - jnp.floor(diff + 0.5)
        if axis == 0:
            diff = diff * scale_x
        total = diff * diff if total is None else total + diff * diff
    return (jnp.exp(-2.0 * total) * live[:, :, None, None]).astype(jnp.bfloat16)


def short_range(hm_ext, pos_ext, coords, ext_index, live_slots, first, count, scale_x):
    chans = hm_ext.shape[0]
    hm3 = hm_ext.reshape(chans, -1, BLOCK)
    pos3 = pos_ext.reshape(3, -1, BLOCK)
    own3 = coords.reshape(3, -1, BLOCK)

    def short_step(index, buffer):
        blocks = first + index * 2 + jnp.arange(2, dtype=jnp.int32)
        idx = jnp.take(ext_index, blocks, axis=1)
        live = jnp.take(live_slots, blocks, axis=1).astype(jnp.float32)
        weights = pair_weights(jnp.take(own3, blocks, axis=1), pos3[:, idx], scale_x, live)
        near = hm3[:, idx]
        msg = jnp.einsum("csbj,sbij->cbi", near, weights, preferred_element_type=jnp.float32)
        msg = (msg * MSG_SCALE).astype(jnp.bfloat16).reshape(chans, 2 * BLOCK)
        return msg

    return lax.fori_loop(0, count // 2, short_step, jnp.zeros((chans, count * BLOCK), jnp.bfloat16))


SIN_COEFS = (3.1415926401307073, -5.167710083507923, 2.5500775232148563, -0.5982912856211671, 0.07765766030589402)
COS_COEFS = (0.9999999532476085, -4.934792830619664, 4.058411352862771, -1.3318765680813944, 0.21968961109803095)
ROOT2 = math.sqrt(2.0)
LIMIT = 16 * 2**20
WIDE_LIMIT = 62 * 10**6
TILE = 256
ANY_SPEC = pl.BlockSpec(memory_space=pl.ANY)
VMEM_SPEC = pl.BlockSpec(memory_space=pltpu.VMEM)


def horner(coefs, scale, u):
    value = coefs[-1] * scale
    for coef in coefs[-2::-1]:
        value = value * u + coef * scale
    return value


def phases_of(turns):
    r = turns - jnp.round(turns)
    u = r * r
    s = r * horner(SIN_COEFS, ROOT2, u)
    c = horner(COS_COEFS, ROOT2, u)
    return 1.0 - s * s, s * c


def three_pieces(values):
    first = values.astype(jnp.bfloat16)
    rest = values - first.astype(jnp.float32)
    second = rest.astype(jnp.bfloat16)
    third = (rest - second.astype(jnp.float32)).astype(jnp.bfloat16)
    return first.astype(jnp.float32), second.astype(jnp.float32), third.astype(jnp.float32)


def structure_kernel(
    tile,
    kf_ref,
    coords_ref,
    h_ref,
    weight_ref,
    count_ref,
    stored_ref,
    out_ref,
    carry_ref,
    ka_ref,
    xs_ref,
    table_ref,
    sems,
):
    waves = kf_ref.shape[1]
    atoms = coords_ref.shape[1]
    chans = h_ref.shape[0]
    kf = kf_ref[...].astype(jnp.float32)
    pad_k = jnp.zeros((7, waves), jnp.float32)
    ka = jnp.concatenate([kf, kf, kf, pad_k], axis=0)
    ka_ref[...] = ka.T.astype(jnp.bfloat16)
    first, second, third = three_pieces(coords_ref[...])
    xs = jnp.concatenate([first, second, third, jnp.zeros((7, atoms), jnp.float32)], axis=0)
    xs_ref[...] = xs.astype(jnp.bfloat16)
    live_atoms = count_ref[0] * BLOCK
    rows = 64
    acc = jnp.zeros((waves, 2 * chans), jnp.float32)
    copies = []
    nt = (((1,), (1,)), ((), ()))
    for start in range(0, atoms, tile):
        xt = xs_ref[:, start : start + tile]
        for k in range(0, waves, rows):
            turns = jnp.dot(ka_ref[k : k + rows, :], xt, preferred_element_type=jnp.float32)
            cosv, sinv = phases_of(turns)
            table_ref[k : k + rows, start : start + tile] = cosv.astype(jnp.bfloat16)
            table_ref[k : k + rows, atoms + start : atoms + start + tile] = sinv.astype(jnp.bfloat16)
        for half in range(2):
            span = pl.ds(half * atoms + start, tile)
            copy = pltpu.make_async_copy(
                table_ref.at[:, span], stored_ref.at[:, span], sems.at[half, start // tile]
            )
            copy.start()
            copies.append(copy)
        lane = lax.broadcasted_iota(jnp.int32, (chans, tile), 1) + start
        ht = jnp.where(lane < live_atoms, h_ref[:, start : start + tile].astype(jnp.float32), 0.0)
        zero = jnp.zeros_like(ht)
        hc = jnp.concatenate([ht, zero], axis=0).astype(jnp.bfloat16)
        hs = jnp.concatenate([zero, ht], axis=0).astype(jnp.bfloat16)
        acc = acc + lax.dot_general(table_ref[:, start : start + tile], hc, nt, preferred_element_type=jnp.float32)
        acc = acc + lax.dot_general(
            table_ref[:, atoms + start : atoms + start + tile], hs, nt, preferred_element_type=jnp.float32
        )
    out_ref[...] = acc.astype(jnp.bfloat16).reshape(out_ref.shape)
    carry_ref[:chans, :] = jnp.dot(weight_ref[...], h_ref[...], preferred_element_type=jnp.float32).astype(
        jnp.bfloat16
    )
    carry_ref[chans:, :] = xs_ref[...]
    for copy in copies:
        copy.wait()


def structure(kvec, coords, h, weight, count, pieces):
    waves, atoms, chans = kvec.shape[1], coords.shape[1], h.shape[0]
    return pl.pallas_call(
        functools.partial(structure_kernel, TILE),
        out_shape=(
            jax.ShapeDtypeStruct((waves, 2 * atoms), jnp.bfloat16),
            jax.ShapeDtypeStruct((pieces, waves // pieces, 2 * chans), jnp.bfloat16),
            jax.ShapeDtypeStruct((chans + 16, atoms), jnp.bfloat16),
        ),
        in_specs=[VMEM_SPEC] * 4 + [pl.BlockSpec(memory_space=pltpu.SMEM)],
        out_specs=(ANY_SPEC, VMEM_SPEC, VMEM_SPEC),
        scratch_shapes=[
            pltpu.VMEM((waves, 16), jnp.bfloat16),
            pltpu.VMEM((16, atoms), jnp.bfloat16),
            pltpu.VMEM((waves, 2 * atoms), jnp.bfloat16),
            pltpu.SemaphoreType.DMA((2, atoms // TILE)),
        ],
        compiler_params=pltpu.CompilerParams(vmem_limit_bytes=WIDE_LIMIT),
        name="structure",
    )(kvec, coords, h, weight, count)


def potentials_kernel(filtered_ref, stored_ref, out_ref, table_ref, sems):
    chans = out_ref.shape[1]
    pieces, _, width = out_ref.shape
    atoms = pieces * width
    tn = (((0,), (0,)), ((), ()))
    copies = []
    for piece in range(pieces):
        for half in range(2):
            span = pl.ds(half * atoms + piece * width, width)
            copy = pltpu.make_async_copy(stored_ref.at[:, span], table_ref.at[:, span], sems.at[half, piece])
            copy.start()
            copies.append(copy)
    fc = filtered_ref[:, :chans]
    fs = filtered_ref[:, chans:]
    for piece in range(pieces):
        start = piece * width
        copies[2 * piece].wait()
        copies[2 * piece + 1].wait()
        term = lax.dot_general(
            fc, table_ref[:, start : start + width], tn, preferred_element_type=jnp.float32
        ) + lax.dot_general(
            fs, table_ref[:, atoms + start : atoms + start + width], tn, preferred_element_type=jnp.float32
        )
        out_ref[piece] = (term * (1.0 / math.sqrt(K))).astype(jnp.bfloat16)


def potentials(filtered, table, pieces):
    chans = filtered.shape[1] // 2
    atoms = table.shape[1] // 2
    return pl.pallas_call(
        potentials_kernel,
        out_shape=jax.ShapeDtypeStruct((pieces, chans, atoms // pieces), jnp.bfloat16),
        in_specs=[VMEM_SPEC, ANY_SPEC],
        out_specs=VMEM_SPEC,
        scratch_shapes=[pltpu.VMEM(table.shape, jnp.bfloat16), pltpu.SemaphoreType.DMA((2, pieces))],
        compiler_params=pltpu.CompilerParams(vmem_limit_bytes=WIDE_LIMIT),
        name="potentials",
    )(filtered, table)


def spectral_kernel(scale, arrived_ref, gain_ref, mixing_ref, out_ref):
    chans = mixing_ref.shape[0]
    factor = arrived_ref[0].astype(jnp.float32)
    for piece in range(1, arrived_ref.shape[0]):
        factor = factor + arrived_ref[piece].astype(jnp.float32)
    factor = factor * scale
    high = lax.Precision.HIGHEST
    mixing = mixing_ref[...]
    cos_part = jnp.dot(factor[:, :chans], mixing, precision=high, preferred_element_type=jnp.float32)
    sin_part = jnp.dot(factor[:, chans:], mixing, precision=high, preferred_element_type=jnp.float32)
    filtered = (jnp.concatenate([cos_part, sin_part], axis=1) * gain_ref[...]).astype(jnp.bfloat16)
    for piece in range(out_ref.shape[0]):
        out_ref[piece] = filtered


def spectral(arrived, gain, mixing, total):
    return pl.pallas_call(
        functools.partial(spectral_kernel, 1.0 / math.sqrt(total)),
        out_shape=jax.ShapeDtypeStruct(arrived.shape, jnp.bfloat16),
        in_specs=[VMEM_SPEC] * 3,
        out_specs=VMEM_SPEC,
        compiler_params=pltpu.CompilerParams(vmem_limit_bytes=LIMIT),
        name="spectral",
    )(arrived, gain, mixing)


def update_kernel(arrived_ref, h_ref, msg_ref, live_ref, first_ref, second_ref, out_ref):
    potential = arrived_ref[0].astype(jnp.float32)
    for piece in range(1, arrived_ref.shape[0]):
        potential = potential + arrived_ref[piece].astype(jnp.float32)
    h = h_ref[...]
    stacked = jnp.concatenate([h, msg_ref[...], potential.astype(jnp.bfloat16)], axis=0)
    inner = jnp.dot(first_ref[...], stacked, preferred_element_type=jnp.float32)
    hidden = jax.nn.silu(inner).astype(jnp.bfloat16)
    out = h.astype(jnp.float32) + jnp.dot(second_ref[...], hidden, preferred_element_type=jnp.float32)
    new = jnp.where(live_ref[...] > 0.0, out, 0.0).astype(jnp.bfloat16)
    for piece in range(out_ref.shape[0]):
        out_ref[piece] = new


def update(arrived, h, msg, live, first_layer, second_layer):
    return pl.pallas_call(
        update_kernel,
        out_shape=jax.ShapeDtypeStruct(arrived.shape, jnp.bfloat16),
        in_specs=[VMEM_SPEC] * 6,
        out_specs=VMEM_SPEC,
        compiler_params=pltpu.CompilerParams(vmem_limit_bytes=LIMIT),
        name="update",
    )(arrived, h, msg, live, first_layer, second_layer)


def local(
    features,
    coords,
    neighbours,
    live_slots,
    block_count,
    kvec,
    msg_weight,
    filter_weight,
    mlp_in,
    mlp_out,
):
    width = features.shape[1]
    nblocks = width // BLOCK
    regions = lax.axis_size("atoms")
    groups_waves = lax.axis_size("waves")
    here = lax.axis_index("atoms")
    total = regions * width
    source = neighbours // nblocks
    offset = (source - here) % regions
    which = jnp.where(offset == 0, 1, jnp.where(offset == 1, 2, 0))
    ext_index = which * nblocks + neighbours % nblocks
    kf = kvec.astype(jnp.float32)
    kx = kf[0] / regions
    gain = GAIN_TOP / (4.0 + kx * kx + kf[1] * kf[1] + kf[2] * kf[2])
    h = features
    chans = h.shape[0]
    owned = kf.shape[1] // regions
    table, partial_factor, carry = structure(kvec, coords, h, msg_weight[0], block_count, regions)
    arrived = lax.all_to_all(partial_factor, "atoms", 0, 0, tiled=True)
    carry_ext = with_halo(carry, (("atoms", 1),), width)
    hm_ext = carry_ext[:chans]
    pieces = carry_ext[chans : chans + 9].astype(jnp.float32)
    pos_ext = (pieces[6:9] + pieces[3:6]) + pieces[:3]
    gain_share = lax.dynamic_slice_in_dim(gain, here * owned, owned, 0)
    gain_rows = jnp.broadcast_to(gain_share[:, None], (owned, 2 * chans))
    everyone = spectral(arrived, gain_rows, filter_weight[0], total)
    filtered = lax.all_to_all(everyone, "atoms", 0, 0, tiled=True).reshape(kf.shape[1], 2 * chans)
    partial_potential = potentials(filtered, table, groups_waves)
    per_group = nblocks // groups_waves
    first = lax.axis_index("waves") * per_group
    share = per_group * BLOCK
    potential = lax.all_to_all(partial_potential, "waves", 0, 0, tiled=True)
    msg = short_range(hm_ext, pos_ext, coords, ext_index, live_slots, first, per_group, regions)
    h_share = lax.dynamic_slice_in_dim(h, first * BLOCK, share, 1)
    atom = jnp.arange(share, dtype=jnp.int32) + first * BLOCK
    live_share = (atom < block_count[0] * BLOCK).astype(jnp.float32)[None, :]
    new = update(potential, h_share, msg, live_share, mlp_in[0], mlp_out[0])
    return laid_out(lax.all_to_all(new, "waves", 0, 0, tiled=True), 1)


def solution(mesh):
    in_specs = (
        P(None, "atoms"),
        P(None, "atoms"),
        P(None, "atoms"),
        P(None, "atoms"),
        P("atoms"),
        P(None, "waves"),
        P(),
        P(),
        P(),
        P(),
    )
    out_specs = P(None, "atoms")
    return jax.shard_map(local, mesh=mesh, in_specs=in_specs, out_specs=out_specs, check_vma=False)
```

```python
import functools
import math

import jax
import jax.numpy as jnp
from jax import lax
from jax.experimental import pallas as pl
from jax.experimental.pallas import tpu as pltpu
from jax.sharding import PartitionSpec as P


K = 4096
BLOCK = 128

MSG_SCALE = 0.125
GAIN_TOP = 20.0
SIN_COEFS = (3.1415926401307073, -5.167710083507923, 2.5500775232148563, -0.5982912856211671, 0.07765766030589402)
COS_COEFS = (0.9999999532476085, -4.934792830619664, 4.058411352862771, -1.3318765680813944, 0.21968961109803095)
ROOT2 = math.sqrt(2.0)
TILE = 256
ROWS = 64
LIMIT = 16 * 2**20
VMEM_SPEC = pl.BlockSpec(memory_space=pltpu.VMEM)
SMEM_SPEC = pl.BlockSpec(memory_space=pltpu.SMEM)
ANY_SPEC = pl.BlockSpec(memory_space=pl.ANY)
HBM_SPEC = pl.BlockSpec(memory_space=pltpu.HBM)
PARAMS = pltpu.CompilerParams(vmem_limit_bytes=LIMIT)
NT = (((1,), (1,)), ((), ()))
TN = (((0,), (0,)), ((), ()))


def kept_rows(waves):
    return waves * 5 // 8


def horner(coefs, scale, u):
    value = coefs[-1] * scale
    for coef in coefs[-2::-1]:
        value = value * u + coef * scale
    return value


def phases_of(turns):
    r = turns - jnp.round(turns)
    u = r * r
    s = r * horner(SIN_COEFS, ROOT2, u)
    c = horner(COS_COEFS, ROOT2, u)
    return 1.0 - s * s, s * c


def three_pieces(values):
    first = values.astype(jnp.bfloat16)
    rest = values - first.astype(jnp.float32)
    second = rest.astype(jnp.bfloat16)
    third = (rest - second.astype(jnp.float32)).astype(jnp.bfloat16)
    return first.astype(jnp.float32), second.astype(jnp.float32), third.astype(jnp.float32)


def structure_kernel(
    kvec_ref, coords_ref, h_ref, weight_ref, count_ref, low_ref, high_out, out_ref, carry_out,
    ka_ref, xs_ref, high_ref, carry_ref, sems, carry_sem,
):
    waves = kvec_ref.shape[1]
    atoms = coords_ref.shape[1]
    chans = h_ref.shape[0]
    kept = low_ref.shape[0]
    kf = kvec_ref[...].astype(jnp.float32)
    ka = jnp.concatenate([kf, kf, kf, jnp.zeros((7, waves), jnp.float32)], axis=0)
    ka_ref[...] = ka.T.astype(jnp.bfloat16)
    first, second, third = three_pieces(coords_ref[...])
    xs = jnp.concatenate([first, second, third, jnp.zeros((7, atoms), jnp.float32)], axis=0)
    xs_ref[...] = xs.astype(jnp.bfloat16)
    carry_ref[:chans, :] = jnp.dot(weight_ref[...], h_ref[...], preferred_element_type=jnp.float32).astype(
        jnp.bfloat16
    )
    carry_ref[chans:, :] = xs.astype(jnp.bfloat16)
    carry_copy = pltpu.make_async_copy(carry_ref, carry_out, carry_sem)
    carry_copy.start()
    copies = [carry_copy]
    live_atoms = count_ref[0] * BLOCK
    low_sum = jnp.zeros((kept, 2 * chans), jnp.float32)
    high_sum = jnp.zeros((waves - kept, 2 * chans), jnp.float32)
    for start in range(0, atoms, TILE):
        cos_span = slice(start, start + TILE)
        sin_span = slice(atoms + start, atoms + start + TILE)
        xt = xs_ref[:, cos_span]
        for row in range(0, waves, ROWS):
            turns = jnp.dot(ka_ref[row : row + ROWS, :], xt, preferred_element_type=jnp.float32)
            cosv, sinv = phases_of(turns)
            place, at = (low_ref, row) if row < kept else (high_ref, row - kept)
            place[at : at + ROWS, cos_span] = cosv.astype(jnp.bfloat16)
            place[at : at + ROWS, sin_span] = sinv.astype(jnp.bfloat16)
        for half in range(2):
            span = pl.ds(half * atoms + start, TILE)
            copy = pltpu.make_async_copy(
                high_ref.at[:, span], high_out.at[:, span], sems.at[half, start // TILE]
            )
            copy.start()
            copies.append(copy)
        lane = lax.broadcasted_iota(jnp.int32, (chans, TILE), 1) + start
        ht = jnp.where(lane < live_atoms, h_ref[:, cos_span].astype(jnp.float32), 0.0)
        zero = jnp.zeros_like(ht)
        hc = jnp.concatenate([ht, zero], axis=0).astype(jnp.bfloat16)
        hs = jnp.concatenate([zero, ht], axis=0).astype(jnp.bfloat16)
        f32 = dict(preferred_element_type=jnp.float32)
        low_sum = low_sum + lax.dot_general(low_ref[:, cos_span], hc, NT, **f32)
        low_sum = low_sum + lax.dot_general(low_ref[:, sin_span], hs, NT, **f32)
        high_sum = high_sum + lax.dot_general(high_ref[:, cos_span], hc, NT, **f32)
        high_sum = high_sum + lax.dot_general(high_ref[:, sin_span], hs, NT, **f32)
    owned = out_ref.shape[1]
    out_ref[: kept // owned] = low_sum.astype(jnp.bfloat16).reshape(kept // owned, owned, 2 * chans)
    out_ref[kept // owned :] = high_sum.astype(jnp.bfloat16).reshape(-1, owned, 2 * chans)
    for copy in copies:
        copy.wait()


def structure(kvec, coords, h, weight, count, pieces):
    waves, atoms, chans = kvec.shape[1], coords.shape[1], h.shape[0]
    kept = kept_rows(waves)
    return pl.pallas_call(
        structure_kernel,
        out_shape=(
            jax.ShapeDtypeStruct((kept, 2 * atoms), jnp.bfloat16),
            pltpu.HBM((waves - kept, 2 * atoms), jnp.bfloat16),
            jax.ShapeDtypeStruct((pieces, waves // pieces, 2 * chans), jnp.bfloat16),
            jax.ShapeDtypeStruct((chans + 16, atoms), jnp.bfloat16),
        ),
        in_specs=[VMEM_SPEC] * 4 + [SMEM_SPEC],
        out_specs=(VMEM_SPEC, HBM_SPEC, VMEM_SPEC, ANY_SPEC),
        scratch_shapes=[
            pltpu.VMEM((waves, 16), jnp.bfloat16),
            pltpu.VMEM((16, atoms), jnp.bfloat16),
            pltpu.VMEM((waves - kept, 2 * atoms), jnp.bfloat16),
            pltpu.VMEM((chans + 16, atoms), jnp.bfloat16),
            pltpu.SemaphoreType.DMA((2, atoms // TILE)),
            pltpu.SemaphoreType.DMA,
        ],
        compiler_params=PARAMS,
        name="structure",
    )(kvec, coords, h, weight, count)


def spectral_kernel(arrived_ref, gain_ref, mixing_ref, out_ref):
    chans = mixing_ref.shape[0]
    factor = arrived_ref[0].astype(jnp.float32)
    for piece in range(1, arrived_ref.shape[0]):
        factor = factor + arrived_ref[piece].astype(jnp.float32)
    high = dict(precision=lax.Precision.HIGHEST, preferred_element_type=jnp.float32)
    mixing = mixing_ref[...]
    cos_part = jnp.dot(factor[:, :chans], mixing, **high)
    sin_part = jnp.dot(factor[:, chans:], mixing, **high)
    filtered = (jnp.concatenate([cos_part, sin_part], axis=1) * gain_ref[...]).astype(jnp.bfloat16)
    for piece in range(out_ref.shape[0]):
        out_ref[piece] = filtered


def spectral(arrived, gain, mixing):
    return pl.pallas_call(
        spectral_kernel,
        out_shape=jax.ShapeDtypeStruct(arrived.shape, jnp.bfloat16),
        in_specs=[VMEM_SPEC] * 3,
        out_specs=VMEM_SPEC,
        compiler_params=PARAMS,
        name="spectral",
    )(arrived, gain, mixing)


def potentials_kernel(filtered_ref, low_ref, high_in, out_ref, high_ref, sems):
    chans = out_ref.shape[1]
    pieces, _, width = out_ref.shape
    atoms = pieces * width
    kept = low_ref.shape[0]
    copies = []
    for piece in range(pieces):
        for half in range(2):
            span = pl.ds(half * atoms + piece * width, width)
            copy = pltpu.make_async_copy(high_in.at[:, span], high_ref.at[:, span], sems.at[half, piece])
            copy.start()
            copies.append(copy)
    parts = [
        (filtered_ref[:kept, :chans], low_ref, 0),
        (filtered_ref[:kept, chans:], low_ref, atoms),
        (filtered_ref[kept:, :chans], high_ref, 0),
        (filtered_ref[kept:, chans:], high_ref, atoms),
    ]
    for piece in range(pieces):
        start = piece * width
        copies[2 * piece].wait()
        copies[2 * piece + 1].wait()
        term = jnp.zeros((chans, width), jnp.float32)
        for part, place, base in parts:
            table = place[:, base + start : base + start + width]
            term = term + lax.dot_general(part, table, TN, preferred_element_type=jnp.float32)
        out_ref[piece] = (term * (1.0 / math.sqrt(K))).astype(jnp.bfloat16)


def potentials(filtered, low, high, pieces):
    chans = filtered.shape[1] // 2
    atoms = low.shape[1] // 2
    return pl.pallas_call(
        potentials_kernel,
        out_shape=jax.ShapeDtypeStruct((pieces, chans, atoms // pieces), jnp.bfloat16),
        in_specs=[VMEM_SPEC, VMEM_SPEC, HBM_SPEC],
        out_specs=VMEM_SPEC,
        scratch_shapes=[pltpu.VMEM(high.shape, jnp.bfloat16), pltpu.SemaphoreType.DMA((2, pieces))],
        compiler_params=PARAMS,
        name="potentials",
    )(filtered, low, pltpu.with_memory_space_constraint(high, pltpu.HBM))


def pairs_kernel(
    scale_x, regions, place_ref, idx_ref, live_ref, prev_in, own_in, next_in, h_in, after_in, out_ref,
    ext_ref, share_ref, pos_ref, own_ref, weights_ref, near_ref, sems,
):
    chans = h_in.shape[0]
    width = own_in.shape[1]
    nblocks = width // BLOCK
    slots = idx_ref.shape[1]
    count = out_ref.shape[1] // BLOCK
    here = place_ref[0]
    first = place_ref[1]
    copies = [
        pltpu.make_async_copy(source, ext_ref.at[:, pl.ds(at * width, width)], sems.at[at])
        for at, source in enumerate((prev_in, own_in, next_in))
    ]
    share = pl.ds(pl.multiple_of(first * BLOCK, BLOCK), count * BLOCK)
    copies.append(pltpu.make_async_copy(h_in.at[:, share], share_ref, sems.at[3]))
    for copy in copies:
        copy.start()
    for copy in copies:
        copy.wait()
    out_ref[:chans, :] = share_ref[...]
    pieces = ext_ref[chans : chans + 16, :].astype(jnp.float32)
    pos_ref[0:3, :] = (pieces[6:9] + pieces[3:6]) + pieces[0:3]
    for block in range(count):
        at = pl.multiple_of((nblocks + first + block) * BLOCK, BLOCK)
        columns = pos_ref[:, pl.ds(at, BLOCK)].T
        for axis in range(3):
            own_ref[block, axis] = jnp.broadcast_to(columns[:, axis : axis + 1], (BLOCK, BLOCK))
    exponent = -2.0 * math.log2(math.e)

    def slot_step(slot, carried):
        for block in range(count):
            entry = idx_ref[first + block, slot]
            offset = lax.rem(entry // nblocks - here + regions + 1, regions)
            at = pl.multiple_of((offset * nblocks + lax.rem(entry, nblocks)) * BLOCK, BLOCK)
            alive = live_ref[first + block, slot].astype(jnp.float32)
            near = pos_ref[:, pl.ds(at, BLOCK)]
            total = None
            for axis in range(3):
                diff = own_ref[block, axis] - near[axis : axis + 1, :]
                diff = diff - jnp.round(diff)
                term = diff * diff
                if axis == 0:
                    term = term * (scale_x * scale_x)
                total = term if total is None else total + term
            pair = jnp.exp2(total * exponent).astype(jnp.bfloat16)
            to = pl.multiple_of(slot * BLOCK, BLOCK)
            weights_ref[block, :, pl.ds(to, BLOCK)] = pair
            mapped = ext_ref[:chans, pl.ds(at, BLOCK)].astype(jnp.float32) * alive
            near_ref[block, :, pl.ds(to, BLOCK)] = mapped.astype(jnp.bfloat16)
        return carried

    lax.fori_loop(0, slots, slot_step, 0)
    for block in range(count):
        msg = lax.dot_general(near_ref[block], weights_ref[block], NT, preferred_element_type=jnp.float32)
        out_ref[chans:, block * BLOCK : (block + 1) * BLOCK] = (msg * MSG_SCALE).astype(jnp.bfloat16)


def pairs(place, neighbours, live_slots, prev, own, following, h, after, count, scale_x, regions):
    rows, width = own.shape
    chans = h.shape[0]
    slots = neighbours.shape[1]
    work = slots * count * BLOCK * BLOCK
    return pl.pallas_call(
        functools.partial(pairs_kernel, float(scale_x), regions),
        out_shape=jax.ShapeDtypeStruct((2 * chans, count * BLOCK), jnp.bfloat16),
        in_specs=[SMEM_SPEC] * 3 + [ANY_SPEC] * 5,
        out_specs=VMEM_SPEC,
        scratch_shapes=[
            pltpu.VMEM((rows, 3 * width), jnp.bfloat16),
            pltpu.VMEM((chans, count * BLOCK), jnp.bfloat16),
            pltpu.VMEM((8, 3 * width), jnp.float32),
            pltpu.VMEM((count, 3, BLOCK, BLOCK), jnp.float32),
            pltpu.VMEM((count, BLOCK, slots * BLOCK), jnp.bfloat16),
            pltpu.VMEM((count, chans, slots * BLOCK), jnp.bfloat16),
            pltpu.SemaphoreType.DMA((4,)),
        ],
        compiler_params=PARAMS,
        cost_estimate=pl.CostEstimate(
            flops=work * (2 * chans + 20), bytes_accessed=6 * rows * width, transcendentals=work
        ),
        name="pairs",
    )(place, neighbours, live_slots, prev, own, following, h, after)


def update_kernel(place_ref, count_ref, arrived_ref, known_ref, first_ref, second_ref, out_ref):
    potential = arrived_ref[0].astype(jnp.float32)
    for piece in range(1, arrived_ref.shape[0]):
        potential = potential + arrived_ref[piece].astype(jnp.float32)
    chans, share = potential.shape
    stacked = jnp.concatenate([known_ref[...], potential.astype(jnp.bfloat16)], axis=0)
    inner = lax.dot_general(first_ref[...], stacked, TN, preferred_element_type=jnp.float32)
    hidden = jax.nn.silu(inner).astype(jnp.bfloat16)
    h = known_ref[:chans, :].astype(jnp.float32)
    out = h + jnp.dot(second_ref[...], hidden, preferred_element_type=jnp.float32)
    atom = lax.broadcasted_iota(jnp.int32, (chans, share), 1) + place_ref[1] * BLOCK
    new = jnp.where(atom < count_ref[0] * BLOCK, out, 0.0).astype(jnp.bfloat16)
    for piece in range(out_ref.shape[0]):
        out_ref[piece] = new


def update(place, count, arrived, known, first_layer, second_layer):
    return pl.pallas_call(
        update_kernel,
        out_shape=jax.ShapeDtypeStruct(arrived.shape, jnp.bfloat16),
        in_specs=[SMEM_SPEC] * 2 + [VMEM_SPEC] * 4,
        out_specs=VMEM_SPEC,
        compiler_params=PARAMS,
        name="update",
    )(place, count, arrived, known, first_layer, second_layer)


def laid_out(pieces, dim):
    lengths = list(pieces.shape[1:])
    lengths[dim] *= pieces.shape[0]
    return jnp.moveaxis(pieces, 0, dim).reshape(lengths)


def from_others(pieces, axis):
    return lax.all_to_all(pieces, axis, 0, 0, tiled=True)


def local(
    features,
    coords,
    neighbours,
    live_slots,
    block_count,
    kvec,
    msg_weight,
    filter_weight,
    mlp_in,
    mlp_out,
):
    chans, width = features.shape
    nblocks = width // BLOCK
    regions = lax.axis_size("atoms")
    groups_waves = lax.axis_size("waves")
    here = lax.axis_index("atoms")
    per_group = nblocks // groups_waves
    first = lax.axis_index("waves") * per_group
    place = jnp.stack([here, first]).astype(jnp.int32)
    total = regions * width
    waves = kvec.shape[1]
    owned = waves // regions
    low, high, partial_factor, carry = structure(kvec, coords, features, msg_weight[0], block_count, regions)
    arrived = from_others(partial_factor, "atoms")
    prev = lax.ppermute(carry, "atoms", [(i, (i + 1) % regions) for i in range(regions)])
    following = lax.ppermute(carry, "atoms", [((i + 1) % regions, i) for i in range(regions)])
    kf = lax.dynamic_slice_in_dim(kvec, here * owned, owned, 1).astype(jnp.float32)
    kx = kf[0] / regions
    gain = GAIN_TOP / (4.0 + kx * kx + kf[1] * kf[1] + kf[2] * kf[2])
    gain_rows = jnp.broadcast_to(gain[:, None], (owned, 2 * chans))
    mixing = filter_weight[0] * (1.0 / math.sqrt(total))
    everyone = spectral(arrived, gain_rows, mixing)
    filtered = from_others(everyone, "atoms").reshape(waves, 2 * chans)
    known = pairs(
        place, neighbours.T, live_slots.T, prev, carry, following, features, everyone, per_group, regions, regions
    )
    partial_potential = potentials(filtered, low, high, groups_waves)
    potential = from_others(partial_potential, "waves")
    new = update(place, block_count, potential, known, mlp_in[0].T, mlp_out[0])
    return laid_out(from_others(new, "waves"), 1)


def solution(mesh):
    in_specs = (
        P(None, "atoms"),
        P(None, "atoms"),
        P(None, "atoms"),
        P(None, "atoms"),
        P("atoms"),
        P(None, "waves"),
        P(),
        P(),
        P(),
        P(),
    )
    out_specs = P(None, "atoms")
    return jax.shard_map(local, mesh=mesh, in_specs=in_specs, out_specs=out_specs, check_vma=False)
```

```python
import functools
import math

import jax
import jax.numpy as jnp
from jax import lax
from jax.experimental import pallas as pl
from jax.experimental.pallas import tpu as pltpu
from jax.sharding import PartitionSpec as P


K = 4096
BLOCK = 128

MSG_SCALE = 0.125
GAIN_TOP = 20.0
SIN_COEFS = (3.1415926401307073, -5.167710083507923, 2.5500775232148563, -0.5982912856211671, 0.07765766030589402)
COS_COEFS = (0.9999999532476085, -4.934792830619664, 4.058411352862771, -1.3318765680813944, 0.21968961109803095)
ROOT2 = math.sqrt(2.0)
TILE = 256
ROWS = 64
LIMIT = 16 * 2**20
VMEM_SPEC = pl.BlockSpec(memory_space=pltpu.VMEM)
SMEM_SPEC = pl.BlockSpec(memory_space=pltpu.SMEM)
ANY_SPEC = pl.BlockSpec(memory_space=pl.ANY)
HBM_SPEC = pl.BlockSpec(memory_space=pltpu.HBM)
PARAMS = pltpu.CompilerParams(vmem_limit_bytes=LIMIT)
NT = (((1,), (1,)), ((), ()))
TN = (((0,), (0,)), ((), ()))


def kept_rows(waves):
    return waves * 5 // 8


def horner(coefs, scale, u):
    value = coefs[-1] * scale
    for coef in coefs[-2::-1]:
        value = value * u + coef * scale
    return value


def phases_of(turns):
    r = turns - jnp.round(turns)
    u = r * r
    s = r * horner(SIN_COEFS, ROOT2, u)
    c = horner(COS_COEFS, ROOT2, u)
    return 1.0 - s * s, s * c


def three_pieces(values):
    first = values.astype(jnp.bfloat16)
    rest = values - first.astype(jnp.float32)
    second = rest.astype(jnp.bfloat16)
    third = (rest - second.astype(jnp.float32)).astype(jnp.bfloat16)
    return first.astype(jnp.float32), second.astype(jnp.float32), third.astype(jnp.float32)


def structure_kernel(
    scale, regions, place_ref, count_ref, kvec_in, coords_in, h_in, weight_in, mixing_in,
    low_ref, high_out, out_ref, carry_ref, gain_ref, mixing_ref,
    kvec_ref, coords_ref, h_ref, weight_ref, ka_ref, xs_ref, high_ref, in_sems, sems,
):
    waves = kvec_ref.shape[1]
    chans, atoms = h_ref.shape
    kept = low_ref.shape[0]
    owned = out_ref.shape[1]
    f32 = dict(preferred_element_type=jnp.float32)
    taken = [
        pltpu.make_async_copy(source, target, in_sems.at[at])
        for at, (source, target) in enumerate(
            (
                (kvec_in, kvec_ref),
                (coords_in, coords_ref),
                (h_in, h_ref),
                (weight_in, weight_ref),
                (mixing_in, mixing_ref),
            )
        )
    ]
    for copy in taken:
        copy.start()
    taken[0].wait()
    kf = kvec_ref[...].astype(jnp.float32)
    ka = jnp.concatenate([kf, kf, kf, jnp.zeros((7, waves), jnp.float32)], axis=0)
    ka_ref[...] = ka.T.astype(jnp.bfloat16)
    kx = kf[0:1] / regions
    gain = GAIN_TOP / (4.0 + kx * kx + kf[1:2] * kf[1:2] + kf[2:3] * kf[2:3])
    lane = lax.broadcasted_iota(jnp.int32, (owned, waves), 1)
    own = lane == lax.broadcasted_iota(jnp.int32, (owned, waves), 0) + place_ref[0] * owned
    mine = jnp.sum(jnp.where(own, jnp.broadcast_to(gain, (owned, waves)), 0.0), axis=1, keepdims=True)
    gain_ref[...] = jnp.broadcast_to(mine * scale, gain_ref.shape)
    taken[1].wait()
    first, second, third = three_pieces(coords_ref[...])
    xs = jnp.concatenate([first, second, third, jnp.zeros((7, atoms), jnp.float32)], axis=0)
    xs_ref[...] = xs.astype(jnp.bfloat16)
    gap = jnp.zeros((5, atoms), jnp.float32)
    spread = jnp.concatenate([first, gap, second, gap, third, gap], axis=0)
    carry_ref[chans:, :] = spread.astype(jnp.bfloat16)
    live_atoms = count_ref[0] * BLOCK
    low_sum = jnp.zeros((kept, 2 * chans), jnp.float32)
    high_sum = jnp.zeros((waves - kept, 2 * chans), jnp.float32)
    copies = []
    for start in range(0, atoms, TILE):
        cos_span = slice(start, start + TILE)
        sin_span = slice(atoms + start, atoms + start + TILE)
        xt = xs_ref[:, cos_span]
        for row in range(0, waves, ROWS):
            turns = jnp.dot(ka_ref[row : row + ROWS, :], xt, **f32)
            cosv, sinv = phases_of(turns)
            place, at = (low_ref, row) if row < kept else (high_ref, row - kept)
            place[at : at + ROWS, cos_span] = cosv.astype(jnp.bfloat16)
            place[at : at + ROWS, sin_span] = sinv.astype(jnp.bfloat16)
        for half in range(2):
            span = pl.ds(half * atoms + start, TILE)
            copy = pltpu.make_async_copy(high_ref.at[:, span], high_out.at[:, span], sems.at[half, start // TILE])
            copy.start()
            copies.append(copy)
        if start == 0:
            for copy in taken[2:]:
                copy.wait()
        carry_ref[:chans, cos_span] = jnp.dot(weight_ref[...], h_ref[:, cos_span], **f32).astype(jnp.bfloat16)
        atom = lax.broadcasted_iota(jnp.int32, (chans, TILE), 1) + start
        ht = jnp.where(atom < live_atoms, h_ref[:, cos_span].astype(jnp.float32), 0.0)
        zero = jnp.zeros_like(ht)
        hc = jnp.concatenate([ht, zero], axis=0).astype(jnp.bfloat16)
        hs = jnp.concatenate([zero, ht], axis=0).astype(jnp.bfloat16)
        low_sum = low_sum + lax.dot_general(low_ref[:, cos_span], hc, NT, **f32)
        low_sum = low_sum + lax.dot_general(low_ref[:, sin_span], hs, NT, **f32)
        high_sum = high_sum + lax.dot_general(high_ref[:, cos_span], hc, NT, **f32)
        high_sum = high_sum + lax.dot_general(high_ref[:, sin_span], hs, NT, **f32)
    out_ref[: kept // owned] = low_sum.astype(jnp.bfloat16).reshape(kept // owned, owned, 2 * chans)
    out_ref[kept // owned :] = high_sum.astype(jnp.bfloat16).reshape(-1, owned, 2 * chans)
    for copy in copies:
        copy.wait()


def in_hbm(*arrays):
    return tuple(pltpu.with_memory_space_constraint(array, pltpu.HBM) for array in arrays)


def structure(place, count, kvec, coords, h, weight, mixing, scale, regions):
    waves, atoms, chans = kvec.shape[1], coords.shape[1], h.shape[0]
    kept = kept_rows(waves)
    owned = waves // regions
    return pl.pallas_call(
        functools.partial(structure_kernel, scale, float(regions)),
        out_shape=(
            jax.ShapeDtypeStruct((kept, 2 * atoms), jnp.bfloat16),
            pltpu.HBM((waves - kept, 2 * atoms), jnp.bfloat16),
            jax.ShapeDtypeStruct((regions, owned, 2 * chans), jnp.bfloat16),
            jax.ShapeDtypeStruct((chans + 24, atoms), jnp.bfloat16),
            jax.ShapeDtypeStruct((owned, 2 * chans), jnp.float32),
            jax.ShapeDtypeStruct(mixing.shape, jnp.float32),
        ),
        in_specs=[SMEM_SPEC] * 2 + [HBM_SPEC] * 5,
        out_specs=(VMEM_SPEC, HBM_SPEC) + (VMEM_SPEC,) * 4,
        scratch_shapes=[
            pltpu.VMEM(kvec.shape, jnp.int32),
            pltpu.VMEM(coords.shape, jnp.float32),
            pltpu.VMEM(h.shape, jnp.bfloat16),
            pltpu.VMEM(weight.shape, jnp.bfloat16),
            pltpu.VMEM((waves, 16), jnp.bfloat16),
            pltpu.VMEM((16, atoms), jnp.bfloat16),
            pltpu.VMEM((waves - kept, 2 * atoms), jnp.bfloat16),
            pltpu.SemaphoreType.DMA((5,)),
            pltpu.SemaphoreType.DMA((2, atoms // TILE)),
        ],
        compiler_params=PARAMS,
        name="structure",
    )(place, count, *in_hbm(kvec, coords, h, weight, mixing))


def spectral_kernel(arrived_ref, gain_ref, mixing_ref, out_ref):
    chans = mixing_ref.shape[0]
    factor = arrived_ref[0].astype(jnp.float32)
    for piece in range(1, arrived_ref.shape[0]):
        factor = factor + arrived_ref[piece].astype(jnp.float32)
    high = dict(precision=lax.Precision.HIGHEST, preferred_element_type=jnp.float32)
    mixing = mixing_ref[...]
    cos_part = jnp.dot(factor[:, :chans], mixing, **high)
    sin_part = jnp.dot(factor[:, chans:], mixing, **high)
    filtered = (jnp.concatenate([cos_part, sin_part], axis=1) * gain_ref[...]).astype(jnp.bfloat16)
    for piece in range(out_ref.shape[0]):
        out_ref[piece] = filtered


def spectral(arrived, gain, mixing):
    return pl.pallas_call(
        spectral_kernel,
        out_shape=jax.ShapeDtypeStruct(arrived.shape, jnp.bfloat16),
        in_specs=[VMEM_SPEC] * 3,
        out_specs=VMEM_SPEC,
        compiler_params=PARAMS,
        name="spectral",
    )(arrived, gain, mixing)


def potentials_kernel(filtered_ref, low_ref, high_in, out_ref, high_ref, sum_ref, sems):
    chans = out_ref.shape[1]
    pieces, _, width = out_ref.shape
    atoms = pieces * width
    kept = low_ref.shape[0]
    copies = []
    for piece in range(pieces):
        for half in range(2):
            span = pl.ds(half * atoms + piece * width, width)
            copy = pltpu.make_async_copy(high_in.at[:, span], high_ref.at[:, span], sems.at[half, piece])
            copy.start()
            copies.append(copy)

    def term(rows, table, piece):
        cos_span = slice(piece * width, (piece + 1) * width)
        sin_span = slice(atoms + piece * width, atoms + (piece + 1) * width)
        f32 = dict(preferred_element_type=jnp.float32)
        return lax.dot_general(filtered_ref[rows, :chans], table[:, cos_span], TN, **f32) + lax.dot_general(
            filtered_ref[rows, chans:], table[:, sin_span], TN, **f32
        )

    for piece in range(pieces):
        sum_ref[piece] = term(slice(0, kept), low_ref, piece)
    for piece in range(pieces):
        copies[2 * piece].wait()
        copies[2 * piece + 1].wait()
        whole = sum_ref[piece] + term(slice(kept, filtered_ref.shape[0]), high_ref, piece)
        out_ref[piece] = (whole * (1.0 / math.sqrt(K))).astype(jnp.bfloat16)


def potentials(filtered, low, high, pieces):
    chans = filtered.shape[1] // 2
    atoms = low.shape[1] // 2
    return pl.pallas_call(
        potentials_kernel,
        out_shape=jax.ShapeDtypeStruct((pieces, chans, atoms // pieces), jnp.bfloat16),
        in_specs=[VMEM_SPEC, VMEM_SPEC, HBM_SPEC],
        out_specs=VMEM_SPEC,
        scratch_shapes=[
            pltpu.VMEM(high.shape, jnp.bfloat16),
            pltpu.VMEM((pieces, chans, atoms // pieces), jnp.float32),
            pltpu.SemaphoreType.DMA((2, pieces)),
        ],
        compiler_params=PARAMS,
        name="potentials",
    )(filtered, low, *in_hbm(high))


def pairs_kernel(
    scale_x, regions, place_ref, count_ref, idx_ref, live_ref, prev_in, own_in, next_in, h_in, first_in, second_in,
    inner_ref, share_ref, alive_ref, third_ref, second_ref,
    ext_ref, first_ref, pos_ref, own_ref, weights_ref, near_ref, sems,
):
    chans = h_in.shape[0]
    width = own_in.shape[1]
    nblocks = width // BLOCK
    slots = idx_ref.shape[1]
    count = share_ref.shape[1] // BLOCK
    here = place_ref[0]
    first = place_ref[1]
    share = pl.ds(pl.multiple_of(first * BLOCK, BLOCK), count * BLOCK)
    moves = [(source, ext_ref.at[:, pl.ds(at * width, width)]) for at, source in enumerate((prev_in, own_in, next_in))]
    moves += [(h_in.at[:, share], share_ref), (first_in, first_ref), (second_in, second_ref)]
    copies = [pltpu.make_async_copy(source, target, sems.at[at]) for at, (source, target) in enumerate(moves)]
    for copy in copies:
        copy.start()
    atom = lax.broadcasted_iota(jnp.int32, alive_ref.shape, 1) + first * BLOCK
    alive_ref[...] = jnp.where(atom < count_ref[0] * BLOCK, 1.0, 0.0)
    for copy in copies:
        copy.wait()
    pieces = [ext_ref[chans + 8 * at : chans + 8 * at + 8, :].astype(jnp.float32) for at in range(3)]
    pos_ref[...] = (pieces[2] + pieces[1]) + pieces[0]
    for block in range(count):
        at = pl.multiple_of((nblocks + first + block) * BLOCK, BLOCK)
        columns = pos_ref[:, pl.ds(at, BLOCK)].T
        for axis in range(3):
            own_ref[block, axis] = jnp.broadcast_to(columns[:, axis : axis + 1], (BLOCK, BLOCK))
    exponent = -2.0 * math.log2(math.e)

    def slot_step(slot, carried):
        for block in range(count):
            entry = idx_ref[first + block, slot]
            offset = lax.rem(entry // nblocks - here + regions + 1, regions)
            at = pl.multiple_of((offset * nblocks + lax.rem(entry, nblocks)) * BLOCK, BLOCK)
            used = live_ref[first + block, slot].astype(jnp.float32)
            near = pos_ref[:, pl.ds(at, BLOCK)]
            total = None
            for axis in range(3):
                diff = own_ref[block, axis] - near[axis : axis + 1, :]
                diff = diff - jnp.round(diff)
                term = diff * diff
                if axis == 0:
                    term = term * (scale_x * scale_x)
                total = term if total is None else total + term
            pair = jnp.exp2(total * exponent).astype(jnp.bfloat16)
            to = pl.multiple_of(slot * BLOCK, BLOCK)
            weights_ref[block, :, pl.ds(to, BLOCK)] = pair
            mapped = ext_ref[:chans, pl.ds(at, BLOCK)].astype(jnp.float32) * used
            near_ref[block, :, pl.ds(to, BLOCK)] = mapped.astype(jnp.bfloat16)
        return carried

    lax.fori_loop(0, slots, slot_step, 0)
    f32 = dict(preferred_element_type=jnp.float32)
    outer = first_ref[: 2 * chans, :]
    third_ref[...] = first_ref[2 * chans :, :].astype(jnp.float32).T.astype(jnp.bfloat16)
    for block in range(count):
        span = slice(block * BLOCK, (block + 1) * BLOCK)
        msg = lax.dot_general(near_ref[block], weights_ref[block], NT, **f32)
        msg = (msg * MSG_SCALE).astype(jnp.bfloat16)
        known = jnp.concatenate([share_ref[:, span], msg], axis=0)
        inner_ref[:, span] = lax.dot_general(outer, known, TN, **f32)


def pairs(place, live_blocks, neighbours, live_slots, prev, own, following, h, first, second, count, regions):
    rows, width = own.shape
    chans = h.shape[0]
    hidden = first.shape[1]
    slots = neighbours.shape[1]
    share = count * BLOCK
    work = slots * share * BLOCK
    return pl.pallas_call(
        functools.partial(pairs_kernel, float(regions), regions),
        out_shape=(
            jax.ShapeDtypeStruct((hidden, share), jnp.float32),
            jax.ShapeDtypeStruct((chans, share), jnp.bfloat16),
            jax.ShapeDtypeStruct((8, share), jnp.float32),
            jax.ShapeDtypeStruct((hidden, chans), jnp.bfloat16),
            jax.ShapeDtypeStruct(second.shape, jnp.bfloat16),
        ),
        in_specs=[SMEM_SPEC] * 4 + [ANY_SPEC] * 3 + [HBM_SPEC] * 3,
        out_specs=(VMEM_SPEC,) * 5,
        scratch_shapes=[
            pltpu.VMEM((rows, 3 * width), jnp.bfloat16),
            pltpu.VMEM(first.shape, jnp.bfloat16),
            pltpu.VMEM((8, 3 * width), jnp.float32),
            pltpu.VMEM((count, 3, BLOCK, BLOCK), jnp.float32),
            pltpu.VMEM((count, BLOCK, slots * BLOCK), jnp.bfloat16),
            pltpu.VMEM((count, chans, slots * BLOCK), jnp.bfloat16),
            pltpu.SemaphoreType.DMA((6,)),
        ],
        compiler_params=PARAMS,
        cost_estimate=pl.CostEstimate(
            flops=work * (2 * chans + 20), bytes_accessed=6 * rows * width, transcendentals=work
        ),
        name="pairs",
    )(place, live_blocks, neighbours, live_slots, prev, own, following, *in_hbm(h, first, second))


def update_kernel(arrived_ref, inner_ref, share_ref, alive_ref, third_ref, second_ref, out_ref):
    potential = arrived_ref[0].astype(jnp.float32)
    for piece in range(1, arrived_ref.shape[0]):
        potential = potential + arrived_ref[piece].astype(jnp.float32)
    f32 = dict(preferred_element_type=jnp.float32)
    inner = inner_ref[...] + jnp.dot(third_ref[...], potential.astype(jnp.bfloat16), **f32)
    hidden = jax.nn.silu(inner).astype(jnp.bfloat16)
    out = share_ref[...].astype(jnp.float32) + jnp.dot(second_ref[...], hidden, **f32)
    new = jnp.where(alive_ref[0:1, :] > 0.0, out, 0.0).astype(jnp.bfloat16)
    for piece in range(out_ref.shape[0]):
        out_ref[piece] = new


def update(arrived, known):
    return pl.pallas_call(
        update_kernel,
        out_shape=jax.ShapeDtypeStruct(arrived.shape, jnp.bfloat16),
        in_specs=[VMEM_SPEC] * 6,
        out_specs=VMEM_SPEC,
        compiler_params=PARAMS,
        name="update",
    )(arrived, *known)


def laid_out(pieces, dim):
    lengths = list(pieces.shape[1:])
    lengths[dim] *= pieces.shape[0]
    return jnp.moveaxis(pieces, 0, dim).reshape(lengths)


def from_others(pieces, axis):
    return lax.all_to_all(pieces, axis, 0, 0, tiled=True)


def local(
    features,
    coords,
    neighbours,
    live_slots,
    block_count,
    kvec,
    msg_weight,
    filter_weight,
    mlp_in,
    mlp_out,
):
    chans, width = features.shape
    nblocks = width // BLOCK
    regions = lax.axis_size("atoms")
    groups_waves = lax.axis_size("waves")
    here = lax.axis_index("atoms")
    per_group = nblocks // groups_waves
    first = lax.axis_index("waves") * per_group
    place = jnp.stack([here, first]).astype(jnp.int32)
    total = regions * width
    waves = kvec.shape[1]
    low, high, partial_factor, carry, gain_rows, mixing = structure(
        place, block_count, kvec, coords, features, msg_weight[0], filter_weight[0], 1.0 / math.sqrt(total), regions
    )
    arrived = from_others(partial_factor, "atoms")
    prev = lax.ppermute(carry, "atoms", [(i, (i + 1) % regions) for i in range(regions)])
    following = lax.ppermute(carry, "atoms", [((i + 1) % regions, i) for i in range(regions)])
    everyone = spectral(arrived, gain_rows, mixing)
    filtered = from_others(everyone, "atoms").reshape(waves, 2 * chans)
    partial_potential = potentials(filtered, low, high, groups_waves)
    potential = from_others(partial_potential, "waves")
    known = pairs(
        place, block_count, neighbours.T, live_slots.T, prev, carry, following,
        features, mlp_in[0].T, mlp_out[0], per_group, regions,
    )
    new = update(potential, known)
    return laid_out(from_others(new, "waves"), 1)


def solution(mesh):
    in_specs = (
        P(None, "atoms"),
        P(None, "atoms"),
        P(None, "atoms"),
        P(None, "atoms"),
        P("atoms"),
        P(None, "waves"),
        P(),
        P(),
        P(),
        P(),
    )
    out_specs = P(None, "atoms")
    return jax.shard_map(local, mesh=mesh, in_specs=in_specs, out_specs=out_specs, check_vma=False)
```

```python
import functools
import math

import jax
import jax.numpy as jnp
from jax import lax
from jax.experimental import pallas as pl
from jax.experimental.pallas import tpu as pltpu
from jax.sharding import PartitionSpec as P


K = 4096
BLOCK = 128

MSG_SCALE = 0.125
GAIN_TOP = 20.0
SIN_COEFS = (3.1415902702069918, -5.167406733272337, 2.5440105185033337, -0.5594624554679438)
COS_COEFS = (0.9999999532476085, -4.934792830619664, 4.058411352862771, -1.3318765680813944, 0.21968961109803095)
ROOT2 = math.sqrt(2.0)
TILE = 256
ROWS = 64
LIMIT = 16 * 2**20
VMEM_SPEC = pl.BlockSpec(memory_space=pltpu.VMEM)
SMEM_SPEC = pl.BlockSpec(memory_space=pltpu.SMEM)
ANY_SPEC = pl.BlockSpec(memory_space=pl.ANY)
HBM_SPEC = pl.BlockSpec(memory_space=pltpu.HBM)
PARAMS = pltpu.CompilerParams(vmem_limit_bytes=LIMIT)
NT = (((1,), (1,)), ((), ()))
TN = (((0,), (0,)), ((), ()))


def kept_rows(waves):
    return waves * 3 // 4


def horner(coefs, scale, u):
    value = coefs[-1] * scale
    for coef in coefs[-2::-1]:
        value = value * u + coef * scale
    return value


def phases_of(turns):
    r = turns - jnp.round(turns)
    u = r * r
    s = r * horner(SIN_COEFS, ROOT2, u)
    c = horner(COS_COEFS, ROOT2, u)
    return 1.0 - s * s, s * c


def three_pieces(values):
    first = values.astype(jnp.bfloat16)
    rest = values - first.astype(jnp.float32)
    second = rest.astype(jnp.bfloat16)
    third = (rest - second.astype(jnp.float32)).astype(jnp.bfloat16)
    return first.astype(jnp.float32), second.astype(jnp.float32), third.astype(jnp.float32)


def structure_kernel(
    scale, regions, place_ref, count_ref, kvec_in, coords_in, h_in, weight_in, mixing_in,
    low_ref, high_out, out_ref, carry_out, gain_ref, mixing_ref,
    kvec_ref, coords_ref, h_ref, weight_ref, ka_ref, masked_ref, high_ref, carry_ref, in_sems, sems,
):
    waves = kvec_ref.shape[1]
    chans, atoms = h_ref.shape
    kept = low_ref.shape[0]
    owned = out_ref.shape[1]
    f32 = dict(preferred_element_type=jnp.float32)
    taken = [
        pltpu.make_async_copy(source, target, in_sems.at[at])
        for at, (source, target) in enumerate(
            (
                (kvec_in, kvec_ref),
                (coords_in, coords_ref),
                (h_in, h_ref),
                (weight_in, weight_ref),
                (mixing_in, mixing_ref),
            )
        )
    ]
    for copy in taken:
        copy.start()
    taken[0].wait()
    kf = kvec_ref[...].astype(jnp.float32)
    ahead, behind = jnp.zeros((3, waves), jnp.float32), jnp.zeros((2, waves), jnp.float32)
    ka = jnp.concatenate([part for axis in range(3) for part in (ahead, *(-kf[axis : axis + 1],) * 3, behind)], axis=0)
    ka_ref[...] = ka.T.astype(jnp.bfloat16)
    kx = kf[0:1] / regions
    gain = GAIN_TOP / (4.0 + kx * kx + kf[1:2] * kf[1:2] + kf[2:3] * kf[2:3])
    lane = lax.broadcasted_iota(jnp.int32, (owned, waves), 1)
    own = lane == lax.broadcasted_iota(jnp.int32, (owned, waves), 0) + place_ref[0] * owned
    mine = jnp.sum(jnp.where(own, jnp.broadcast_to(gain, (owned, waves)), 0.0), axis=1, keepdims=True)
    gain_ref[...] = jnp.broadcast_to(mine * scale, gain_ref.shape)
    taken[1].wait()
    pieces = three_pieces(coords_ref[...])
    ones, gap = jnp.ones((3, atoms), jnp.float32), jnp.zeros((2, atoms), jnp.float32)
    for axis in range(3):
        rows = jnp.concatenate([ones, *(-piece[axis : axis + 1] for piece in pieces), gap], axis=0)
        carry_ref[chans + 8 * axis : chans + 8 * axis + 8, :] = rows.astype(jnp.bfloat16)
    for copy in taken[2:]:
        copy.wait()
    live_atoms = count_ref[0] * BLOCK
    atom = lax.broadcasted_iota(jnp.int32, (chans, atoms), 1)
    masked_ref[...] = jnp.where(atom < live_atoms, h_ref[...].astype(jnp.float32), 0.0).astype(jnp.bfloat16)
    zero = jnp.zeros((chans, TILE), jnp.bfloat16)
    sums = {}

    def add_up(place, at, row, start):
        ht = masked_ref[:, start : start + TILE]
        cosv = place[at : at + ROWS, start : start + TILE]
        sinv = place[at : at + ROWS, atoms + start : atoms + start + TILE]
        term = lax.dot_general(cosv, jnp.concatenate([ht, zero], axis=0), NT, **f32)
        term = term + lax.dot_general(sinv, jnp.concatenate([zero, ht], axis=0), NT, **f32)
        sums[row] = term if start == 0 else sums[row] + term
        if start + TILE == atoms:
            whole = sums.pop(row).astype(jnp.bfloat16)
            out_ref[row // owned : (row + ROWS) // owned] = whole.reshape(ROWS // owned, owned, 2 * chans)

    pending = []
    copies = []
    for row in [*range(kept, waves, ROWS), *range(0, kept, ROWS)]:
        place, at = (low_ref, row) if row < kept else (high_ref, row - kept)
        if row == 0:
            copies = [
                pltpu.make_async_copy(high_ref, high_out, sems.at[0]),
                pltpu.make_async_copy(carry_ref, carry_out, sems.at[1]),
            ]
            for copy in copies:
                copy.start()
        for start in range(0, atoms, TILE):
            cos_span = slice(start, start + TILE)
            sin_span = slice(atoms + start, atoms + start + TILE)
            turns = jnp.dot(ka_ref[row : row + ROWS, :], carry_ref[chans:, cos_span], **f32)
            cosv, sinv = phases_of(turns)
            place[at : at + ROWS, cos_span] = cosv.astype(jnp.bfloat16)
            place[at : at + ROWS, sin_span] = sinv.astype(jnp.bfloat16)
            if row == kept:
                carry_ref[:chans, cos_span] = jnp.dot(weight_ref[...], h_ref[:, cos_span], **f32).astype(jnp.bfloat16)
            pending.append((place, at, row, start))
            if len(pending) > 1:
                add_up(*pending.pop(0))
    add_up(*pending.pop(0))
    for copy in copies:
        copy.wait()


def in_hbm(*arrays):
    return tuple(pltpu.with_memory_space_constraint(array, pltpu.HBM) for array in arrays)


def structure(place, count, kvec, coords, h, weight, mixing, scale, regions):
    waves, atoms, chans = kvec.shape[1], coords.shape[1], h.shape[0]
    kept = kept_rows(waves)
    owned = waves // regions
    return pl.pallas_call(
        functools.partial(structure_kernel, scale, float(regions)),
        out_shape=(
            jax.ShapeDtypeStruct((kept, 2 * atoms), jnp.bfloat16),
            pltpu.HBM((waves - kept, 2 * atoms), jnp.bfloat16),
            jax.ShapeDtypeStruct((regions, owned, 2 * chans), jnp.bfloat16),
            pltpu.HBM((chans + 24, atoms), jnp.bfloat16),
            jax.ShapeDtypeStruct((owned, 2 * chans), jnp.float32),
            jax.ShapeDtypeStruct(mixing.shape, jnp.float32),
        ),
        in_specs=[SMEM_SPEC] * 2 + [HBM_SPEC] * 5,
        out_specs=(VMEM_SPEC, HBM_SPEC, VMEM_SPEC, HBM_SPEC, VMEM_SPEC, VMEM_SPEC),
        scratch_shapes=[
            pltpu.VMEM(kvec.shape, jnp.int32),
            pltpu.VMEM(coords.shape, jnp.float32),
            pltpu.VMEM(h.shape, jnp.bfloat16),
            pltpu.VMEM(weight.shape, jnp.bfloat16),
            pltpu.VMEM((waves, 24), jnp.bfloat16),
            pltpu.VMEM(h.shape, jnp.bfloat16),
            pltpu.VMEM((waves - kept, 2 * atoms), jnp.bfloat16),
            pltpu.VMEM((chans + 24, atoms), jnp.bfloat16),
            pltpu.SemaphoreType.DMA((5,)),
            pltpu.SemaphoreType.DMA((2,)),
        ],
        compiler_params=PARAMS,
        name="structure",
    )(place, count, *in_hbm(kvec, coords, h, weight, mixing))


def spectral_kernel(arrived_ref, gain_ref, mixing_ref, out_ref):
    chans = mixing_ref.shape[0]
    factor = arrived_ref[0].astype(jnp.float32)
    for piece in range(1, arrived_ref.shape[0]):
        factor = factor + arrived_ref[piece].astype(jnp.float32)
    high = dict(precision=lax.Precision.HIGHEST, preferred_element_type=jnp.float32)
    mixing = mixing_ref[...]
    cos_part = jnp.dot(factor[:, :chans], mixing, **high)
    sin_part = jnp.dot(factor[:, chans:], mixing, **high)
    filtered = (jnp.concatenate([cos_part, sin_part], axis=1) * gain_ref[...]).astype(jnp.bfloat16)
    for piece in range(out_ref.shape[0]):
        out_ref[piece] = filtered


def spectral(arrived, gain, mixing):
    return pl.pallas_call(
        spectral_kernel,
        out_shape=jax.ShapeDtypeStruct(arrived.shape, jnp.bfloat16),
        in_specs=[VMEM_SPEC] * 3,
        out_specs=VMEM_SPEC,
        compiler_params=PARAMS,
        name="spectral",
    )(arrived, gain, mixing)


def potentials_kernel(filtered_ref, low_ref, high_in, out_ref, high_ref, across_ref, sum_ref, sem):
    chans = out_ref.shape[1]
    pieces, _, width = out_ref.shape
    atoms = pieces * width
    kept, waves = low_ref.shape[0], filtered_ref.shape[0]
    copy = pltpu.make_async_copy(high_in, high_ref, sem)
    copy.start()
    across_ref[...] = filtered_ref[...].astype(jnp.float32).T.astype(jnp.bfloat16)

    def term(rows, table, piece):
        cos_span = slice(piece * width, (piece + 1) * width)
        sin_span = slice(atoms + piece * width, atoms + (piece + 1) * width)
        f32 = dict(preferred_element_type=jnp.float32)
        return jnp.dot(across_ref[:chans, rows], table[:, cos_span], **f32) + jnp.dot(
            across_ref[chans:, rows], table[:, sin_span], **f32
        )

    for piece in range(pieces):
        sum_ref[piece] = term(slice(0, kept), low_ref, piece)
    copy.wait()
    for piece in range(pieces):
        whole = sum_ref[piece] + term(slice(kept, waves), high_ref, piece)
        out_ref[piece] = (whole * (1.0 / math.sqrt(K))).astype(jnp.bfloat16)


def potentials(filtered, low, high, pieces):
    chans = filtered.shape[1] // 2
    atoms = low.shape[1] // 2
    return pl.pallas_call(
        potentials_kernel,
        out_shape=jax.ShapeDtypeStruct((pieces, chans, atoms // pieces), jnp.bfloat16),
        in_specs=[VMEM_SPEC, VMEM_SPEC, HBM_SPEC],
        out_specs=VMEM_SPEC,
        scratch_shapes=[
            pltpu.VMEM(high.shape, jnp.bfloat16),
            pltpu.VMEM((2 * chans, filtered.shape[0]), jnp.bfloat16),
            pltpu.VMEM((pieces, chans, atoms // pieces), jnp.float32),
            pltpu.SemaphoreType.DMA,
        ],
        compiler_params=PARAMS,
        name="potentials",
    )(filtered, low, *in_hbm(high))


def pairs_kernel(
    scale_x, regions, unroll, place_ref, count_ref, idx_ref, live_ref, prev_in, next_in, own_in, h_in, first_in, second_in,
    inner_ref, share_ref, alive_ref, third_ref, second_ref,
    ext_ref, first_ref, own_ref, pos_ref, weights_ref, near_ref, sum_ref, sems,
):
    chans = h_in.shape[0]
    width = own_in.shape[1]
    nblocks = width // BLOCK
    slots = idx_ref.shape[1]
    count = share_ref.shape[1] // BLOCK
    here = place_ref[0]
    first = place_ref[1]
    share = pl.ds(pl.multiple_of(first * BLOCK, BLOCK), count * BLOCK)
    moves = [(source, ext_ref.at[:, pl.ds(at * width, width)]) for at, source in enumerate((prev_in, own_in, next_in))]
    moves += [(h_in.at[:, share], share_ref), (first_in, first_ref), (second_in, second_ref)]
    copies = [pltpu.make_async_copy(source, target, sems.at[at]) for at, (source, target) in enumerate(moves)]
    for copy in copies:
        copy.start()
    atom = lax.broadcasted_iota(jnp.int32, alive_ref.shape, 1) + first * BLOCK
    alive_ref[...] = jnp.where(atom < count_ref[0] * BLOCK, 1.0, 0.0)
    for copy in copies:
        copy.wait()
    f32 = dict(preferred_element_type=jnp.float32)
    column = lax.broadcasted_iota(jnp.int32, (8, 8), 1)
    pick = jnp.where((column >= 3) & (column < 6), 1.0, 0.0).astype(jnp.bfloat16)
    row = lax.broadcasted_iota(jnp.int32, (8, BLOCK), 0)
    lead = jnp.where(row < 3, 1.0, 0.0).astype(jnp.bfloat16)
    for axis in range(3):
        rows = slice(chans + 8 * axis, chans + 8 * axis + 8)
        for start in range(0, 3 * width, 4 * BLOCK):
            span = slice(start, start + 4 * BLOCK)
            pos_ref[axis, :, span] = jnp.dot(pick, ext_ref[rows, span], **f32)
    for block in range(count):
        at = pl.multiple_of((nblocks + first + block) * BLOCK, BLOCK)
        for axis in range(3):
            rows = ext_ref[chans + 8 * axis : chans + 8 * axis + 8, pl.ds(at, BLOCK)].astype(jnp.float32)
            swapped = jnp.concatenate([-rows[3:6], rows[0:3], rows[6:8]], axis=0)
            own_ref[block, axis] = jnp.dot(swapped.T.astype(jnp.bfloat16), lead, **f32)
        sum_ref[block] = jnp.zeros((chans, BLOCK), jnp.float32)
        weights_ref[block] = jnp.zeros(weights_ref.shape[1:], jnp.bfloat16)
        near_ref[block] = jnp.zeros(near_ref.shape[1:], jnp.bfloat16)
    exponent = -2.0 * math.log2(math.e)
    part_rows = 16

    def add_up(block):
        sum_ref[block] += lax.dot_general(near_ref[block], weights_ref[block], NT, **f32)

    def slots_step(step, carried):
        for block in range(count):
            add_up(block)
        for block in range(count):
            for part in range(unroll):
                slot = step * unroll + part
                entry = idx_ref[first + block, slot]
                where = jnp.bitwise_and(entry + (regions + 1 - here) * nblocks, regions * nblocks - 1)
                span = pl.ds(pl.multiple_of(where * BLOCK, BLOCK), BLOCK)
                to = slice(part * BLOCK, (part + 1) * BLOCK)
                used = live_ref[first + block, slot].astype(jnp.float32)
                mapped = ext_ref[:chans, span].astype(jnp.float32) * used
                near_ref[block, :, to] = mapped.astype(jnp.bfloat16)
                minus = [jnp.tile(pos_ref[axis, :, span], (part_rows // 8, 1)) for axis in range(3)]
                for start in range(0, BLOCK, part_rows):
                    rows = slice(start, start + part_rows)
                    total = None
                    for axis in range(3):
                        diff = own_ref[block, axis, rows, :] + minus[axis]
                        diff = diff - jnp.round(diff)
                        term = diff * diff
                        if axis == 0:
                            term = term * (scale_x * scale_x)
                        total = term if total is None else total + term
                    weights_ref[block, rows, to] = jnp.exp2(total * exponent).astype(jnp.bfloat16)
        return carried

    lax.fori_loop(0, slots // unroll, slots_step, 0)
    outer = first_ref[: 2 * chans, :]
    third_ref[...] = first_ref[2 * chans :, :].astype(jnp.float32).T.astype(jnp.bfloat16)
    for block in range(count):
        add_up(block)
        span = slice(block * BLOCK, (block + 1) * BLOCK)
        msg = (sum_ref[block] * MSG_SCALE).astype(jnp.bfloat16)
        known = jnp.concatenate([share_ref[:, span], msg], axis=0)
        inner_ref[:, span] = lax.dot_general(outer, known, TN, **f32)


def pairs(place, live_blocks, neighbours, live_slots, prev, own, following, h, first, second, count, regions):
    rows, width = own.shape
    chans = h.shape[0]
    hidden = first.shape[1]
    slots = neighbours.shape[1]
    share = count * BLOCK
    work = slots * share * BLOCK
    unroll = 3 if slots % 3 == 0 else 1
    return pl.pallas_call(
        functools.partial(pairs_kernel, float(regions), regions, unroll),
        out_shape=(
            jax.ShapeDtypeStruct((hidden, share), jnp.float32),
            jax.ShapeDtypeStruct((chans, share), jnp.bfloat16),
            jax.ShapeDtypeStruct((8, share), jnp.float32),
            jax.ShapeDtypeStruct((hidden, chans), jnp.bfloat16),
            jax.ShapeDtypeStruct(second.shape, jnp.bfloat16),
        ),
        in_specs=[SMEM_SPEC] * 4 + [ANY_SPEC] * 2 + [HBM_SPEC] * 4,
        out_specs=(VMEM_SPEC,) * 5,
        scratch_shapes=[
            pltpu.VMEM((rows, 3 * width), jnp.bfloat16),
            pltpu.VMEM(first.shape, jnp.bfloat16),
            pltpu.VMEM((count, 3, BLOCK, BLOCK), jnp.float32),
            pltpu.VMEM((3, 8, 3 * width), jnp.float32),
            pltpu.VMEM((count, BLOCK, unroll * BLOCK), jnp.bfloat16),
            pltpu.VMEM((count, chans, unroll * BLOCK), jnp.bfloat16),
            pltpu.VMEM((count, chans, BLOCK), jnp.float32),
            pltpu.SemaphoreType.DMA((6,)),
        ],
        compiler_params=PARAMS,
        cost_estimate=pl.CostEstimate(
            flops=work * (2 * chans + 20), bytes_accessed=6 * rows * width, transcendentals=work
        ),
        name="pairs",
    )(place, live_blocks, neighbours, live_slots, prev, following, *in_hbm(own, h, first, second))


def update_kernel(arrived_ref, inner_ref, share_ref, alive_ref, third_ref, second_ref, out_ref):
    potential = arrived_ref[0].astype(jnp.float32)
    for piece in range(1, arrived_ref.shape[0]):
        potential = potential + arrived_ref[piece].astype(jnp.float32)
    f32 = dict(preferred_element_type=jnp.float32)
    inner = inner_ref[...] + jnp.dot(third_ref[...], potential.astype(jnp.bfloat16), **f32)
    hidden = jax.nn.silu(inner).astype(jnp.bfloat16)
    out = share_ref[...].astype(jnp.float32) + jnp.dot(second_ref[...], hidden, **f32)
    new = jnp.where(alive_ref[0:1, :] > 0.0, out, 0.0).astype(jnp.bfloat16)
    for piece in range(out_ref.shape[0]):
        out_ref[piece] = new


def update(arrived, known):
    return pl.pallas_call(
        update_kernel,
        out_shape=jax.ShapeDtypeStruct(arrived.shape, jnp.bfloat16),
        in_specs=[VMEM_SPEC] * 6,
        out_specs=VMEM_SPEC,
        compiler_params=PARAMS,
        name="update",
    )(arrived, *known)


def laid_out(pieces, dim):
    lengths = list(pieces.shape[1:])
    lengths[dim] *= pieces.shape[0]
    return jnp.moveaxis(pieces, 0, dim).reshape(lengths)


def from_others(pieces, axis):
    return lax.all_to_all(pieces, axis, 0, 0, tiled=True)


def local(
    features,
    coords,
    neighbours,
    live_slots,
    block_count,
    kvec,
    msg_weight,
    filter_weight,
    mlp_in,
    mlp_out,
):
    chans, width = features.shape
    nblocks = width // BLOCK
    regions = lax.axis_size("atoms")
    groups_waves = lax.axis_size("waves")
    here = lax.axis_index("atoms")
    per_group = nblocks // groups_waves
    first = lax.axis_index("waves") * per_group
    place = jnp.stack([here, first]).astype(jnp.int32)
    total = regions * width
    waves = kvec.shape[1]
    low, high, partial_factor, carry, gain_rows, mixing = structure(
        place, block_count, kvec, coords, features, msg_weight[0], filter_weight[0], 1.0 / math.sqrt(total), regions
    )
    arrived = from_others(partial_factor, "atoms")
    prev = lax.ppermute(carry, "atoms", [(i, (i + 1) % regions) for i in range(regions)])
    following = lax.ppermute(carry, "atoms", [((i + 1) % regions, i) for i in range(regions)])
    everyone = spectral(arrived, gain_rows, mixing)
    filtered = from_others(everyone, "atoms").reshape(waves, 2 * chans)
    partial_potential = potentials(filtered, low, high, groups_waves)
    potential = from_others(partial_potential, "waves")
    known = pairs(
        place, block_count, neighbours.T, live_slots.T, prev, carry, following,
        features, mlp_in[0].T, mlp_out[0], per_group, regions,
    )
    new = update(potential, known)
    return laid_out(from_others(new, "waves"), 1)


def solution(mesh):
    in_specs = (
        P(None, "atoms"),
        P(None, "atoms"),
        P(None, "atoms"),
        P(None, "atoms"),
        P("atoms"),
        P(None, "waves"),
        P(),
        P(),
        P(),
        P(),
    )
    out_specs = P(None, "atoms")
    return jax.shard_map(local, mesh=mesh, in_specs=in_specs, out_specs=out_specs, check_vma=False)
```

```python
import functools
import math

import jax
import jax.numpy as jnp
from jax import lax
from jax.experimental import pallas as pl
from jax.experimental.pallas import tpu as pltpu
from jax.sharding import PartitionSpec as P


K = 4096
BLOCK = 128

MSG_SCALE = 0.125
GAIN_TOP = 20.0
ALPHA = 8.0**0.25
SIN_COEFS = tuple(ALPHA / math.sqrt(2.0) * c for c in (2.221430356581745, -0.9131746556274619, 0.10983828651966959))
TILE = 256
ROWS = 128
LIMIT = 16 * 2**20
VMEM_SPEC = pl.BlockSpec(memory_space=pltpu.VMEM)
SMEM_SPEC = pl.BlockSpec(memory_space=pltpu.SMEM)
ANY_SPEC = pl.BlockSpec(memory_space=pl.ANY)
HBM_SPEC = pl.BlockSpec(memory_space=pltpu.HBM)
PARAMS = pltpu.CompilerParams(vmem_limit_bytes=LIMIT)
NT = (((1,), (1,)), ((), ()))
TN = (((0,), (0,)), ((), ()))


def kept_rows(waves):
    return waves * 3 // 4


def phases_of(turns):
    r = turns - jnp.round(turns)
    u = r * r
    s = r * ((SIN_COEFS[2] * u + SIN_COEFS[1]) * u + SIN_COEFS[0])
    q = s * s
    w = math.sqrt(8.0) - q
    return 1.0 - q * w, (s * (w * lax.rsqrt(w))) * (math.sqrt(2.0) - q)


def three_pieces(values):
    first = values.astype(jnp.bfloat16)
    rest = values - first.astype(jnp.float32)
    second = rest.astype(jnp.bfloat16)
    third = (rest - second.astype(jnp.float32)).astype(jnp.bfloat16)
    return first.astype(jnp.float32), second.astype(jnp.float32), third.astype(jnp.float32)


def structure_kernel(
    scale, regions, place_ref, count_ref, kvec_in, coords_in, h_in, weight_in, mixing_in,
    low_ref, high_out, out_ref, carry_out, gain_ref, mixing_ref,
    kvec_ref, coords_ref, h_ref, weight_ref, ka_ref, masked_ref, high_ref, carry_ref, in_sems, sems,
):
    waves = kvec_ref.shape[1]
    chans, atoms = h_ref.shape
    kept = low_ref.shape[0]
    owned = out_ref.shape[1]
    f32 = dict(preferred_element_type=jnp.float32)
    taken = [
        pltpu.make_async_copy(source, target, in_sems.at[at])
        for at, (source, target) in enumerate(
            (
                (kvec_in, kvec_ref),
                (coords_in, coords_ref),
                (h_in, h_ref),
                (weight_in, weight_ref),
                (mixing_in, mixing_ref),
            )
        )
    ]
    for copy in taken:
        copy.start()
    taken[0].wait()
    kf = kvec_ref[...].astype(jnp.float32)
    ahead, behind = jnp.zeros((3, waves), jnp.float32), jnp.zeros((2, waves), jnp.float32)
    ka = jnp.concatenate([part for axis in range(3) for part in (ahead, *(-kf[axis : axis + 1],) * 3, behind)], axis=0)
    ka_ref[...] = ka.T.astype(jnp.bfloat16)
    kx = kf[0:1] / regions
    gain = GAIN_TOP / (4.0 + kx * kx + kf[1:2] * kf[1:2] + kf[2:3] * kf[2:3])
    lane = lax.broadcasted_iota(jnp.int32, (owned, waves), 1)
    own = lane == lax.broadcasted_iota(jnp.int32, (owned, waves), 0) + place_ref[0] * owned
    mine = jnp.sum(jnp.where(own, jnp.broadcast_to(gain, (owned, waves)), 0.0), axis=1, keepdims=True)
    gain_ref[...] = jnp.broadcast_to(mine * scale, gain_ref.shape)
    taken[1].wait()
    pieces = three_pieces(coords_ref[...])
    ones, gap = jnp.ones((3, atoms), jnp.float32), jnp.zeros((2, atoms), jnp.float32)
    for axis in range(3):
        rows = jnp.concatenate([ones, *(-piece[axis : axis + 1] for piece in pieces), gap], axis=0)
        carry_ref[chans + 8 * axis : chans + 8 * axis + 8, :] = rows.astype(jnp.bfloat16)
    for copy in taken[2:]:
        copy.wait()
    live_atoms = count_ref[0] * BLOCK
    atom = lax.broadcasted_iota(jnp.int32, (chans, atoms), 1)
    masked_ref[...] = jnp.where(atom < live_atoms, h_ref[...].astype(jnp.float32), 0.0).astype(jnp.bfloat16)
    zero = jnp.zeros((chans, TILE), jnp.bfloat16)
    sums = {}

    def add_up(place, at, row, start):
        ht = masked_ref[:, start : start + TILE]
        cosv = place[at : at + ROWS, start : start + TILE]
        sinv = place[at : at + ROWS, atoms + start : atoms + start + TILE]
        term = lax.dot_general(cosv, jnp.concatenate([ht, zero], axis=0), NT, **f32)
        term = term + lax.dot_general(sinv, jnp.concatenate([zero, ht], axis=0), NT, **f32)
        sums[row] = term if start == 0 else sums[row] + term
        if start + TILE == atoms:
            whole = sums.pop(row).astype(jnp.bfloat16)
            out_ref[row // owned : (row + ROWS) // owned] = whole.reshape(ROWS // owned, owned, 2 * chans)

    pending = []
    copies = []
    for row in [*range(kept, waves, ROWS), *range(0, kept, ROWS)]:
        place, at = (low_ref, row) if row < kept else (high_ref, row - kept)
        if row == 0:
            copies = [
                pltpu.make_async_copy(high_ref, high_out, sems.at[0]),
                pltpu.make_async_copy(carry_ref, carry_out, sems.at[1]),
            ]
            for copy in copies:
                copy.start()
        for start in range(0, atoms, TILE):
            cos_span = slice(start, start + TILE)
            sin_span = slice(atoms + start, atoms + start + TILE)
            turns = jnp.dot(ka_ref[row : row + ROWS, :], carry_ref[chans:, cos_span], **f32)
            cosv, sinv = phases_of(turns)
            place[at : at + ROWS, cos_span] = cosv.astype(jnp.bfloat16)
            place[at : at + ROWS, sin_span] = sinv.astype(jnp.bfloat16)
            if row == kept:
                carry_ref[:chans, cos_span] = jnp.dot(weight_ref[...], h_ref[:, cos_span], **f32).astype(jnp.bfloat16)
            pending.append((place, at, row, start))
            if len(pending) > 1:
                add_up(*pending.pop(0))
    add_up(*pending.pop(0))
    for copy in copies:
        copy.wait()


def in_hbm(*arrays):
    return tuple(pltpu.with_memory_space_constraint(array, pltpu.HBM) for array in arrays)


def structure(place, count, kvec, coords, h, weight, mixing, scale, regions):
    waves, atoms, chans = kvec.shape[1], coords.shape[1], h.shape[0]
    kept = kept_rows(waves)
    owned = waves // regions
    return pl.pallas_call(
        functools.partial(structure_kernel, scale, float(regions)),
        out_shape=(
            jax.ShapeDtypeStruct((kept, 2 * atoms), jnp.bfloat16),
            pltpu.HBM((waves - kept, 2 * atoms), jnp.bfloat16),
            jax.ShapeDtypeStruct((regions, owned, 2 * chans), jnp.bfloat16),
            pltpu.HBM((chans + 24, atoms), jnp.bfloat16),
            jax.ShapeDtypeStruct((owned, 2 * chans), jnp.float32),
            jax.ShapeDtypeStruct(mixing.shape, jnp.float32),
        ),
        in_specs=[SMEM_SPEC] * 2 + [HBM_SPEC] * 5,
        out_specs=(VMEM_SPEC, HBM_SPEC, VMEM_SPEC, HBM_SPEC, VMEM_SPEC, VMEM_SPEC),
        scratch_shapes=[
            pltpu.VMEM(kvec.shape, jnp.int32),
            pltpu.VMEM(coords.shape, jnp.float32),
            pltpu.VMEM(h.shape, jnp.bfloat16),
            pltpu.VMEM(weight.shape, jnp.bfloat16),
            pltpu.VMEM((waves, 24), jnp.bfloat16),
            pltpu.VMEM(h.shape, jnp.bfloat16),
            pltpu.VMEM((waves - kept, 2 * atoms), jnp.bfloat16),
            pltpu.VMEM((chans + 24, atoms), jnp.bfloat16),
            pltpu.SemaphoreType.DMA((5,)),
            pltpu.SemaphoreType.DMA((2,)),
        ],
        compiler_params=PARAMS,
        name="structure",
    )(place, count, *in_hbm(kvec, coords, h, weight, mixing))


def spectral_kernel(arrived_ref, gain_ref, mixing_ref, out_ref):
    chans = mixing_ref.shape[0]
    factor = arrived_ref[0].astype(jnp.float32)
    for piece in range(1, arrived_ref.shape[0]):
        factor = factor + arrived_ref[piece].astype(jnp.float32)
    high = dict(precision=lax.Precision.HIGHEST, preferred_element_type=jnp.float32)
    mixing = mixing_ref[...]
    cos_part = jnp.dot(factor[:, :chans], mixing, **high)
    sin_part = jnp.dot(factor[:, chans:], mixing, **high)
    filtered = (jnp.concatenate([cos_part, sin_part], axis=1) * gain_ref[...]).astype(jnp.bfloat16)
    for piece in range(out_ref.shape[0]):
        out_ref[piece] = filtered


def spectral(arrived, gain, mixing):
    return pl.pallas_call(
        spectral_kernel,
        out_shape=jax.ShapeDtypeStruct(arrived.shape, jnp.bfloat16),
        in_specs=[VMEM_SPEC] * 3,
        out_specs=VMEM_SPEC,
        compiler_params=PARAMS,
        name="spectral",
    )(arrived, gain, mixing)


def potentials_kernel(filtered_ref, low_ref, high_in, out_ref, high_ref, across_ref, sum_ref, sem):
    chans = out_ref.shape[1]
    pieces, _, width = out_ref.shape
    atoms = pieces * width
    kept, waves = low_ref.shape[0], filtered_ref.shape[0]
    copy = pltpu.make_async_copy(high_in, high_ref, sem)
    copy.start()
    across_ref[...] = filtered_ref[...].astype(jnp.float32).T.astype(jnp.bfloat16)

    def term(rows, table, piece):
        cos_span = slice(piece * width, (piece + 1) * width)
        sin_span = slice(atoms + piece * width, atoms + (piece + 1) * width)
        f32 = dict(preferred_element_type=jnp.float32)
        return jnp.dot(across_ref[:chans, rows], table[:, cos_span], **f32) + jnp.dot(
            across_ref[chans:, rows], table[:, sin_span], **f32
        )

    for piece in range(pieces):
        sum_ref[piece] = term(slice(0, kept), low_ref, piece)
    copy.wait()
    for piece in range(pieces):
        whole = sum_ref[piece] + term(slice(kept, waves), high_ref, piece)
        out_ref[piece] = (whole * (1.0 / math.sqrt(K))).astype(jnp.bfloat16)


def potentials(filtered, low, high, pieces):
    chans = filtered.shape[1] // 2
    atoms = low.shape[1] // 2
    return pl.pallas_call(
        potentials_kernel,
        out_shape=jax.ShapeDtypeStruct((pieces, chans, atoms // pieces), jnp.bfloat16),
        in_specs=[VMEM_SPEC, VMEM_SPEC, HBM_SPEC],
        out_specs=VMEM_SPEC,
        scratch_shapes=[
            pltpu.VMEM(high.shape, jnp.bfloat16),
            pltpu.VMEM((2 * chans, filtered.shape[0]), jnp.bfloat16),
            pltpu.VMEM((pieces, chans, atoms // pieces), jnp.float32),
            pltpu.SemaphoreType.DMA,
        ],
        compiler_params=PARAMS,
        name="potentials",
    )(filtered, low, *in_hbm(high))


def pairs_kernel(
    scale_x, regions, unroll, place_ref, count_ref, idx_ref, live_ref, prev_in, next_in, own_in, h_in, first_in, second_in,
    inner_ref, share_ref, alive_ref, third_ref, second_ref,
    ext_ref, first_ref, own_ref, pos_ref, weights_ref, near_ref, sum_ref, sems,
):
    chans = h_in.shape[0]
    width = own_in.shape[1]
    nblocks = width // BLOCK
    slots = idx_ref.shape[1]
    count = share_ref.shape[1] // BLOCK
    here = place_ref[0]
    first = place_ref[1]
    share = pl.ds(pl.multiple_of(first * BLOCK, BLOCK), count * BLOCK)
    moves = []
    for rows in (pl.ds(chans, ext_ref.shape[0] - chans), pl.ds(0, chans)):
        for at, source in enumerate((prev_in, own_in, next_in)):
            moves.append((source.at[rows, :], ext_ref.at[rows, pl.ds(at * width, width)]))
    moves += [(h_in.at[:, share], share_ref), (first_in, first_ref), (second_in, second_ref)]
    copies = [pltpu.make_async_copy(source, target, sems.at[at]) for at, (source, target) in enumerate(moves)]
    for copy in copies:
        copy.start()
    atom = lax.broadcasted_iota(jnp.int32, alive_ref.shape, 1) + first * BLOCK
    alive_ref[...] = jnp.where(atom < count_ref[0] * BLOCK, 1.0, 0.0)
    for copy in copies[:3]:
        copy.wait()
    f32 = dict(preferred_element_type=jnp.float32)
    column = lax.broadcasted_iota(jnp.int32, (8, 8), 1)
    pick = jnp.where((column >= 3) & (column < 6), 1.0, 0.0).astype(jnp.bfloat16)
    row = lax.broadcasted_iota(jnp.int32, (8, BLOCK), 0)
    lead = jnp.where(row < 3, 1.0, 0.0).astype(jnp.bfloat16)
    for axis in range(3):
        rows = slice(chans + 8 * axis, chans + 8 * axis + 8)
        for start in range(0, 3 * width, 4 * BLOCK):
            span = slice(start, start + 4 * BLOCK)
            pos_ref[axis, :, span] = jnp.dot(pick, ext_ref[rows, span], **f32)
    for block in range(count):
        at = pl.multiple_of((nblocks + first + block) * BLOCK, BLOCK)
        for axis in range(3):
            rows = ext_ref[chans + 8 * axis : chans + 8 * axis + 8, pl.ds(at, BLOCK)].astype(jnp.float32)
            swapped = jnp.concatenate([-rows[3:6], rows[0:3], rows[6:8]], axis=0)
            own_ref[block, axis] = jnp.dot(swapped.T.astype(jnp.bfloat16), lead, **f32)
        sum_ref[block] = jnp.zeros((chans, BLOCK), jnp.float32)
        weights_ref[block] = jnp.zeros(weights_ref.shape[1:], jnp.bfloat16)
        near_ref[block] = jnp.zeros(near_ref.shape[1:], jnp.bfloat16)
    for copy in copies[3:6]:
        copy.wait()
    exponent = -2.0 * math.log2(math.e)
    part_rows = 16

    def add_up(block):
        sum_ref[block] += lax.dot_general(near_ref[block], weights_ref[block], NT, **f32)

    def slots_step(step, carried):
        for block in range(count):
            add_up(block)
        for block in range(count):
            for part in range(unroll):
                slot = step * unroll + part
                entry = idx_ref[first + block, slot]
                where = jnp.bitwise_and(entry + (regions + 1 - here) * nblocks, regions * nblocks - 1)
                span = pl.ds(pl.multiple_of(where * BLOCK, BLOCK), BLOCK)
                to = slice(part * BLOCK, (part + 1) * BLOCK)
                used = live_ref[first + block, slot].astype(jnp.float32)
                mapped = ext_ref[:chans, span].astype(jnp.float32) * used
                near_ref[block, :, to] = mapped.astype(jnp.bfloat16)
                minus = [jnp.tile(pos_ref[axis, :, span], (part_rows // 8, 1)) for axis in range(3)]
                for start in range(0, BLOCK, part_rows):
                    rows = slice(start, start + part_rows)
                    total = None
                    for axis in range(3):
                        diff = own_ref[block, axis, rows, :] + minus[axis]
                        diff = diff - jnp.round(diff)
                        term = diff * diff
                        if axis == 0:
                            term = term * (scale_x * scale_x)
                        total = term if total is None else total + term
                    weights_ref[block, rows, to] = jnp.exp2(total * exponent).astype(jnp.bfloat16)
        return carried

    lax.fori_loop(0, slots // unroll, slots_step, 0)
    for copy in copies[6:]:
        copy.wait()
    outer = first_ref[: 2 * chans, :]
    third_ref[...] = first_ref[2 * chans :, :].astype(jnp.float32).T.astype(jnp.bfloat16)
    for block in range(count):
        add_up(block)
        span = slice(block * BLOCK, (block + 1) * BLOCK)
        msg = (sum_ref[block] * MSG_SCALE).astype(jnp.bfloat16)
        known = jnp.concatenate([share_ref[:, span], msg], axis=0)
        inner_ref[:, span] = lax.dot_general(outer, known, TN, **f32)


def pairs(place, live_blocks, neighbours, live_slots, prev, own, following, h, first, second, count, regions):
    rows, width = own.shape
    chans = h.shape[0]
    hidden = first.shape[1]
    slots = neighbours.shape[1]
    share = count * BLOCK
    work = slots * share * BLOCK
    unroll = 3 if slots % 3 == 0 else 1
    return pl.pallas_call(
        functools.partial(pairs_kernel, float(regions), regions, unroll),
        out_shape=(
            jax.ShapeDtypeStruct((hidden, share), jnp.float32),
            jax.ShapeDtypeStruct((chans, share), jnp.bfloat16),
            jax.ShapeDtypeStruct((8, share), jnp.float32),
            jax.ShapeDtypeStruct((hidden, chans), jnp.bfloat16),
            jax.ShapeDtypeStruct(second.shape, jnp.bfloat16),
        ),
        in_specs=[SMEM_SPEC] * 4 + [ANY_SPEC] * 2 + [HBM_SPEC] * 4,
        out_specs=(VMEM_SPEC,) * 5,
        scratch_shapes=[
            pltpu.VMEM((rows, 3 * width), jnp.bfloat16),
            pltpu.VMEM(first.shape, jnp.bfloat16),
            pltpu.VMEM((count, 3, BLOCK, BLOCK), jnp.float32),
            pltpu.VMEM((3, 8, 3 * width), jnp.float32),
            pltpu.VMEM((count, BLOCK, unroll * BLOCK), jnp.bfloat16),
            pltpu.VMEM((count, chans, unroll * BLOCK), jnp.bfloat16),
            pltpu.VMEM((count, chans, BLOCK), jnp.float32),
            pltpu.SemaphoreType.DMA((9,)),
        ],
        compiler_params=PARAMS,
        cost_estimate=pl.CostEstimate(
            flops=work * (2 * chans + 20), bytes_accessed=6 * rows * width, transcendentals=work
        ),
        name="pairs",
    )(place, live_blocks, neighbours, live_slots, prev, following, *in_hbm(own, h, first, second))


def update_kernel(arrived_ref, inner_ref, share_ref, alive_ref, third_ref, second_ref, out_ref):
    potential = arrived_ref[0].astype(jnp.float32)
    for piece in range(1, arrived_ref.shape[0]):
        potential = potential + arrived_ref[piece].astype(jnp.float32)
    f32 = dict(preferred_element_type=jnp.float32)
    inner = inner_ref[...] + jnp.dot(third_ref[...], potential.astype(jnp.bfloat16), **f32)
    hidden = jax.nn.silu(inner).astype(jnp.bfloat16)
    out = share_ref[...].astype(jnp.float32) + jnp.dot(second_ref[...], hidden, **f32)
    new = jnp.where(alive_ref[0:1, :] > 0.0, out, 0.0).astype(jnp.bfloat16)
    for piece in range(out_ref.shape[0]):
        out_ref[piece] = new


def update(arrived, known):
    return pl.pallas_call(
        update_kernel,
        out_shape=jax.ShapeDtypeStruct(arrived.shape, jnp.bfloat16),
        in_specs=[VMEM_SPEC] * 6,
        out_specs=VMEM_SPEC,
        compiler_params=PARAMS,
        name="update",
    )(arrived, *known)


def laid_out(pieces, dim):
    lengths = list(pieces.shape[1:])
    lengths[dim] *= pieces.shape[0]
    return jnp.moveaxis(pieces, 0, dim).reshape(lengths)


def from_others(pieces, axis):
    return lax.all_to_all(pieces, axis, 0, 0, tiled=True)


def local(
    features,
    coords,
    neighbours,
    live_slots,
    block_count,
    kvec,
    msg_weight,
    filter_weight,
    mlp_in,
    mlp_out,
):
    chans, width = features.shape
    nblocks = width // BLOCK
    regions = lax.axis_size("atoms")
    groups_waves = lax.axis_size("waves")
    here = lax.axis_index("atoms")
    per_group = nblocks // groups_waves
    first = lax.axis_index("waves") * per_group
    place = jnp.stack([here, first]).astype(jnp.int32)
    total = regions * width
    waves = kvec.shape[1]
    low, high, partial_factor, carry, gain_rows, mixing = structure(
        place, block_count, kvec, coords, features, msg_weight[0], filter_weight[0], 1.0 / math.sqrt(total), regions
    )
    arrived = from_others(partial_factor, "atoms")
    prev = lax.ppermute(carry, "atoms", [(i, (i + 1) % regions) for i in range(regions)])
    following = lax.ppermute(carry, "atoms", [((i + 1) % regions, i) for i in range(regions)])
    everyone = spectral(arrived, gain_rows, mixing)
    filtered = from_others(everyone, "atoms").reshape(waves, 2 * chans)
    partial_potential = potentials(filtered, low, high, groups_waves)
    potential = from_others(partial_potential, "waves")
    known = pairs(
        place, block_count, neighbours.T, live_slots.T, prev, carry, following,
        features, mlp_in[0].T, mlp_out[0], per_group, regions,
    )
    new = update(potential, known)
    return laid_out(from_others(new, "waves"), 1)


def solution(mesh):
    in_specs = (
        P(None, "atoms"),
        P(None, "atoms"),
        P(None, "atoms"),
        P(None, "atoms"),
        P("atoms"),
        P(None, "waves"),
        P(),
        P(),
        P(),
        P(),
    )
    out_specs = P(None, "atoms")
    return jax.shard_map(local, mesh=mesh, in_specs=in_specs, out_specs=out_specs, check_vma=False)
```

```python
import functools
import math

import jax
import jax.numpy as jnp
from jax import lax
from jax.experimental import pallas as pl
from jax.experimental.pallas import tpu as pltpu
from jax.sharding import PartitionSpec as P


K = 4096
BLOCK = 128

MSG_SCALE = 0.125
GAIN_TOP = 20.0
ALPHA = 8.0**0.25
SIN_COEFS = tuple(ALPHA / math.sqrt(2.0) * c for c in (2.221430356581745, -0.9131746556274619, 0.10983828651966959))
TILE = 256
ROWS = 128
LIMIT = 16 * 2**20
VMEM_SPEC = pl.BlockSpec(memory_space=pltpu.VMEM)
SMEM_SPEC = pl.BlockSpec(memory_space=pltpu.SMEM)
ANY_SPEC = pl.BlockSpec(memory_space=pl.ANY)
HBM_SPEC = pl.BlockSpec(memory_space=pltpu.HBM)
PARAMS = pltpu.CompilerParams(vmem_limit_bytes=LIMIT)
NT = (((1,), (1,)), ((), ()))
TN = (((0,), (0,)), ((), ()))


def kept_rows(waves):
    return waves * 3 // 4


def phases_of(turns):
    r = turns - jnp.round(turns)
    u = r * r
    s = r * ((SIN_COEFS[2] * u + SIN_COEFS[1]) * u + SIN_COEFS[0])
    q = s * s
    w = math.sqrt(8.0) - q
    return 1.0 - q * w, (s * (w * lax.rsqrt(w))) * (math.sqrt(2.0) - q)


def three_pieces(values):
    first = values.astype(jnp.bfloat16)
    rest = values - first.astype(jnp.float32)
    second = rest.astype(jnp.bfloat16)
    third = (rest - second.astype(jnp.float32)).astype(jnp.bfloat16)
    return first.astype(jnp.float32), second.astype(jnp.float32), third.astype(jnp.float32)


def structure_kernel(
    scale, regions, place_ref, count_ref, kvec_in, coords_in, h_in, weight_in, mixing_in,
    low_ref, high_out, out_ref, carry_out, gain_ref, mixing_ref,
    kvec_ref, coords_ref, h_ref, weight_ref, ka_ref, masked_ref, high_ref, carry_ref, in_sems, sems,
):
    waves = kvec_ref.shape[1]
    chans, atoms = h_ref.shape
    kept = low_ref.shape[0]
    owned = out_ref.shape[1]
    f32 = dict(preferred_element_type=jnp.float32)
    taken = [
        pltpu.make_async_copy(source, target, in_sems.at[at])
        for at, (source, target) in enumerate(
            (
                (kvec_in, kvec_ref),
                (coords_in, coords_ref),
                (h_in, h_ref),
                (weight_in, weight_ref),
                (mixing_in, mixing_ref),
            )
        )
    ]
    for copy in taken:
        copy.start()
    taken[0].wait()
    kf = kvec_ref[...].astype(jnp.float32)
    behind = jnp.zeros((5, waves), jnp.float32)
    ka = jnp.concatenate([-kf, behind] * 3, axis=0)
    ka_ref[...] = ka.T.astype(jnp.bfloat16)
    kx = kf[0:1] / regions
    gain = GAIN_TOP / (4.0 + kx * kx + kf[1:2] * kf[1:2] + kf[2:3] * kf[2:3])
    lane = lax.broadcasted_iota(jnp.int32, (owned, waves), 1)
    own = lane == lax.broadcasted_iota(jnp.int32, (owned, waves), 0) + place_ref[0] * owned
    mine = jnp.sum(jnp.where(own, jnp.broadcast_to(gain, (owned, waves)), 0.0), axis=1, keepdims=True)
    gain_ref[...] = jnp.broadcast_to(mine * scale, gain_ref.shape)
    taken[1].wait()
    gap = jnp.zeros((5, atoms), jnp.float32)
    for at, piece in enumerate(three_pieces(-coords_ref[...])):
        rows = jnp.concatenate([piece, gap], axis=0)
        carry_ref[chans + 8 * at : chans + 8 * at + 8, :] = rows.astype(jnp.bfloat16)
    for copy in taken[2:]:
        copy.wait()
    live_atoms = count_ref[0] * BLOCK
    atom = lax.broadcasted_iota(jnp.int32, (chans, atoms), 1)
    masked_ref[...] = jnp.where(atom < live_atoms, h_ref[...].astype(jnp.float32), 0.0).astype(jnp.bfloat16)
    zero = jnp.zeros((chans, TILE), jnp.bfloat16)
    sums = {}

    def add_up(place, at, row, start):
        ht = masked_ref[:, start : start + TILE]
        cosv = place[at : at + ROWS, start : start + TILE]
        sinv = place[at : at + ROWS, atoms + start : atoms + start + TILE]
        term = lax.dot_general(cosv, jnp.concatenate([ht, zero], axis=0), NT, **f32)
        term = term + lax.dot_general(sinv, jnp.concatenate([zero, ht], axis=0), NT, **f32)
        sums[row] = term if start == 0 else sums[row] + term
        if start + TILE == atoms:
            whole = sums.pop(row).astype(jnp.bfloat16)
            out_ref[row // owned : (row + ROWS) // owned] = whole.reshape(ROWS // owned, owned, 2 * chans)

    pending = []
    copies = []
    for row in [*range(kept, waves, ROWS), *range(0, kept, ROWS)]:
        place, at = (low_ref, row) if row < kept else (high_ref, row - kept)
        if row == 0:
            copies = [
                pltpu.make_async_copy(high_ref, high_out, sems.at[0]),
                pltpu.make_async_copy(carry_ref, carry_out, sems.at[1]),
            ]
            for copy in copies:
                copy.start()
        for start in range(0, atoms, TILE):
            cos_span = slice(start, start + TILE)
            sin_span = slice(atoms + start, atoms + start + TILE)
            turns = jnp.dot(ka_ref[row : row + ROWS, :], carry_ref[chans:, cos_span], **f32)
            cosv, sinv = phases_of(turns)
            place[at : at + ROWS, cos_span] = cosv.astype(jnp.bfloat16)
            place[at : at + ROWS, sin_span] = sinv.astype(jnp.bfloat16)
            if row == kept:
                carry_ref[:chans, cos_span] = jnp.dot(weight_ref[...], h_ref[:, cos_span], **f32).astype(jnp.bfloat16)
            pending.append((place, at, row, start))
            if len(pending) > 1:
                add_up(*pending.pop(0))
    add_up(*pending.pop(0))
    for copy in copies:
        copy.wait()


def in_hbm(*arrays):
    return tuple(pltpu.with_memory_space_constraint(array, pltpu.HBM) for array in arrays)


def structure(place, count, kvec, coords, h, weight, mixing, scale, regions):
    waves, atoms, chans = kvec.shape[1], coords.shape[1], h.shape[0]
    kept = kept_rows(waves)
    owned = waves // regions
    return pl.pallas_call(
        functools.partial(structure_kernel, scale, float(regions)),
        out_shape=(
            jax.ShapeDtypeStruct((kept, 2 * atoms), jnp.bfloat16),
            pltpu.HBM((waves - kept, 2 * atoms), jnp.bfloat16),
            jax.ShapeDtypeStruct((regions, owned, 2 * chans), jnp.bfloat16),
            pltpu.HBM((chans + 24, atoms), jnp.bfloat16),
            jax.ShapeDtypeStruct((owned, 2 * chans), jnp.float32),
            jax.ShapeDtypeStruct(mixing.shape, jnp.float32),
        ),
        in_specs=[SMEM_SPEC] * 2 + [HBM_SPEC] * 5,
        out_specs=(VMEM_SPEC, HBM_SPEC, VMEM_SPEC, HBM_SPEC, VMEM_SPEC, VMEM_SPEC),
        scratch_shapes=[
            pltpu.VMEM(kvec.shape, jnp.int32),
            pltpu.VMEM(coords.shape, jnp.float32),
            pltpu.VMEM(h.shape, jnp.bfloat16),
            pltpu.VMEM(weight.shape, jnp.bfloat16),
            pltpu.VMEM((waves, 24), jnp.bfloat16),
            pltpu.VMEM(h.shape, jnp.bfloat16),
            pltpu.VMEM((waves - kept, 2 * atoms), jnp.bfloat16),
            pltpu.VMEM((chans + 24, atoms), jnp.bfloat16),
            pltpu.SemaphoreType.DMA((5,)),
            pltpu.SemaphoreType.DMA((2,)),
        ],
        compiler_params=PARAMS,
        name="structure",
    )(place, count, *in_hbm(kvec, coords, h, weight, mixing))


def spectral_kernel(arrived_ref, gain_ref, mixing_ref, out_ref):
    chans = mixing_ref.shape[0]
    factor = arrived_ref[0].astype(jnp.float32)
    for piece in range(1, arrived_ref.shape[0]):
        factor = factor + arrived_ref[piece].astype(jnp.float32)
    high = dict(precision=lax.Precision.HIGHEST, preferred_element_type=jnp.float32)
    mixing = mixing_ref[...]
    cos_part = jnp.dot(factor[:, :chans], mixing, **high)
    sin_part = jnp.dot(factor[:, chans:], mixing, **high)
    filtered = (jnp.concatenate([cos_part, sin_part], axis=1) * gain_ref[...]).astype(jnp.bfloat16)
    for piece in range(out_ref.shape[0]):
        out_ref[piece] = filtered


def spectral(arrived, gain, mixing):
    return pl.pallas_call(
        spectral_kernel,
        out_shape=jax.ShapeDtypeStruct(arrived.shape, jnp.bfloat16),
        in_specs=[VMEM_SPEC] * 3,
        out_specs=VMEM_SPEC,
        compiler_params=PARAMS,
        name="spectral",
    )(arrived, gain, mixing)


def potentials_kernel(
    filtered_ref, low_ref, high_in, prev_in, next_in, own_in,
    out_ref, pos_ref, high_ref, rows_ref, across_ref, sum_ref, sems,
):
    chans = out_ref.shape[1]
    pieces, _, width = out_ref.shape
    atoms = pieces * width
    kept, waves = low_ref.shape[0], filtered_ref.shape[0]
    region = own_in.shape[1]
    moves = [(high_in, high_ref)]
    for at, source in enumerate((prev_in, own_in, next_in)):
        moves.append((source.at[pl.ds(chans, 24), :], rows_ref.at[:, pl.ds(at * region, region)]))
    copies = [pltpu.make_async_copy(source, target, sems.at[at]) for at, (source, target) in enumerate(moves)]
    for copy in copies:
        copy.start()
    across_ref[...] = filtered_ref[...].astype(jnp.float32).T.astype(jnp.bfloat16)

    def term(rows, table, piece):
        cos_span = slice(piece * width, (piece + 1) * width)
        sin_span = slice(atoms + piece * width, atoms + (piece + 1) * width)
        f32 = dict(preferred_element_type=jnp.float32)
        return jnp.dot(across_ref[:chans, rows], table[:, cos_span], **f32) + jnp.dot(
            across_ref[chans:, rows], table[:, sin_span], **f32
        )

    for piece in range(pieces):
        sum_ref[piece] = term(slice(0, kept), low_ref, piece)
    for copy in copies:
        copy.wait()
    parts = [rows_ref[8 * at : 8 * at + 8, :].astype(jnp.float32) for at in range(3)]
    pos_ref[...] = (parts[2] + parts[1]) + parts[0]
    for piece in range(pieces):
        whole = sum_ref[piece] + term(slice(kept, waves), high_ref, piece)
        out_ref[piece] = (whole * (1.0 / math.sqrt(K))).astype(jnp.bfloat16)


def potentials(filtered, low, high, prev, following, own, pieces):
    chans = filtered.shape[1] // 2
    atoms = low.shape[1] // 2
    return pl.pallas_call(
        potentials_kernel,
        out_shape=(
            jax.ShapeDtypeStruct((pieces, chans, atoms // pieces), jnp.bfloat16),
            jax.ShapeDtypeStruct((8, 3 * atoms), jnp.float32),
        ),
        in_specs=[VMEM_SPEC, VMEM_SPEC, HBM_SPEC, ANY_SPEC, ANY_SPEC, HBM_SPEC],
        out_specs=(VMEM_SPEC, VMEM_SPEC),
        scratch_shapes=[
            pltpu.VMEM(high.shape, jnp.bfloat16),
            pltpu.VMEM((24, 3 * atoms), jnp.bfloat16),
            pltpu.VMEM((2 * chans, filtered.shape[0]), jnp.bfloat16),
            pltpu.VMEM((pieces, chans, atoms // pieces), jnp.float32),
            pltpu.SemaphoreType.DMA((4,)),
        ],
        compiler_params=PARAMS,
        name="potentials",
    )(filtered, low, *in_hbm(high), prev, following, *in_hbm(own))


def pairs_kernel(
    scale_x, regions, unroll, place_ref, count_ref, idx_ref, live_ref, pos_ref,
    prev_in, next_in, own_in, h_in, first_in, second_in,
    inner_ref, share_ref, alive_ref, third_ref, second_ref,
    ext_ref, first_ref, own_ref, weights_ref, near_ref, sum_ref, sems,
):
    chans, width = h_in.shape
    nblocks = width // BLOCK
    slots = idx_ref.shape[1]
    count = share_ref.shape[1] // BLOCK
    here = place_ref[0]
    first = place_ref[1]
    f32 = dict(preferred_element_type=jnp.float32)
    share = pl.ds(pl.multiple_of(first * BLOCK, BLOCK), count * BLOCK)
    moves = []
    for at, source in enumerate((prev_in, own_in, next_in)):
        moves.append((source.at[pl.ds(0, chans), :], ext_ref.at[:, pl.ds(at * width, width)]))
    moves += [(h_in.at[:, share], share_ref), (first_in, first_ref), (second_in, second_ref)]
    copies = [pltpu.make_async_copy(source, target, sems.at[at]) for at, (source, target) in enumerate(moves)]
    for copy in copies:
        copy.start()
    atom = lax.broadcasted_iota(jnp.int32, alive_ref.shape, 1) + first * BLOCK
    alive_ref[...] = jnp.where(atom < count_ref[0] * BLOCK, 1.0, 0.0)
    for block in range(count):
        at = pl.multiple_of((nblocks + first + block) * BLOCK, BLOCK)
        columns = -pos_ref[:, pl.ds(at, BLOCK)].T
        for axis in range(3):
            own_ref[block, axis] = jnp.broadcast_to(columns[:, axis : axis + 1], (BLOCK, BLOCK))
        sum_ref[block] = jnp.zeros((chans, BLOCK), jnp.float32)
    exponent = -2.0 * math.log2(math.e)
    part_rows = 16

    def span_of(block, slot):
        entry = idx_ref[first + block, slot]
        where = jnp.bitwise_and(entry + (regions + 1 - here) * nblocks, regions * nblocks - 1)
        return pl.ds(pl.multiple_of(where * BLOCK, BLOCK), BLOCK)

    def weigh(block, step):
        for part in range(unroll):
            span = span_of(block, step * unroll + part)
            to = slice(part * BLOCK, (part + 1) * BLOCK)
            minus = [jnp.broadcast_to(pos_ref[axis : axis + 1, span], (part_rows, BLOCK)) for axis in range(3)]
            for start in range(0, BLOCK, part_rows):
                rows = slice(start, start + part_rows)
                total = None
                for axis in range(3):
                    diff = own_ref[block, axis, rows, :] + minus[axis]
                    diff = diff - jnp.round(diff)
                    term = diff * diff
                    if axis == 0:
                        term = term * (scale_x * scale_x)
                    total = term if total is None else total + term
                weights_ref[block, rows, to] = jnp.exp2(total * exponent).astype(jnp.bfloat16)

    def add_up(block, step):
        for part in range(unroll):
            slot = step * unroll + part
            used = live_ref[first + block, slot].astype(jnp.float32)
            mapped = ext_ref[:, span_of(block, slot)].astype(jnp.float32) * used
            near_ref[block, :, part * BLOCK : (part + 1) * BLOCK] = mapped.astype(jnp.bfloat16)
        sum_ref[block] += lax.dot_general(near_ref[block], weights_ref[block], NT, **f32)

    steps = slots // unroll
    for block in range(count):
        weigh(block, 0)
    for copy in copies[:3]:
        copy.wait()

    def slots_step(step, carried):
        for block in range(count):
            add_up(block, step - 1)
            weigh(block, step)
        return carried

    lax.fori_loop(1, steps, slots_step, 0)
    for block in range(count):
        add_up(block, steps - 1)
    for copy in copies[3:]:
        copy.wait()
    outer = first_ref[: 2 * chans, :]
    third_ref[...] = first_ref[2 * chans :, :].astype(jnp.float32).T.astype(jnp.bfloat16)
    for block in range(count):
        span = slice(block * BLOCK, (block + 1) * BLOCK)
        msg = (sum_ref[block] * MSG_SCALE).astype(jnp.bfloat16)
        known = jnp.concatenate([share_ref[:, span], msg], axis=0)
        inner_ref[:, span] = lax.dot_general(outer, known, TN, **f32)


def pairs(place, live_blocks, neighbours, live_slots, positions, prev, own, following, h, first, second, count, regions):
    chans, width = h.shape
    hidden = first.shape[1]
    slots = neighbours.shape[1]
    share = count * BLOCK
    work = slots * share * BLOCK
    unroll = 3 if slots % 3 == 0 else 1
    return pl.pallas_call(
        functools.partial(pairs_kernel, float(regions), regions, unroll),
        out_shape=(
            jax.ShapeDtypeStruct((hidden, share), jnp.float32),
            jax.ShapeDtypeStruct((chans, share), jnp.bfloat16),
            jax.ShapeDtypeStruct((8, share), jnp.float32),
            jax.ShapeDtypeStruct((hidden, chans), jnp.bfloat16),
            jax.ShapeDtypeStruct(second.shape, jnp.bfloat16),
        ),
        in_specs=[SMEM_SPEC] * 4 + [VMEM_SPEC] + [ANY_SPEC] * 2 + [HBM_SPEC] * 4,
        out_specs=(VMEM_SPEC,) * 5,
        scratch_shapes=[
            pltpu.VMEM((chans, 3 * width), jnp.bfloat16),
            pltpu.VMEM(first.shape, jnp.bfloat16),
            pltpu.VMEM((count, 3, BLOCK, BLOCK), jnp.float32),
            pltpu.VMEM((count, BLOCK, unroll * BLOCK), jnp.bfloat16),
            pltpu.VMEM((count, chans, unroll * BLOCK), jnp.bfloat16),
            pltpu.VMEM((count, chans, BLOCK), jnp.float32),
            pltpu.SemaphoreType.DMA((6,)),
        ],
        compiler_params=PARAMS,
        cost_estimate=pl.CostEstimate(
            flops=work * (2 * chans + 20), bytes_accessed=6 * chans * width, transcendentals=work
        ),
        name="pairs",
    )(place, live_blocks, neighbours, live_slots, positions, prev, following, *in_hbm(own, h, first, second))


def update_kernel(arrived_ref, inner_ref, share_ref, alive_ref, third_ref, second_ref, out_ref):
    potential = arrived_ref[0].astype(jnp.float32)
    for piece in range(1, arrived_ref.shape[0]):
        potential = potential + arrived_ref[piece].astype(jnp.float32)
    f32 = dict(preferred_element_type=jnp.float32)
    inner = inner_ref[...] + jnp.dot(third_ref[...], potential.astype(jnp.bfloat16), **f32)
    hidden = jax.nn.silu(inner).astype(jnp.bfloat16)
    out = share_ref[...].astype(jnp.float32) + jnp.dot(second_ref[...], hidden, **f32)
    new = jnp.where(alive_ref[0:1, :] > 0.0, out, 0.0).astype(jnp.bfloat16)
    for piece in range(out_ref.shape[0]):
        out_ref[piece] = new


def update(arrived, known):
    return pl.pallas_call(
        update_kernel,
        out_shape=jax.ShapeDtypeStruct(arrived.shape, jnp.bfloat16),
        in_specs=[VMEM_SPEC] * 6,
        out_specs=VMEM_SPEC,
        compiler_params=PARAMS,
        name="update",
    )(arrived, *known)


def laid_out(pieces, dim):
    lengths = list(pieces.shape[1:])
    lengths[dim] *= pieces.shape[0]
    return jnp.moveaxis(pieces, 0, dim).reshape(lengths)


def from_others(pieces, axis):
    return lax.all_to_all(pieces, axis, 0, 0, tiled=True)


def local(
    features,
    coords,
    neighbours,
    live_slots,
    block_count,
    kvec,
    msg_weight,
    filter_weight,
    mlp_in,
    mlp_out,
):
    chans, width = features.shape
    nblocks = width // BLOCK
    regions = lax.axis_size("atoms")
    groups_waves = lax.axis_size("waves")
    here = lax.axis_index("atoms")
    per_group = nblocks // groups_waves
    first = lax.axis_index("waves") * per_group
    place = jnp.stack([here, first]).astype(jnp.int32)
    total = regions * width
    waves = kvec.shape[1]
    low, high, partial_factor, carry, gain_rows, mixing = structure(
        place, block_count, kvec, coords, features, msg_weight[0], filter_weight[0], 1.0 / math.sqrt(total), regions
    )
    arrived = from_others(partial_factor, "atoms")
    prev = lax.ppermute(carry, "atoms", [(i, (i + 1) % regions) for i in range(regions)])
    following = lax.ppermute(carry, "atoms", [((i + 1) % regions, i) for i in range(regions)])
    everyone = spectral(arrived, gain_rows, mixing)
    filtered = from_others(everyone, "atoms").reshape(waves, 2 * chans)
    partial_potential, positions = potentials(filtered, low, high, prev, following, carry, groups_waves)
    potential = from_others(partial_potential, "waves")
    known = pairs(
        place, block_count, neighbours.T, live_slots.T, positions, prev, carry, following,
        features, mlp_in[0].T, mlp_out[0], per_group, regions,
    )
    new = update(potential, known)
    return laid_out(from_others(new, "waves"), 1)


def solution(mesh):
    in_specs = (
        P(None, "atoms"),
        P(None, "atoms"),
        P(None, "atoms"),
        P(None, "atoms"),
        P("atoms"),
        P(None, "waves"),
        P(),
        P(),
        P(),
        P(),
    )
    out_specs = P(None, "atoms")
    return jax.shard_map(local, mesh=mesh, in_specs=in_specs, out_specs=out_specs, check_vma=False)
```

```python
import functools
import math

import jax
import jax.numpy as jnp
from jax import lax
from jax.experimental import pallas as pl
from jax.experimental.pallas import tpu as pltpu
from jax.sharding import PartitionSpec as P


K = 4096
BLOCK = 128

MSG_SCALE = 0.125
GAIN_TOP = 20.0
ALPHA = 8.0**0.25
SIN_COEFS = tuple(ALPHA / math.sqrt(2.0) * c for c in (2.221430356581745, -0.9131746556274619, 0.10983828651966959))
TILE = 256
ROWS = 128
LIMIT = 16 * 2**20
VMEM_SPEC = pl.BlockSpec(memory_space=pltpu.VMEM)
SMEM_SPEC = pl.BlockSpec(memory_space=pltpu.SMEM)
ANY_SPEC = pl.BlockSpec(memory_space=pl.ANY)
HBM_SPEC = pl.BlockSpec(memory_space=pltpu.HBM)
PARAMS = pltpu.CompilerParams(vmem_limit_bytes=LIMIT)
NT = (((1,), (1,)), ((), ()))
TN = (((0,), (0,)), ((), ()))


def kept_rows(waves):
    return waves * 3 // 4


def phases_of(turns):
    r = turns - jnp.round(turns)
    u = r * r
    s = r * ((SIN_COEFS[2] * u + SIN_COEFS[1]) * u + SIN_COEFS[0])
    q = s * s
    w = math.sqrt(8.0) - q
    return 1.0 - q * w, (s * (w * lax.rsqrt(w))) * (math.sqrt(2.0) - q)


def three_pieces(values):
    first = values.astype(jnp.bfloat16)
    rest = values - first.astype(jnp.float32)
    second = rest.astype(jnp.bfloat16)
    third = (rest - second.astype(jnp.float32)).astype(jnp.bfloat16)
    return first.astype(jnp.float32), second.astype(jnp.float32), third.astype(jnp.float32)


def structure_kernel(
    scale, regions, place_ref, count_ref, kvec_in, coords_in, h_in, weight_in, mixing_in,
    low_ref, high_out, kept_ref, sent_ref, carry_out, gain_ref, mixing_ref,
    kvec_ref, coords_ref, h_ref, weight_ref, ka_ref, masked_ref, high_ref, carry_ref, whole_ref, gains_ref, in_sems, sems,
):
    waves = kvec_ref.shape[1]
    chans, atoms = h_ref.shape
    kept = low_ref.shape[0]
    half = kept_ref.shape[0]
    core = jnp.bitwise_and(place_ref[0], 1)
    mine = pl.ds(pl.multiple_of(core * half, half), half)
    theirs = pl.ds(pl.multiple_of((1 - core) * half, half), half)
    f32 = dict(preferred_element_type=jnp.float32)
    taken = [
        pltpu.make_async_copy(source, target, in_sems.at[at])
        for at, (source, target) in enumerate(
            (
                (kvec_in, kvec_ref),
                (coords_in, coords_ref),
                (h_in, h_ref),
                (weight_in, weight_ref),
                (mixing_in, mixing_ref),
            )
        )
    ]
    for copy in taken:
        copy.start()
    taken[0].wait()
    kf = kvec_ref[...].astype(jnp.float32)
    ahead, behind = jnp.zeros((3, waves), jnp.float32), jnp.zeros((2, waves), jnp.float32)
    ka = jnp.concatenate([part for axis in range(3) for part in (ahead, *(-kf[axis : axis + 1],) * 3, behind)], axis=0)
    ka_ref[...] = ka.T.astype(jnp.bfloat16)
    kx = kf[0:1] / regions
    gain = GAIN_TOP / (4.0 + kx * kx + kf[1:2] * kf[1:2] + kf[2:3] * kf[2:3])
    columns = jnp.broadcast_to(gain * scale, (8, waves)).T
    gains_ref[...] = jnp.broadcast_to(columns[:, 0:1], gains_ref.shape)
    gain_ref[...] = gains_ref[mine, :]
    taken[1].wait()
    pieces = three_pieces(coords_ref[...])
    ones, gap = jnp.ones((3, atoms), jnp.float32), jnp.zeros((2, atoms), jnp.float32)
    for axis in range(3):
        rows = jnp.concatenate([ones, *(-piece[axis : axis + 1] for piece in pieces), gap], axis=0)
        carry_ref[chans + 8 * axis : chans + 8 * axis + 8, :] = rows.astype(jnp.bfloat16)
    for copy in taken[2:]:
        copy.wait()
    live_atoms = count_ref[0] * BLOCK
    atom = lax.broadcasted_iota(jnp.int32, (chans, atoms), 1)
    masked_ref[...] = jnp.where(atom < live_atoms, h_ref[...].astype(jnp.float32), 0.0).astype(jnp.bfloat16)
    zero = jnp.zeros((chans, TILE), jnp.bfloat16)
    sums = {}

    def add_up(place, at, row, start):
        ht = masked_ref[:, start : start + TILE]
        cosv = place[at : at + ROWS, start : start + TILE]
        sinv = place[at : at + ROWS, atoms + start : atoms + start + TILE]
        term = lax.dot_general(cosv, jnp.concatenate([ht, zero], axis=0), NT, **f32)
        term = term + lax.dot_general(sinv, jnp.concatenate([zero, ht], axis=0), NT, **f32)
        sums[row] = term if start == 0 else sums[row] + term
        if start + TILE == atoms:
            whole_ref[row : row + ROWS, :] = sums.pop(row)

    pending = []
    copies = []
    for row in [*range(kept, waves, ROWS), *range(0, kept, ROWS)]:
        place, at = (low_ref, row) if row < kept else (high_ref, row - kept)
        if row == 0:
            copies = [
                pltpu.make_async_copy(high_ref, high_out, sems.at[0]),
                pltpu.make_async_copy(carry_ref, carry_out, sems.at[1]),
            ]
            for copy in copies:
                copy.start()
        for start in range(0, atoms, TILE):
            cos_span = slice(start, start + TILE)
            sin_span = slice(atoms + start, atoms + start + TILE)
            turns = jnp.dot(ka_ref[row : row + ROWS, :], carry_ref[chans:, cos_span], **f32)
            cosv, sinv = phases_of(turns)
            place[at : at + ROWS, cos_span] = cosv.astype(jnp.bfloat16)
            place[at : at + ROWS, sin_span] = sinv.astype(jnp.bfloat16)
            if row == kept:
                carry_ref[:chans, cos_span] = jnp.dot(weight_ref[...], h_ref[:, cos_span], **f32).astype(jnp.bfloat16)
            pending.append((place, at, row, start))
            if len(pending) > 1:
                add_up(*pending.pop(0))
    add_up(*pending.pop(0))
    kept_ref[...] = whole_ref[mine, :]
    sent_ref[...] = whole_ref[theirs, :].astype(jnp.bfloat16)
    for copy in copies:
        copy.wait()


def in_hbm(*arrays):
    return tuple(pltpu.with_memory_space_constraint(array, pltpu.HBM) for array in arrays)


def structure(place, count, kvec, coords, h, weight, mixing, scale, regions):
    waves, atoms, chans = kvec.shape[1], coords.shape[1], h.shape[0]
    kept = kept_rows(waves)
    return pl.pallas_call(
        functools.partial(structure_kernel, scale, float(regions)),
        out_shape=(
            jax.ShapeDtypeStruct((kept, 2 * atoms), jnp.bfloat16),
            pltpu.HBM((waves - kept, 2 * atoms), jnp.bfloat16),
            jax.ShapeDtypeStruct((waves // 2, 2 * chans), jnp.float32),
            jax.ShapeDtypeStruct((waves // 2, 2 * chans), jnp.bfloat16),
            pltpu.HBM((chans + 24, atoms), jnp.bfloat16),
            jax.ShapeDtypeStruct((waves // 2, 2 * chans), jnp.float32),
            jax.ShapeDtypeStruct(mixing.shape, jnp.float32),
        ),
        in_specs=[SMEM_SPEC] * 2 + [HBM_SPEC] * 5,
        out_specs=(VMEM_SPEC, HBM_SPEC, VMEM_SPEC, VMEM_SPEC, HBM_SPEC, VMEM_SPEC, VMEM_SPEC),
        scratch_shapes=[
            pltpu.VMEM(kvec.shape, jnp.int32),
            pltpu.VMEM(coords.shape, jnp.float32),
            pltpu.VMEM(h.shape, jnp.bfloat16),
            pltpu.VMEM(weight.shape, jnp.bfloat16),
            pltpu.VMEM((waves, 24), jnp.bfloat16),
            pltpu.VMEM(h.shape, jnp.bfloat16),
            pltpu.VMEM((waves - kept, 2 * atoms), jnp.bfloat16),
            pltpu.VMEM((chans + 24, atoms), jnp.bfloat16),
            pltpu.VMEM((waves, 2 * chans), jnp.float32),
            pltpu.VMEM((waves, 2 * chans), jnp.float32),
            pltpu.SemaphoreType.DMA((5,)),
            pltpu.SemaphoreType.DMA((2,)),
        ],
        compiler_params=PARAMS,
        name="structure",
    )(place, count, *in_hbm(kvec, coords, h, weight, mixing))


def spectral_kernel(kept_ref, arrived_ref, gain_ref, mixing_ref, out_ref):
    chans = mixing_ref.shape[0]
    factor = kept_ref[...] + arrived_ref[...].astype(jnp.float32)
    high = dict(precision=lax.Precision.HIGHEST, preferred_element_type=jnp.float32)
    mixing = mixing_ref[...]
    cos_part = jnp.dot(factor[:, :chans], mixing, **high)
    sin_part = jnp.dot(factor[:, chans:], mixing, **high)
    out_ref[...] = (jnp.concatenate([cos_part, sin_part], axis=1) * gain_ref[...]).astype(jnp.bfloat16)


def spectral(kept, arrived, gain, mixing):
    return pl.pallas_call(
        spectral_kernel,
        out_shape=jax.ShapeDtypeStruct(arrived.shape, jnp.bfloat16),
        in_specs=[VMEM_SPEC] * 4,
        out_specs=VMEM_SPEC,
        compiler_params=PARAMS,
        name="spectral",
    )(kept, arrived, gain, mixing)


def potentials_kernel(
    place_ref, own_ref, other_ref, low_ref, high_in, out_ref, filtered_ref, high_ref, across_ref, sum_ref, sem,
):
    chans = out_ref.shape[1]
    pieces, _, width = out_ref.shape
    atoms = pieces * width
    kept, waves = low_ref.shape[0], filtered_ref.shape[0]
    copy = pltpu.make_async_copy(high_in, high_ref, sem)
    copy.start()
    half = own_ref.shape[0]
    core = jnp.bitwise_and(place_ref[0], 1)
    filtered_ref[pl.ds(pl.multiple_of(core * half, half), half), :] = own_ref[...]
    filtered_ref[pl.ds(pl.multiple_of((1 - core) * half, half), half), :] = other_ref[...]
    across_ref[...] = filtered_ref[...].astype(jnp.float32).T.astype(jnp.bfloat16)

    def term(rows, table, piece):
        cos_span = slice(piece * width, (piece + 1) * width)
        sin_span = slice(atoms + piece * width, atoms + (piece + 1) * width)
        f32 = dict(preferred_element_type=jnp.float32)
        return jnp.dot(across_ref[:chans, rows], table[:, cos_span], **f32) + jnp.dot(
            across_ref[chans:, rows], table[:, sin_span], **f32
        )

    for piece in range(pieces):
        sum_ref[piece] = term(slice(0, kept), low_ref, piece)
    copy.wait()
    for piece in range(pieces):
        whole = sum_ref[piece] + term(slice(kept, waves), high_ref, piece)
        out_ref[piece] = (whole * (1.0 / math.sqrt(K))).astype(jnp.bfloat16)


def potentials(place, own, other, low, high, pieces):
    chans = own.shape[1] // 2
    waves = 2 * own.shape[0]
    atoms = low.shape[1] // 2
    return pl.pallas_call(
        potentials_kernel,
        out_shape=jax.ShapeDtypeStruct((pieces, chans, atoms // pieces), jnp.bfloat16),
        in_specs=[SMEM_SPEC, VMEM_SPEC, VMEM_SPEC, VMEM_SPEC, HBM_SPEC],
        out_specs=VMEM_SPEC,
        scratch_shapes=[
            pltpu.VMEM((waves, 2 * chans), jnp.bfloat16),
            pltpu.VMEM(high.shape, jnp.bfloat16),
            pltpu.VMEM((2 * chans, waves), jnp.bfloat16),
            pltpu.VMEM((pieces, chans, atoms // pieces), jnp.float32),
            pltpu.SemaphoreType.DMA,
        ],
        compiler_params=PARAMS,
        name="potentials",
    )(place, own, other, low, *in_hbm(high))


def pairs_kernel(
    scale_x, regions, unroll, place_ref, count_ref, idx_ref, live_ref, prev_in, next_in, own_in, h_in, first_in, second_in,
    inner_ref, share_ref, alive_ref, third_ref, second_ref,
    ext_ref, first_ref, own_ref, pos_ref, weights_ref, near_ref, sum_ref, sems,
):
    chans = h_in.shape[0]
    width = own_in.shape[1]
    nblocks = width // BLOCK
    slots = idx_ref.shape[1]
    count = share_ref.shape[1] // BLOCK
    here = place_ref[0]
    first = place_ref[1]
    share = pl.ds(pl.multiple_of(first * BLOCK, BLOCK), count * BLOCK)
    moves = []
    for rows in (pl.ds(chans, ext_ref.shape[0] - chans), pl.ds(0, chans)):
        for at, source in enumerate((prev_in, own_in, next_in)):
            moves.append((source.at[rows, :], ext_ref.at[rows, pl.ds(at * width, width)]))
    moves += [(h_in.at[:, share], share_ref), (first_in, first_ref), (second_in, second_ref)]
    copies = [pltpu.make_async_copy(source, target, sems.at[at]) for at, (source, target) in enumerate(moves)]
    for copy in copies:
        copy.start()
    atom = lax.broadcasted_iota(jnp.int32, alive_ref.shape, 1) + first * BLOCK
    alive_ref[...] = jnp.where(atom < count_ref[0] * BLOCK, 1.0, 0.0)
    for copy in copies[:3]:
        copy.wait()
    f32 = dict(preferred_element_type=jnp.float32)
    column = lax.broadcasted_iota(jnp.int32, (8, 8), 1)
    pick = jnp.where((column >= 3) & (column < 6), 1.0, 0.0).astype(jnp.bfloat16)
    row = lax.broadcasted_iota(jnp.int32, (8, BLOCK), 0)
    lead = jnp.where(row < 3, 1.0, 0.0).astype(jnp.bfloat16)
    for axis in range(3):
        rows = slice(chans + 8 * axis, chans + 8 * axis + 8)
        for start in range(0, 3 * width, 4 * BLOCK):
            span = slice(start, start + 4 * BLOCK)
            pos_ref[axis, :, span] = jnp.dot(pick, ext_ref[rows, span], **f32)
    for block in range(count):
        at = pl.multiple_of((nblocks + first + block) * BLOCK, BLOCK)
        for axis in range(3):
            rows = ext_ref[chans + 8 * axis : chans + 8 * axis + 8, pl.ds(at, BLOCK)].astype(jnp.float32)
            swapped = jnp.concatenate([-rows[3:6], rows[0:3], rows[6:8]], axis=0)
            own_ref[block, axis] = jnp.dot(swapped.T.astype(jnp.bfloat16), lead, **f32)
        sum_ref[block] = jnp.zeros((chans, BLOCK), jnp.float32)
        weights_ref[block] = jnp.zeros(weights_ref.shape[1:], jnp.bfloat16)
        near_ref[block] = jnp.zeros(near_ref.shape[1:], jnp.bfloat16)
    for copy in copies[3:6]:
        copy.wait()
    exponent = -2.0 * math.log2(math.e)
    part_rows = 16

    def add_up(block):
        sum_ref[block] += lax.dot_general(near_ref[block], weights_ref[block], NT, **f32)

    def slots_step(step, carried):
        for block in range(count):
            add_up(block)
        for block in range(count):
            for part in range(unroll):
                slot = step * unroll + part
                entry = idx_ref[first + block, slot]
                where = jnp.bitwise_and(entry + (regions + 1 - here) * nblocks, regions * nblocks - 1)
                span = pl.ds(pl.multiple_of(where * BLOCK, BLOCK), BLOCK)
                to = slice(part * BLOCK, (part + 1) * BLOCK)
                used = live_ref[first + block, slot].astype(jnp.float32)
                mapped = ext_ref[:chans, span].astype(jnp.float32) * used
                near_ref[block, :, to] = mapped.astype(jnp.bfloat16)
                minus = [jnp.tile(pos_ref[axis, :, span], (part_rows // 8, 1)) for axis in range(3)]
                for start in range(0, BLOCK, part_rows):
                    rows = slice(start, start + part_rows)
                    total = None
                    for axis in range(3):
                        diff = own_ref[block, axis, rows, :] + minus[axis]
                        diff = diff - jnp.round(diff)
                        term = diff * diff
                        if axis == 0:
                            term = term * (scale_x * scale_x)
                        total = term if total is None else total + term
                    weights_ref[block, rows, to] = jnp.exp2(total * exponent).astype(jnp.bfloat16)
        return carried

    lax.fori_loop(0, slots // unroll, slots_step, 0)
    for copy in copies[6:]:
        copy.wait()
    outer = first_ref[: 2 * chans, :]
    third_ref[...] = first_ref[2 * chans :, :].astype(jnp.float32).T.astype(jnp.bfloat16)
    for block in range(count):
        add_up(block)
        span = slice(block * BLOCK, (block + 1) * BLOCK)
        msg = (sum_ref[block] * MSG_SCALE).astype(jnp.bfloat16)
        known = jnp.concatenate([share_ref[:, span], msg], axis=0)
        inner_ref[:, span] = lax.dot_general(outer, known, TN, **f32)


def pairs(place, live_blocks, neighbours, live_slots, prev, own, following, h, first, second, count, regions):
    rows, width = own.shape
    chans = h.shape[0]
    hidden = first.shape[1]
    slots = neighbours.shape[1]
    share = count * BLOCK
    work = slots * share * BLOCK
    unroll = 3 if slots % 3 == 0 else 1
    return pl.pallas_call(
        functools.partial(pairs_kernel, float(regions), regions, unroll),
        out_shape=(
            jax.ShapeDtypeStruct((hidden, share), jnp.float32),
            jax.ShapeDtypeStruct((chans, share), jnp.bfloat16),
            jax.ShapeDtypeStruct((8, share), jnp.float32),
            jax.ShapeDtypeStruct((hidden, chans), jnp.bfloat16),
            jax.ShapeDtypeStruct(second.shape, jnp.bfloat16),
        ),
        in_specs=[SMEM_SPEC] * 4 + [ANY_SPEC] * 2 + [HBM_SPEC] * 4,
        out_specs=(VMEM_SPEC,) * 5,
        scratch_shapes=[
            pltpu.VMEM((rows, 3 * width), jnp.bfloat16),
            pltpu.VMEM(first.shape, jnp.bfloat16),
            pltpu.VMEM((count, 3, BLOCK, BLOCK), jnp.float32),
            pltpu.VMEM((3, 8, 3 * width), jnp.float32),
            pltpu.VMEM((count, BLOCK, unroll * BLOCK), jnp.bfloat16),
            pltpu.VMEM((count, chans, unroll * BLOCK), jnp.bfloat16),
            pltpu.VMEM((count, chans, BLOCK), jnp.float32),
            pltpu.SemaphoreType.DMA((9,)),
        ],
        compiler_params=PARAMS,
        cost_estimate=pl.CostEstimate(
            flops=work * (2 * chans + 20), bytes_accessed=6 * rows * width, transcendentals=work
        ),
        name="pairs",
    )(place, live_blocks, neighbours, live_slots, prev, following, *in_hbm(own, h, first, second))


def update_kernel(arrived_ref, inner_ref, share_ref, alive_ref, third_ref, second_ref, out_ref):
    potential = arrived_ref[0].astype(jnp.float32)
    for piece in range(1, arrived_ref.shape[0]):
        potential = potential + arrived_ref[piece].astype(jnp.float32)
    f32 = dict(preferred_element_type=jnp.float32)
    inner = inner_ref[...] + jnp.dot(third_ref[...], potential.astype(jnp.bfloat16), **f32)
    hidden = jax.nn.silu(inner).astype(jnp.bfloat16)
    out = share_ref[...].astype(jnp.float32) + jnp.dot(second_ref[...], hidden, **f32)
    new = jnp.where(alive_ref[0:1, :] > 0.0, out, 0.0).astype(jnp.bfloat16)
    for piece in range(out_ref.shape[0]):
        out_ref[piece] = new


def update(arrived, known):
    return pl.pallas_call(
        update_kernel,
        out_shape=jax.ShapeDtypeStruct(arrived.shape, jnp.bfloat16),
        in_specs=[VMEM_SPEC] * 6,
        out_specs=VMEM_SPEC,
        compiler_params=PARAMS,
        name="update",
    )(arrived, *known)


def laid_out(pieces, dim):
    lengths = list(pieces.shape[1:])
    lengths[dim] *= pieces.shape[0]
    return jnp.moveaxis(pieces, 0, dim).reshape(lengths)


def shifted(cells, regions, groups, step):
    pairs_of = []
    for region in range(regions):
        to = region + step
        turned = 0 if 0 <= to < regions else groups // 2
        for group in range(groups):
            pairs_of.append((region * groups + group, to % regions * groups + (group ^ turned)))
    return lax.ppermute(cells, ("atoms", "waves"), pairs_of)


def from_others(pieces, axis):
    return lax.all_to_all(pieces, axis, 0, 0, tiled=True)


def local(
    features,
    coords,
    neighbours,
    live_slots,
    block_count,
    kvec,
    msg_weight,
    filter_weight,
    mlp_in,
    mlp_out,
):
    _, width = features.shape
    nblocks = width // BLOCK
    regions = lax.axis_size("atoms")
    groups_waves = lax.axis_size("waves")
    here = lax.axis_index("atoms")
    per_group = nblocks // groups_waves
    first = lax.axis_index("waves") * per_group
    place = jnp.stack([here, first]).astype(jnp.int32)
    total = regions * width
    low, high, factor, sent, carry, gain_rows, mixing = structure(
        place, block_count, kvec, coords, features, msg_weight[0], filter_weight[0], 1.0 / math.sqrt(total), regions
    )
    exchanges = (1, 2, 6, 8, 24)
    for step, flip in enumerate(exchanges):
        arrived = lax.ppermute(sent, "atoms", [(i, i ^ flip) for i in range(regions)])
        if step + 1 < len(exchanges):
            factor = factor + arrived.astype(jnp.float32)
            sent = factor.astype(jnp.bfloat16)
    prev = shifted(carry, regions, groups_waves, 1)
    following = shifted(carry, regions, groups_waves, -1)
    filtered = spectral(factor, arrived, gain_rows, mixing)
    other = lax.ppermute(filtered, "atoms", [(i, i ^ 1) for i in range(regions)])
    partial_potential = potentials(place, filtered, other, low, high, groups_waves)
    potential = from_others(partial_potential, "waves")
    known = pairs(
        place, block_count, neighbours.T, live_slots.T, prev, carry, following,
        features, mlp_in[0].T, mlp_out[0], per_group, regions,
    )
    new = update(potential, known)
    return laid_out(from_others(new, "waves"), 1)


def solution(mesh):
    in_specs = (
        P(None, "atoms"),
        P(None, "atoms"),
        P(None, "atoms"),
        P(None, "atoms"),
        P("atoms"),
        P(None, "waves"),
        P(),
        P(),
        P(),
        P(),
    )
    out_specs = P(None, "atoms")
    return jax.shard_map(local, mesh=mesh, in_specs=in_specs, out_specs=out_specs, check_vma=False)
```

```python
import functools
import math

import jax
import jax.numpy as jnp
from jax import lax
from jax.experimental import pallas as pl
from jax.experimental.pallas import tpu as pltpu
from jax.sharding import PartitionSpec as P


K = 4096
BLOCK = 128

MSG_SCALE = 0.125
GAIN_TOP = 20.0
ALPHA = 8.0**0.25
SIN_COEFS = tuple(ALPHA / math.sqrt(2.0) * c for c in (2.221430356581745, -0.9131746556274619, 0.10983828651966959))
TILE = 256
ROWS = 128
LIMIT = 16 * 2**20
VMEM_SPEC = pl.BlockSpec(memory_space=pltpu.VMEM)
SMEM_SPEC = pl.BlockSpec(memory_space=pltpu.SMEM)
ANY_SPEC = pl.BlockSpec(memory_space=pl.ANY)
HBM_SPEC = pl.BlockSpec(memory_space=pltpu.HBM)
PARAMS = pltpu.CompilerParams(vmem_limit_bytes=LIMIT)
NT = (((1,), (1,)), ((), ()))
TN = (((0,), (0,)), ((), ()))


def kept_rows(waves):
    return waves * 3 // 4


def phases_of(turns):
    r = turns - jnp.round(turns)
    u = r * r
    s = r * ((SIN_COEFS[2] * u + SIN_COEFS[1]) * u + SIN_COEFS[0])
    q = s * s
    w = math.sqrt(8.0) - q
    return 1.0 - q * w, (s * (w * lax.rsqrt(w))) * (math.sqrt(2.0) - q)


def three_pieces(values):
    first = values.astype(jnp.bfloat16)
    rest = values - first.astype(jnp.float32)
    second = rest.astype(jnp.bfloat16)
    third = (rest - second.astype(jnp.float32)).astype(jnp.bfloat16)
    return first.astype(jnp.float32), second.astype(jnp.float32), third.astype(jnp.float32)


def structure_kernel(
    scale, regions, place_ref, count_ref, kvec_in, coords_in, h_in, weight_in, mixing_in,
    low_ref, high_out, kept_ref, sent_ref, carry_out, gain_ref, mixing_ref,
    kvec_ref, coords_ref, h_ref, weight_ref, ka_ref, masked_ref, high_ref, carry_ref, whole_ref, gains_ref, in_sems, sems,
):
    waves = kvec_ref.shape[1]
    chans, atoms = h_ref.shape
    kept = low_ref.shape[0]
    half = kept_ref.shape[0]
    core = jnp.bitwise_and(place_ref[0], 1)
    mine = pl.ds(pl.multiple_of(core * half, half), half)
    theirs = pl.ds(pl.multiple_of((1 - core) * half, half), half)
    f32 = dict(preferred_element_type=jnp.float32)
    taken = [
        pltpu.make_async_copy(source, target, in_sems.at[at])
        for at, (source, target) in enumerate(
            (
                (kvec_in, kvec_ref),
                (coords_in, coords_ref),
                (h_in, h_ref),
                (weight_in, weight_ref),
                (mixing_in, mixing_ref),
            )
        )
    ]
    for copy in taken:
        copy.start()
    taken[0].wait()
    kf = kvec_ref[...].astype(jnp.float32)
    ahead, behind = jnp.zeros((3, waves), jnp.float32), jnp.zeros((2, waves), jnp.float32)
    ka = jnp.concatenate([part for axis in range(3) for part in (ahead, *(-kf[axis : axis + 1],) * 3, behind)], axis=0)
    ka_ref[...] = ka.T.astype(jnp.bfloat16)
    kx = kf[0:1] / regions
    gain = GAIN_TOP / (4.0 + kx * kx + kf[1:2] * kf[1:2] + kf[2:3] * kf[2:3])
    columns = jnp.broadcast_to(gain * scale, (8, waves)).T
    gains_ref[...] = jnp.broadcast_to(columns[:, 0:1], gains_ref.shape)
    gain_ref[...] = gains_ref[mine, :]
    taken[1].wait()
    pieces = three_pieces(coords_ref[...])
    ones, gap = jnp.ones((3, atoms), jnp.float32), jnp.zeros((2, atoms), jnp.float32)
    for axis in range(3):
        rows = jnp.concatenate([ones, *(-piece[axis : axis + 1] for piece in pieces), gap], axis=0)
        carry_ref[chans + 8 * axis : chans + 8 * axis + 8, :] = rows.astype(jnp.bfloat16)
    for copy in taken[2:]:
        copy.wait()
    live_atoms = count_ref[0] * BLOCK
    atom = lax.broadcasted_iota(jnp.int32, (chans, atoms), 1)
    masked_ref[...] = jnp.where(atom < live_atoms, h_ref[...].astype(jnp.float32), 0.0).astype(jnp.bfloat16)
    zero = jnp.zeros((chans, TILE), jnp.bfloat16)
    sums = {}

    def add_up(place, at, row, start):
        ht = masked_ref[:, start : start + TILE]
        cosv = place[at : at + ROWS, start : start + TILE]
        sinv = place[at : at + ROWS, atoms + start : atoms + start + TILE]
        term = lax.dot_general(cosv, jnp.concatenate([ht, zero], axis=0), NT, **f32)
        term = term + lax.dot_general(sinv, jnp.concatenate([zero, ht], axis=0), NT, **f32)
        sums[row] = term if start == 0 else sums[row] + term
        if start + TILE == atoms:
            whole_ref[row : row + ROWS, :] = sums.pop(row)

    pending = []
    copies = []
    for row in [*range(kept, waves, ROWS), *range(0, kept, ROWS)]:
        place, at = (low_ref, row) if row < kept else (high_ref, row - kept)
        if row == 0:
            copies = [
                pltpu.make_async_copy(high_ref, high_out, sems.at[0]),
                pltpu.make_async_copy(carry_ref, carry_out, sems.at[1]),
            ]
            for copy in copies:
                copy.start()
        for start in range(0, atoms, TILE):
            cos_span = slice(start, start + TILE)
            sin_span = slice(atoms + start, atoms + start + TILE)
            turns = jnp.dot(ka_ref[row : row + ROWS, :], carry_ref[chans:, cos_span], **f32)
            cosv, sinv = phases_of(turns)
            place[at : at + ROWS, cos_span] = cosv.astype(jnp.bfloat16)
            place[at : at + ROWS, sin_span] = sinv.astype(jnp.bfloat16)
            if row == kept:
                carry_ref[:chans, cos_span] = jnp.dot(weight_ref[...], h_ref[:, cos_span], **f32).astype(jnp.bfloat16)
            pending.append((place, at, row, start))
            if len(pending) > 1:
                add_up(*pending.pop(0))
    add_up(*pending.pop(0))
    kept_ref[...] = whole_ref[mine, :]
    sent_ref[...] = whole_ref[theirs, :].astype(jnp.bfloat16)
    for copy in copies:
        copy.wait()


def in_hbm(*arrays):
    return tuple(pltpu.with_memory_space_constraint(array, pltpu.HBM) for array in arrays)


def structure(place, count, kvec, coords, h, weight, mixing, scale, regions):
    waves, atoms, chans = kvec.shape[1], coords.shape[1], h.shape[0]
    kept = kept_rows(waves)
    return pl.pallas_call(
        functools.partial(structure_kernel, scale, float(regions)),
        out_shape=(
            jax.ShapeDtypeStruct((kept, 2 * atoms), jnp.bfloat16),
            pltpu.HBM((waves - kept, 2 * atoms), jnp.bfloat16),
            jax.ShapeDtypeStruct((waves // 2, 2 * chans), jnp.float32),
            jax.ShapeDtypeStruct((waves // 2, 2 * chans), jnp.bfloat16),
            pltpu.HBM((chans + 24, atoms), jnp.bfloat16),
            jax.ShapeDtypeStruct((waves // 2, 2 * chans), jnp.float32),
            jax.ShapeDtypeStruct(mixing.shape, jnp.float32),
        ),
        in_specs=[SMEM_SPEC] * 2 + [HBM_SPEC] * 5,
        out_specs=(VMEM_SPEC, HBM_SPEC, VMEM_SPEC, VMEM_SPEC, HBM_SPEC, VMEM_SPEC, VMEM_SPEC),
        scratch_shapes=[
            pltpu.VMEM(kvec.shape, jnp.int32),
            pltpu.VMEM(coords.shape, jnp.float32),
            pltpu.VMEM(h.shape, jnp.bfloat16),
            pltpu.VMEM(weight.shape, jnp.bfloat16),
            pltpu.VMEM((waves, 24), jnp.bfloat16),
            pltpu.VMEM(h.shape, jnp.bfloat16),
            pltpu.VMEM((waves - kept, 2 * atoms), jnp.bfloat16),
            pltpu.VMEM((chans + 24, atoms), jnp.bfloat16),
            pltpu.VMEM((waves, 2 * chans), jnp.float32),
            pltpu.VMEM((waves, 2 * chans), jnp.float32),
            pltpu.SemaphoreType.DMA((5,)),
            pltpu.SemaphoreType.DMA((2,)),
        ],
        compiler_params=PARAMS,
        name="structure",
    )(place, count, *in_hbm(kvec, coords, h, weight, mixing))


def spectral_kernel(kept_ref, arrived_ref, gain_ref, mixing_ref, out_ref):
    chans = mixing_ref.shape[0]
    factor = kept_ref[...] + arrived_ref[...].astype(jnp.float32)
    high = dict(precision=lax.Precision.HIGHEST, preferred_element_type=jnp.float32)
    mixing = mixing_ref[...]
    cos_part = jnp.dot(factor[:, :chans], mixing, **high)
    sin_part = jnp.dot(factor[:, chans:], mixing, **high)
    out_ref[...] = (jnp.concatenate([cos_part, sin_part], axis=1) * gain_ref[...]).astype(jnp.bfloat16)


def spectral(kept, arrived, gain, mixing):
    return pl.pallas_call(
        spectral_kernel,
        out_shape=jax.ShapeDtypeStruct(arrived.shape, jnp.bfloat16),
        in_specs=[VMEM_SPEC] * 4,
        out_specs=VMEM_SPEC,
        compiler_params=PARAMS,
        name="spectral",
    )(kept, arrived, gain, mixing)


def potentials_kernel(
    place_ref, own_ref, other_ref, low_ref, high_in, out_ref, filtered_ref, high_ref, across_ref, sum_ref, sem,
):
    chans = out_ref.shape[1]
    pieces, _, width = out_ref.shape
    atoms = pieces * width
    kept, waves = low_ref.shape[0], filtered_ref.shape[0]
    copy = pltpu.make_async_copy(high_in, high_ref, sem)
    copy.start()
    half = own_ref.shape[0]
    core = jnp.bitwise_and(place_ref[0], 1)
    filtered_ref[pl.ds(pl.multiple_of(core * half, half), half), :] = own_ref[...]
    filtered_ref[pl.ds(pl.multiple_of((1 - core) * half, half), half), :] = other_ref[...]
    across_ref[...] = filtered_ref[...].astype(jnp.float32).T.astype(jnp.bfloat16)

    def term(rows, table, piece):
        cos_span = slice(piece * width, (piece + 1) * width)
        sin_span = slice(atoms + piece * width, atoms + (piece + 1) * width)
        f32 = dict(preferred_element_type=jnp.float32)
        return jnp.dot(across_ref[:chans, rows], table[:, cos_span], **f32) + jnp.dot(
            across_ref[chans:, rows], table[:, sin_span], **f32
        )

    for piece in range(pieces):
        sum_ref[piece] = term(slice(0, kept), low_ref, piece)
    copy.wait()
    for piece in range(pieces):
        whole = sum_ref[piece] + term(slice(kept, waves), high_ref, piece)
        out_ref[piece] = (whole * (1.0 / math.sqrt(K))).astype(jnp.bfloat16)


def potentials(place, own, other, low, high, pieces):
    chans = own.shape[1] // 2
    waves = 2 * own.shape[0]
    atoms = low.shape[1] // 2
    return pl.pallas_call(
        potentials_kernel,
        out_shape=jax.ShapeDtypeStruct((pieces, chans, atoms // pieces), jnp.bfloat16),
        in_specs=[SMEM_SPEC, VMEM_SPEC, VMEM_SPEC, VMEM_SPEC, HBM_SPEC],
        out_specs=VMEM_SPEC,
        scratch_shapes=[
            pltpu.VMEM((waves, 2 * chans), jnp.bfloat16),
            pltpu.VMEM(high.shape, jnp.bfloat16),
            pltpu.VMEM((2 * chans, waves), jnp.bfloat16),
            pltpu.VMEM((pieces, chans, atoms // pieces), jnp.float32),
            pltpu.SemaphoreType.DMA,
        ],
        compiler_params=PARAMS,
        name="potentials",
    )(place, own, other, low, *in_hbm(high))


def pairs_kernel(
    scale_x, regions, unroll, place_ref, count_ref, idx_ref, live_ref, prev_in, next_in, own_in, h_in, first_in, second_in,
    inner_ref, share_ref, alive_ref, third_ref, second_ref,
    ext_ref, first_ref, own_ref, pos_ref, weights_ref, near_ref, sum_ref, sems,
):
    chans = h_in.shape[0]
    width = own_in.shape[1]
    nblocks = width // BLOCK
    slots = idx_ref.shape[1]
    count = share_ref.shape[1] // BLOCK
    here = place_ref[0]
    first = place_ref[1]
    share = pl.ds(pl.multiple_of(first * BLOCK, BLOCK), count * BLOCK)
    moves = []
    for rows in (pl.ds(chans, ext_ref.shape[0] - chans), pl.ds(0, chans)):
        for at, source in enumerate((prev_in, own_in, next_in)):
            moves.append((source.at[rows, :], ext_ref.at[rows, pl.ds(at * width, width)]))
    moves += [(h_in.at[:, share], share_ref), (first_in, first_ref), (second_in, second_ref)]
    copies = [pltpu.make_async_copy(source, target, sems.at[at]) for at, (source, target) in enumerate(moves)]
    for copy in copies:
        copy.start()
    atom = lax.broadcasted_iota(jnp.int32, alive_ref.shape, 1) + first * BLOCK
    alive_ref[...] = jnp.where(atom < count_ref[0] * BLOCK, 1.0, 0.0)
    for copy in copies[:3]:
        copy.wait()
    f32 = dict(preferred_element_type=jnp.float32)
    column = lax.broadcasted_iota(jnp.int32, (8, 8), 1)
    pick = jnp.where((column >= 3) & (column < 6), 1.0, 0.0).astype(jnp.bfloat16)
    row = lax.broadcasted_iota(jnp.int32, (8, BLOCK), 0)
    lead = jnp.where(row < 3, 1.0, 0.0).astype(jnp.bfloat16)
    for axis in range(3):
        rows = slice(chans + 8 * axis, chans + 8 * axis + 8)
        for start in range(0, 3 * width, 4 * BLOCK):
            span = slice(start, start + 4 * BLOCK)
            pos_ref[axis, :, span] = jnp.dot(pick, ext_ref[rows, span], **f32)
    for block in range(count):
        at = pl.multiple_of((nblocks + first + block) * BLOCK, BLOCK)
        for axis in range(3):
            rows = ext_ref[chans + 8 * axis : chans + 8 * axis + 8, pl.ds(at, BLOCK)].astype(jnp.float32)
            swapped = jnp.concatenate([-rows[3:6], rows[0:3], rows[6:8]], axis=0)
            own_ref[block, axis] = jnp.dot(swapped.T.astype(jnp.bfloat16), lead, **f32)
        sum_ref[block] = jnp.zeros((chans, BLOCK), jnp.float32)
        weights_ref[block] = jnp.zeros(weights_ref.shape[1:], jnp.bfloat16)
        near_ref[block] = jnp.zeros(near_ref.shape[1:], jnp.bfloat16)
    for copy in copies[3:6]:
        copy.wait()
    exponent = -2.0 * math.log2(math.e)
    part_rows = 16

    def add_up(block):
        sum_ref[block] += lax.dot_general(near_ref[block], weights_ref[block], NT, **f32)

    def slots_step(step, carried):
        for block in range(count):
            add_up(block)
        for block in range(count):
            for part in range(unroll):
                slot = step * unroll + part
                entry = idx_ref[first + block, slot]
                where = jnp.bitwise_and(entry + (regions + 1 - here) * nblocks, regions * nblocks - 1)
                span = pl.ds(pl.multiple_of(where * BLOCK, BLOCK), BLOCK)
                to = slice(part * BLOCK, (part + 1) * BLOCK)
                used = live_ref[first + block, slot].astype(jnp.float32)
                mapped = ext_ref[:chans, span].astype(jnp.float32) * used
                near_ref[block, :, to] = mapped.astype(jnp.bfloat16)
                minus = [jnp.tile(pos_ref[axis, :, span], (part_rows // 8, 1)) for axis in range(3)]
                for start in range(0, BLOCK, part_rows):
                    rows = slice(start, start + part_rows)
                    total = None
                    for axis in range(3):
                        diff = own_ref[block, axis, rows, :] + minus[axis]
                        diff = diff - jnp.round(diff)
                        term = diff * diff
                        if axis == 0:
                            term = term * (scale_x * scale_x)
                        total = term if total is None else total + term
                    weights_ref[block, rows, to] = jnp.exp2(total * exponent).astype(jnp.bfloat16)
        return carried

    lax.fori_loop(0, slots // unroll, slots_step, 0)
    for copy in copies[6:]:
        copy.wait()
    outer = first_ref[: 2 * chans, :]
    third_ref[...] = first_ref[2 * chans :, :].astype(jnp.float32).T.astype(jnp.bfloat16)
    for block in range(count):
        add_up(block)
        span = slice(block * BLOCK, (block + 1) * BLOCK)
        msg = (sum_ref[block] * MSG_SCALE).astype(jnp.bfloat16)
        known = jnp.concatenate([share_ref[:, span], msg], axis=0)
        inner_ref[:, span] = lax.dot_general(outer, known, TN, **f32)


def pairs(place, live_blocks, neighbours, live_slots, prev, own, following, h, first, second, count, regions):
    rows, width = own.shape
    chans = h.shape[0]
    hidden = first.shape[1]
    slots = neighbours.shape[1]
    share = count * BLOCK
    work = slots * share * BLOCK
    unroll = 3 if slots % 3 == 0 else 1
    return pl.pallas_call(
        functools.partial(pairs_kernel, float(regions), regions, unroll),
        out_shape=(
            jax.ShapeDtypeStruct((hidden, share), jnp.float32),
            jax.ShapeDtypeStruct((chans, share), jnp.bfloat16),
            jax.ShapeDtypeStruct((8, share), jnp.float32),
            jax.ShapeDtypeStruct((hidden, chans), jnp.bfloat16),
            jax.ShapeDtypeStruct(second.shape, jnp.bfloat16),
        ),
        in_specs=[SMEM_SPEC] * 4 + [ANY_SPEC] * 2 + [HBM_SPEC] * 4,
        out_specs=(VMEM_SPEC,) * 5,
        scratch_shapes=[
            pltpu.VMEM((rows, 3 * width), jnp.bfloat16),
            pltpu.VMEM(first.shape, jnp.bfloat16),
            pltpu.VMEM((count, 3, BLOCK, BLOCK), jnp.float32),
            pltpu.VMEM((3, 8, 3 * width), jnp.float32),
            pltpu.VMEM((count, BLOCK, unroll * BLOCK), jnp.bfloat16),
            pltpu.VMEM((count, chans, unroll * BLOCK), jnp.bfloat16),
            pltpu.VMEM((count, chans, BLOCK), jnp.float32),
            pltpu.SemaphoreType.DMA((9,)),
        ],
        compiler_params=PARAMS,
        cost_estimate=pl.CostEstimate(
            flops=work * (2 * chans + 20), bytes_accessed=6 * rows * width, transcendentals=work
        ),
        name="pairs",
    )(place, live_blocks, neighbours, live_slots, prev, following, *in_hbm(own, h, first, second))


def update_kernel(arrived_ref, inner_ref, share_ref, alive_ref, third_ref, second_ref, out_ref):
    potential = arrived_ref[0].astype(jnp.float32)
    for piece in range(1, arrived_ref.shape[0]):
        potential = potential + arrived_ref[piece].astype(jnp.float32)
    f32 = dict(preferred_element_type=jnp.float32)
    inner = inner_ref[...] + jnp.dot(third_ref[...], potential.astype(jnp.bfloat16), **f32)
    hidden = jax.nn.silu(inner).astype(jnp.bfloat16)
    out = share_ref[...].astype(jnp.float32) + jnp.dot(second_ref[...], hidden, **f32)
    new = jnp.where(alive_ref[0:1, :] > 0.0, out, 0.0).astype(jnp.bfloat16)
    for piece in range(out_ref.shape[0]):
        out_ref[piece] = new


def update(arrived, known):
    return pl.pallas_call(
        update_kernel,
        out_shape=jax.ShapeDtypeStruct(arrived.shape, jnp.bfloat16),
        in_specs=[VMEM_SPEC] * 6,
        out_specs=VMEM_SPEC,
        compiler_params=PARAMS,
        name="update",
    )(arrived, *known)


def laid_out(pieces, dim):
    lengths = list(pieces.shape[1:])
    lengths[dim] *= pieces.shape[0]
    return jnp.moveaxis(pieces, 0, dim).reshape(lengths)


def shifted(cells, regions, groups, step):
    pairs_of = []
    for region in range(regions):
        to = region + step
        turned = 0 if 0 <= to < regions else groups // 2
        for group in range(groups):
            pairs_of.append((region * groups + group, to % regions * groups + (group ^ turned)))
    return lax.ppermute(cells, ("atoms", "waves"), pairs_of)


def from_others(pieces, axis):
    return lax.all_to_all(pieces, axis, 0, 0, tiled=True)


def local(
    features,
    coords,
    neighbours,
    live_slots,
    block_count,
    kvec,
    msg_weight,
    filter_weight,
    mlp_in,
    mlp_out,
):
    _, width = features.shape
    nblocks = width // BLOCK
    regions = lax.axis_size("atoms")
    groups_waves = lax.axis_size("waves")
    here = lax.axis_index("atoms")
    per_group = nblocks // groups_waves
    first = lax.axis_index("waves") * per_group
    place = jnp.stack([here, first]).astype(jnp.int32)
    total = regions * width
    low, high, factor, sent, carry, gain_rows, mixing = structure(
        place, block_count, kvec, coords, features, msg_weight[0], filter_weight[0], 1.0 / math.sqrt(total), regions
    )
    exchanges = ((1, 1), (2, 8), (6, 24), (8, 2), (24, 6))
    for step, flips in enumerate(exchanges):
        arrived = lax.ppermute(sent, "atoms", [(i, i ^ flips[i % 2]) for i in range(regions)])
        if step + 1 < len(exchanges):
            factor = factor + arrived.astype(jnp.float32)
            sent = factor.astype(jnp.bfloat16)
    prev = shifted(carry, regions, groups_waves, 1)
    following = shifted(carry, regions, groups_waves, -1)
    filtered = spectral(factor, arrived, gain_rows, mixing)
    other = lax.ppermute(filtered, "atoms", [(i, i ^ 1) for i in range(regions)])
    partial_potential = potentials(place, filtered, other, low, high, groups_waves)
    potential = from_others(partial_potential, "waves")
    known = pairs(
        place, block_count, neighbours.T, live_slots.T, prev, carry, following,
        features, mlp_in[0].T, mlp_out[0], per_group, regions,
    )
    new = update(potential, known)
    return laid_out(from_others(new, "waves"), 1)


def solution(mesh):
    in_specs = (
        P(None, "atoms"),
        P(None, "atoms"),
        P(None, "atoms"),
        P(None, "atoms"),
        P("atoms"),
        P(None, "waves"),
        P(),
        P(),
        P(),
        P(),
    )
    out_specs = P(None, "atoms")
    return jax.shard_map(local, mesh=mesh, in_specs=in_specs, out_specs=out_specs, check_vma=False)
```

```python
import functools
import math

import jax
import jax.numpy as jnp
from jax import lax
from jax.experimental import pallas as pl
from jax.experimental.pallas import tpu as pltpu
from jax.sharding import PartitionSpec as P


K = 4096
BLOCK = 128

MSG_SCALE = 0.125
GAIN_TOP = 20.0
ALPHA = 8.0**0.25
SIN_COEFS = tuple(ALPHA / math.sqrt(2.0) * c for c in (2.221430356581745, -0.9131746556274619, 0.10983828651966959))
TILE = 256
ROWS = 128
LIMIT = 16 * 2**20
VMEM_SPEC = pl.BlockSpec(memory_space=pltpu.VMEM)
SMEM_SPEC = pl.BlockSpec(memory_space=pltpu.SMEM)
ANY_SPEC = pl.BlockSpec(memory_space=pl.ANY)
HBM_SPEC = pl.BlockSpec(memory_space=pltpu.HBM)
PARAMS = pltpu.CompilerParams(vmem_limit_bytes=LIMIT)
NT = (((1,), (1,)), ((), ()))
TN = (((0,), (0,)), ((), ()))


def kept_rows(waves):
    return waves * 3 // 4


def phases_of(turns):
    r = turns - jnp.round(turns)
    u = r * r
    s = r * ((SIN_COEFS[2] * u + SIN_COEFS[1]) * u + SIN_COEFS[0])
    q = s * s
    w = math.sqrt(8.0) - q
    return 1.0 - q * w, (s * (w * lax.rsqrt(w))) * (math.sqrt(2.0) - q)


def three_pieces(values):
    first = values.astype(jnp.bfloat16)
    rest = values - first.astype(jnp.float32)
    second = rest.astype(jnp.bfloat16)
    third = (rest - second.astype(jnp.float32)).astype(jnp.bfloat16)
    return first.astype(jnp.float32), second.astype(jnp.float32), third.astype(jnp.float32)


def structure_kernel(
    scale, regions, place_ref, count_ref, kvec_in, coords_in, h_in, weight_in, mixing_in,
    low_ref, high_out, kept_ref, sent_ref, carry_out, gain_ref, mixing_ref,
    kvec_ref, coords_ref, h_ref, weight_ref, ka_ref, masked_ref, high_ref, carry_ref, in_sems, sems,
):
    waves = kvec_ref.shape[1]
    chans, atoms = h_ref.shape
    kept = low_ref.shape[0]
    f32 = dict(preferred_element_type=jnp.float32)
    taken = [
        pltpu.make_async_copy(source, target, in_sems.at[at])
        for at, (source, target) in enumerate(
            (
                (kvec_in, kvec_ref),
                (coords_in, coords_ref),
                (h_in, h_ref),
                (weight_in, weight_ref),
                (mixing_in, mixing_ref),
            )
        )
    ]
    for copy in taken:
        copy.start()
    taken[0].wait()
    kf = kvec_ref[...].astype(jnp.float32)
    ahead, behind = jnp.zeros((3, waves), jnp.float32), jnp.zeros((2, waves), jnp.float32)
    ka = jnp.concatenate([part for axis in range(3) for part in (ahead, *(-kf[axis : axis + 1],) * 3, behind)], axis=0)
    ka_ref[...] = ka.T.astype(jnp.bfloat16)
    kx = kf[0:1] / regions
    gain = GAIN_TOP / (4.0 + kx * kx + kf[1:2] * kf[1:2] + kf[2:3] * kf[2:3])
    columns = jnp.broadcast_to(gain * scale, (8, waves)).T
    gain_ref[...] = jnp.broadcast_to(columns[:, 0:1], gain_ref.shape)
    taken[1].wait()
    pieces = three_pieces(coords_ref[...])
    ones, gap = jnp.ones((3, atoms), jnp.float32), jnp.zeros((2, atoms), jnp.float32)
    for axis in range(3):
        rows = jnp.concatenate([ones, *(-piece[axis : axis + 1] for piece in pieces), gap], axis=0)
        carry_ref[chans + 8 * axis : chans + 8 * axis + 8, :] = rows.astype(jnp.bfloat16)
    for copy in taken[2:]:
        copy.wait()
    live_atoms = count_ref[0] * BLOCK
    atom = lax.broadcasted_iota(jnp.int32, (chans, atoms), 1)
    masked_ref[...] = jnp.where(atom < live_atoms, h_ref[...].astype(jnp.float32), 0.0).astype(jnp.bfloat16)
    zero = jnp.zeros((chans, TILE), jnp.bfloat16)
    sums = {}

    def add_up(place, at, row, start):
        ht = masked_ref[:, start : start + TILE]
        cosv = place[at : at + ROWS, start : start + TILE]
        sinv = place[at : at + ROWS, atoms + start : atoms + start + TILE]
        term = lax.dot_general(cosv, jnp.concatenate([ht, zero], axis=0), NT, **f32)
        term = term + lax.dot_general(sinv, jnp.concatenate([zero, ht], axis=0), NT, **f32)
        sums[row] = term if start == 0 else sums[row] + term
        if start + TILE == atoms:
            whole = sums.pop(row)
            kept_ref[row : row + ROWS, :] = whole
            sent_ref[row : row + ROWS, :] = whole.astype(jnp.bfloat16)

    pending = []
    copies = []
    for row in [*range(kept, waves, ROWS), *range(0, kept, ROWS)]:
        place, at = (low_ref, row) if row < kept else (high_ref, row - kept)
        if row == 0:
            copies = [
                pltpu.make_async_copy(high_ref, high_out, sems.at[0]),
                pltpu.make_async_copy(carry_ref, carry_out, sems.at[1]),
            ]
            for copy in copies:
                copy.start()
        for start in range(0, atoms, TILE):
            cos_span = slice(start, start + TILE)
            sin_span = slice(atoms + start, atoms + start + TILE)
            turns = jnp.dot(ka_ref[row : row + ROWS, :], carry_ref[chans:, cos_span], **f32)
            cosv, sinv = phases_of(turns)
            place[at : at + ROWS, cos_span] = cosv.astype(jnp.bfloat16)
            place[at : at + ROWS, sin_span] = sinv.astype(jnp.bfloat16)
            if row == kept:
                carry_ref[:chans, cos_span] = jnp.dot(weight_ref[...], h_ref[:, cos_span], **f32).astype(jnp.bfloat16)
            pending.append((place, at, row, start))
            if len(pending) > 1:
                add_up(*pending.pop(0))
    add_up(*pending.pop(0))
    for copy in copies:
        copy.wait()


def in_hbm(*arrays):
    return tuple(pltpu.with_memory_space_constraint(array, pltpu.HBM) for array in arrays)


def structure(place, count, kvec, coords, h, weight, mixing, scale, regions):
    waves, atoms, chans = kvec.shape[1], coords.shape[1], h.shape[0]
    kept = kept_rows(waves)
    return pl.pallas_call(
        functools.partial(structure_kernel, scale, float(regions)),
        out_shape=(
            jax.ShapeDtypeStruct((kept, 2 * atoms), jnp.bfloat16),
            pltpu.HBM((waves - kept, 2 * atoms), jnp.bfloat16),
            jax.ShapeDtypeStruct((waves, 2 * chans), jnp.float32),
            jax.ShapeDtypeStruct((waves, 2 * chans), jnp.bfloat16),
            pltpu.HBM((chans + 24, atoms), jnp.bfloat16),
            jax.ShapeDtypeStruct((waves, 2 * chans), jnp.float32),
            jax.ShapeDtypeStruct(mixing.shape, jnp.float32),
        ),
        in_specs=[SMEM_SPEC] * 2 + [HBM_SPEC] * 5,
        out_specs=(VMEM_SPEC, HBM_SPEC, VMEM_SPEC, VMEM_SPEC, HBM_SPEC, VMEM_SPEC, VMEM_SPEC),
        scratch_shapes=[
            pltpu.VMEM(kvec.shape, jnp.int32),
            pltpu.VMEM(coords.shape, jnp.float32),
            pltpu.VMEM(h.shape, jnp.bfloat16),
            pltpu.VMEM(weight.shape, jnp.bfloat16),
            pltpu.VMEM((waves, 24), jnp.bfloat16),
            pltpu.VMEM(h.shape, jnp.bfloat16),
            pltpu.VMEM((waves - kept, 2 * atoms), jnp.bfloat16),
            pltpu.VMEM((chans + 24, atoms), jnp.bfloat16),
            pltpu.SemaphoreType.DMA((5,)),
            pltpu.SemaphoreType.DMA((2,)),
        ],
        compiler_params=PARAMS,
        name="structure",
    )(place, count, *in_hbm(kvec, coords, h, weight, mixing))


def spectral_kernel(kept_ref, arrived_ref, gain_ref, mixing_ref, out_ref):
    chans = mixing_ref.shape[0]
    factor = kept_ref[...] + arrived_ref[...].astype(jnp.float32)
    high = dict(precision=lax.Precision.HIGHEST, preferred_element_type=jnp.float32)
    mixing = mixing_ref[...]
    cos_part = jnp.dot(factor[:, :chans], mixing, **high)
    sin_part = jnp.dot(factor[:, chans:], mixing, **high)
    out_ref[...] = (jnp.concatenate([cos_part, sin_part], axis=1) * gain_ref[...]).astype(jnp.bfloat16)


def spectral(kept, arrived, gain, mixing):
    return pl.pallas_call(
        spectral_kernel,
        out_shape=jax.ShapeDtypeStruct(arrived.shape, jnp.bfloat16),
        in_specs=[VMEM_SPEC] * 4,
        out_specs=VMEM_SPEC,
        compiler_params=PARAMS,
        name="spectral",
    )(kept, arrived, gain, mixing)


def potentials_kernel(
    place_ref, own_ref, other_ref, low_ref, high_in, out_ref, high_ref, across_ref, sum_ref, sem,
):
    chans = out_ref.shape[1]
    pieces, _, width = out_ref.shape
    atoms = pieces * width
    kept, waves = low_ref.shape[0], own_ref.shape[0]
    copy = pltpu.make_async_copy(high_in, high_ref, sem)
    copy.start()
    filtered = jnp.where(
        jnp.bitwise_and(place_ref[0], 1) == 1, own_ref[...].astype(jnp.float32), other_ref[...].astype(jnp.float32)
    )
    across_ref[...] = filtered.T.astype(jnp.bfloat16)

    def term(rows, table, piece):
        cos_span = slice(piece * width, (piece + 1) * width)
        sin_span = slice(atoms + piece * width, atoms + (piece + 1) * width)
        f32 = dict(preferred_element_type=jnp.float32)
        return jnp.dot(across_ref[:chans, rows], table[:, cos_span], **f32) + jnp.dot(
            across_ref[chans:, rows], table[:, sin_span], **f32
        )

    for piece in range(pieces):
        sum_ref[piece] = term(slice(0, kept), low_ref, piece)
    copy.wait()
    for piece in range(pieces):
        whole = sum_ref[piece] + term(slice(kept, waves), high_ref, piece)
        out_ref[piece] = (whole * (1.0 / math.sqrt(K))).astype(jnp.bfloat16)


def potentials(place, own, other, low, high, pieces):
    chans = own.shape[1] // 2
    waves = own.shape[0]
    atoms = low.shape[1] // 2
    return pl.pallas_call(
        potentials_kernel,
        out_shape=jax.ShapeDtypeStruct((pieces, chans, atoms // pieces), jnp.bfloat16),
        in_specs=[SMEM_SPEC, VMEM_SPEC, VMEM_SPEC, VMEM_SPEC, HBM_SPEC],
        out_specs=VMEM_SPEC,
        scratch_shapes=[
            pltpu.VMEM(high.shape, jnp.bfloat16),
            pltpu.VMEM((2 * chans, waves), jnp.bfloat16),
            pltpu.VMEM((pieces, chans, atoms // pieces), jnp.float32),
            pltpu.SemaphoreType.DMA,
        ],
        compiler_params=PARAMS,
        name="potentials",
    )(place, own, other, low, *in_hbm(high))


def pairs_kernel(
    scale_x, regions, unroll, place_ref, count_ref, idx_ref, live_ref, prev_in, next_in, own_in, h_in, first_in, second_in,
    inner_ref, share_ref, alive_ref, third_ref, second_ref,
    ext_ref, first_ref, own_ref, pos_ref, weights_ref, near_ref, sum_ref, sems,
):
    chans = h_in.shape[0]
    width = own_in.shape[1]
    nblocks = width // BLOCK
    slots = idx_ref.shape[1]
    count = share_ref.shape[1] // BLOCK
    here = place_ref[0]
    first = place_ref[1]
    share = pl.ds(pl.multiple_of(first * BLOCK, BLOCK), count * BLOCK)
    moves = []
    for rows in (pl.ds(chans, ext_ref.shape[0] - chans), pl.ds(0, chans)):
        for at, source in enumerate((prev_in, own_in, next_in)):
            moves.append((source.at[rows, :], ext_ref.at[rows, pl.ds(at * width, width)]))
    moves += [(h_in.at[:, share], share_ref), (first_in, first_ref), (second_in, second_ref)]
    copies = [pltpu.make_async_copy(source, target, sems.at[at]) for at, (source, target) in enumerate(moves)]
    for copy in copies:
        copy.start()
    atom = lax.broadcasted_iota(jnp.int32, alive_ref.shape, 1) + first * BLOCK
    alive_ref[...] = jnp.where(atom < count_ref[0] * BLOCK, 1.0, 0.0)
    for copy in copies[:3]:
        copy.wait()
    f32 = dict(preferred_element_type=jnp.float32)
    column = lax.broadcasted_iota(jnp.int32, (8, 8), 1)
    pick = jnp.where((column >= 3) & (column < 6), 1.0, 0.0).astype(jnp.bfloat16)
    row = lax.broadcasted_iota(jnp.int32, (8, BLOCK), 0)
    lead = jnp.where(row < 3, 1.0, 0.0).astype(jnp.bfloat16)
    for axis in range(3):
        rows = slice(chans + 8 * axis, chans + 8 * axis + 8)
        for start in range(0, 3 * width, 4 * BLOCK):
            span = slice(start, start + 4 * BLOCK)
            pos_ref[axis, :, span] = jnp.dot(pick, ext_ref[rows, span], **f32)
    for block in range(count):
        at = pl.multiple_of((nblocks + first + block) * BLOCK, BLOCK)
        for axis in range(3):
            rows = ext_ref[chans + 8 * axis : chans + 8 * axis + 8, pl.ds(at, BLOCK)].astype(jnp.float32)
            swapped = jnp.concatenate([-rows[3:6], rows[0:3], rows[6:8]], axis=0)
            own_ref[block, axis] = jnp.dot(swapped.T.astype(jnp.bfloat16), lead, **f32)
        sum_ref[block] = jnp.zeros((chans, BLOCK), jnp.float32)
        weights_ref[block] = jnp.zeros(weights_ref.shape[1:], jnp.bfloat16)
        near_ref[block] = jnp.zeros(near_ref.shape[1:], jnp.bfloat16)
    for copy in copies[3:6]:
        copy.wait()
    exponent = -2.0 * math.log2(math.e)
    part_rows = 16

    def add_up(block):
        sum_ref[block] += lax.dot_general(near_ref[block], weights_ref[block], NT, **f32)

    def slots_step(step, carried):
        for block in range(count):
            add_up(block)
        for block in range(count):
            for part in range(unroll):
                slot = step * unroll + part
                entry = idx_ref[first + block, slot]
                where = jnp.bitwise_and(entry + (regions + 1 - here) * nblocks, regions * nblocks - 1)
                span = pl.ds(pl.multiple_of(where * BLOCK, BLOCK), BLOCK)
                to = slice(part * BLOCK, (part + 1) * BLOCK)
                used = live_ref[first + block, slot].astype(jnp.float32)
                mapped = ext_ref[:chans, span].astype(jnp.float32) * used
                near_ref[block, :, to] = mapped.astype(jnp.bfloat16)
                minus = [jnp.tile(pos_ref[axis, :, span], (part_rows // 8, 1)) for axis in range(3)]
                for start in range(0, BLOCK, part_rows):
                    rows = slice(start, start + part_rows)
                    total = None
                    for axis in range(3):
                        diff = own_ref[block, axis, rows, :] + minus[axis]
                        diff = diff - jnp.round(diff)
                        term = diff * diff
                        if axis == 0:
                            term = term * (scale_x * scale_x)
                        total = term if total is None else total + term
                    weights_ref[block, rows, to] = jnp.exp2(total * exponent).astype(jnp.bfloat16)
        return carried

    lax.fori_loop(0, slots // unroll, slots_step, 0)
    for copy in copies[6:]:
        copy.wait()
    outer = first_ref[: 2 * chans, :]
    third_ref[...] = first_ref[2 * chans :, :].astype(jnp.float32).T.astype(jnp.bfloat16)
    for block in range(count):
        add_up(block)
        span = slice(block * BLOCK, (block + 1) * BLOCK)
        msg = (sum_ref[block] * MSG_SCALE).astype(jnp.bfloat16)
        known = jnp.concatenate([share_ref[:, span], msg], axis=0)
        inner_ref[:, span] = lax.dot_general(outer, known, TN, **f32)


def pairs(place, live_blocks, neighbours, live_slots, prev, own, following, h, first, second, count, regions):
    rows, width = own.shape
    chans = h.shape[0]
    hidden = first.shape[1]
    slots = neighbours.shape[1]
    share = count * BLOCK
    work = slots * share * BLOCK
    unroll = 3 if slots % 3 == 0 else 1
    return pl.pallas_call(
        functools.partial(pairs_kernel, float(regions), regions, unroll),
        out_shape=(
            jax.ShapeDtypeStruct((hidden, share), jnp.float32),
            jax.ShapeDtypeStruct((chans, share), jnp.bfloat16),
            jax.ShapeDtypeStruct((8, share), jnp.float32),
            jax.ShapeDtypeStruct((hidden, chans), jnp.bfloat16),
            jax.ShapeDtypeStruct(second.shape, jnp.bfloat16),
        ),
        in_specs=[SMEM_SPEC] * 4 + [ANY_SPEC] * 2 + [HBM_SPEC] * 4,
        out_specs=(VMEM_SPEC,) * 5,
        scratch_shapes=[
            pltpu.VMEM((rows, 3 * width), jnp.bfloat16),
            pltpu.VMEM(first.shape, jnp.bfloat16),
            pltpu.VMEM((count, 3, BLOCK, BLOCK), jnp.float32),
            pltpu.VMEM((3, 8, 3 * width), jnp.float32),
            pltpu.VMEM((count, BLOCK, unroll * BLOCK), jnp.bfloat16),
            pltpu.VMEM((count, chans, unroll * BLOCK), jnp.bfloat16),
            pltpu.VMEM((count, chans, BLOCK), jnp.float32),
            pltpu.SemaphoreType.DMA((9,)),
        ],
        compiler_params=PARAMS,
        cost_estimate=pl.CostEstimate(
            flops=work * (2 * chans + 20), bytes_accessed=6 * rows * width, transcendentals=work
        ),
        name="pairs",
    )(place, live_blocks, neighbours, live_slots, prev, following, *in_hbm(own, h, first, second))


def update_kernel(arrived_ref, inner_ref, share_ref, alive_ref, third_ref, second_ref, out_ref):
    potential = arrived_ref[0].astype(jnp.float32)
    for piece in range(1, arrived_ref.shape[0]):
        potential = potential + arrived_ref[piece].astype(jnp.float32)
    f32 = dict(preferred_element_type=jnp.float32)
    inner = inner_ref[...] + jnp.dot(third_ref[...], potential.astype(jnp.bfloat16), **f32)
    hidden = jax.nn.silu(inner).astype(jnp.bfloat16)
    out = share_ref[...].astype(jnp.float32) + jnp.dot(second_ref[...], hidden, **f32)
    new = jnp.where(alive_ref[0:1, :] > 0.0, out, 0.0).astype(jnp.bfloat16)
    for piece in range(out_ref.shape[0]):
        out_ref[piece] = new


def update(arrived, known):
    return pl.pallas_call(
        update_kernel,
        out_shape=jax.ShapeDtypeStruct(arrived.shape, jnp.bfloat16),
        in_specs=[VMEM_SPEC] * 6,
        out_specs=VMEM_SPEC,
        compiler_params=PARAMS,
        name="update",
    )(arrived, *known)


def laid_out(pieces, dim):
    lengths = list(pieces.shape[1:])
    lengths[dim] *= pieces.shape[0]
    return jnp.moveaxis(pieces, 0, dim).reshape(lengths)


def shifted(cells, regions, groups, step):
    pairs_of = []
    for region in range(regions):
        to = region + step
        turned = 0 if 0 <= to < regions else groups // 2
        for group in range(groups):
            pairs_of.append((region * groups + group, to % regions * groups + (group ^ turned)))
    return lax.ppermute(cells, ("atoms", "waves"), pairs_of)


def from_others(pieces, axis):
    return lax.all_to_all(pieces, axis, 0, 0, tiled=True)


def local(
    features,
    coords,
    neighbours,
    live_slots,
    block_count,
    kvec,
    msg_weight,
    filter_weight,
    mlp_in,
    mlp_out,
):
    _, width = features.shape
    nblocks = width // BLOCK
    regions = lax.axis_size("atoms")
    groups_waves = lax.axis_size("waves")
    here = lax.axis_index("atoms")
    per_group = nblocks // groups_waves
    first = lax.axis_index("waves") * per_group
    place = jnp.stack([here, first]).astype(jnp.int32)
    total = regions * width
    low, high, factor, sent, carry, gain_rows, mixing = structure(
        place, block_count, kvec, coords, features, msg_weight[0], filter_weight[0], 1.0 / math.sqrt(total), regions
    )
    first_cores, second_cores = range(0, regions, 2), range(1, regions, 2)
    exchanges = [[(i, i + 1) for i in first_cores]]
    exchanges += [[(i, i ^ flip) for i in second_cores] for flip in (2, 6, 8, 24)]
    for step, exchange in enumerate(exchanges):
        arrived = lax.ppermute(sent, "atoms", exchange)
        if step + 1 < len(exchanges):
            factor = factor + arrived.astype(jnp.float32)
            sent = factor.astype(jnp.bfloat16)
    prev = shifted(carry, regions, groups_waves, 1)
    following = shifted(carry, regions, groups_waves, -1)
    filtered = spectral(factor, arrived, gain_rows, mixing)
    other = lax.ppermute(filtered, "atoms", [(i, i - 1) for i in second_cores])
    partial_potential = potentials(place, filtered, other, low, high, groups_waves)
    potential = from_others(partial_potential, "waves")
    known = pairs(
        place, block_count, neighbours.T, live_slots.T, prev, carry, following,
        features, mlp_in[0].T, mlp_out[0], per_group, regions,
    )
    new = update(potential, known)
    return laid_out(from_others(new, "waves"), 1)


def solution(mesh):
    in_specs = (
        P(None, "atoms"),
        P(None, "atoms"),
        P(None, "atoms"),
        P(None, "atoms"),
        P("atoms"),
        P(None, "waves"),
        P(),
        P(),
        P(),
        P(),
    )
    out_specs = P(None, "atoms")
    return jax.shard_map(local, mesh=mesh, in_specs=in_specs, out_specs=out_specs, check_vma=False)
```

```python
import functools
import math

import jax
import jax.numpy as jnp
from jax import lax
from jax.experimental import pallas as pl
from jax.experimental.pallas import tpu as pltpu
from jax.sharding import PartitionSpec as P


K = 4096
BLOCK = 128

MSG_SCALE = 0.125
GAIN_TOP = 20.0
ALPHA = 8.0**0.25
SIN_COEFS = tuple(ALPHA / math.sqrt(2.0) * c for c in (2.221430356581745, -0.9131746556274619, 0.10983828651966959))
TILE = 256
ROWS = 128
LIMIT = 16 * 2**20
VMEM_SPEC = pl.BlockSpec(memory_space=pltpu.VMEM)
SMEM_SPEC = pl.BlockSpec(memory_space=pltpu.SMEM)
ANY_SPEC = pl.BlockSpec(memory_space=pl.ANY)
HBM_SPEC = pl.BlockSpec(memory_space=pltpu.HBM)
PARAMS = pltpu.CompilerParams(vmem_limit_bytes=LIMIT)
NT = (((1,), (1,)), ((), ()))
TN = (((0,), (0,)), ((), ()))


def kept_rows(waves):
    return waves * 3 // 4


def phases_of(turns):
    r = turns - jnp.round(turns)
    u = r * r
    s = r * ((SIN_COEFS[2] * u + SIN_COEFS[1]) * u + SIN_COEFS[0])
    q = s * s
    w = math.sqrt(8.0) - q
    return 1.0 - q * w, (s * (w * lax.rsqrt(w))) * (math.sqrt(2.0) - q)


def three_pieces(values):
    first = values.astype(jnp.bfloat16)
    rest = values - first.astype(jnp.float32)
    second = rest.astype(jnp.bfloat16)
    third = (rest - second.astype(jnp.float32)).astype(jnp.bfloat16)
    return first.astype(jnp.float32), second.astype(jnp.float32), third.astype(jnp.float32)


def structure_kernel(
    scale, regions, count_ref, kvec_in, coords_in, h_in, weight_in, mixing_in,
    low_ref, high_out, kept_ref, sent_ref, carry_out, gain_ref, mixing_ref,
    kvec_ref, coords_ref, h_ref, weight_ref, ka_ref, masked_ref, high_ref, carry_ref, whole_ref, gains_ref, in_sems, sems,
):
    waves = kvec_ref.shape[1]
    chans, atoms = h_ref.shape
    kept = low_ref.shape[0]
    half = kept_ref.shape[0]
    core = jnp.bitwise_and(lax.axis_index("atoms"), 1)
    mine = pl.ds(pl.multiple_of(core * half, half), half)
    theirs = pl.ds(pl.multiple_of((1 - core) * half, half), half)
    f32 = dict(preferred_element_type=jnp.float32)
    taken = [
        pltpu.make_async_copy(source, target, in_sems.at[at])
        for at, (source, target) in enumerate(
            (
                (kvec_in, kvec_ref),
                (coords_in, coords_ref),
                (h_in, h_ref),
                (weight_in, weight_ref),
                (mixing_in, mixing_ref),
            )
        )
    ]
    for copy in taken:
        copy.start()
    taken[0].wait()
    kf = kvec_ref[...].astype(jnp.float32)
    ahead, behind = jnp.zeros((3, waves), jnp.float32), jnp.zeros((2, waves), jnp.float32)
    ka = jnp.concatenate([part for axis in range(3) for part in (ahead, *(-kf[axis : axis + 1],) * 3, behind)], axis=0)
    ka_ref[...] = ka.T.astype(jnp.bfloat16)
    kx = kf[0:1] / regions
    gain = GAIN_TOP / (4.0 + kx * kx + kf[1:2] * kf[1:2] + kf[2:3] * kf[2:3])
    columns = jnp.broadcast_to(gain * scale, (8, waves)).T
    gains_ref[...] = jnp.broadcast_to(columns[:, 0:1], gains_ref.shape)
    gain_ref[...] = gains_ref[mine, :]
    taken[1].wait()
    pieces = three_pieces(coords_ref[...])
    ones, gap = jnp.ones((3, atoms), jnp.float32), jnp.zeros((2, atoms), jnp.float32)
    for axis in range(3):
        rows = jnp.concatenate([ones, *(-piece[axis : axis + 1] for piece in pieces), gap], axis=0)
        carry_ref[chans + 8 * axis : chans + 8 * axis + 8, :] = rows.astype(jnp.bfloat16)
    for copy in taken[2:]:
        copy.wait()
    live_atoms = count_ref[0] * BLOCK
    atom = lax.broadcasted_iota(jnp.int32, (chans, atoms), 1)
    masked_ref[...] = jnp.where(atom < live_atoms, h_ref[...].astype(jnp.float32), 0.0).astype(jnp.bfloat16)
    zero = jnp.zeros((chans, TILE), jnp.bfloat16)
    sums = {}

    def add_up(place, at, row, start):
        ht = masked_ref[:, start : start + TILE]
        cosv = place[at : at + ROWS, start : start + TILE]
        sinv = place[at : at + ROWS, atoms + start : atoms + start + TILE]
        term = lax.dot_general(cosv, jnp.concatenate([ht, zero], axis=0), NT, **f32)
        term = term + lax.dot_general(sinv, jnp.concatenate([zero, ht], axis=0), NT, **f32)
        sums[row] = term if start == 0 else sums[row] + term
        if start + TILE == atoms:
            whole_ref[row : row + ROWS, :] = sums.pop(row)

    pending = []
    copies = []
    for row in [*range(kept, waves, ROWS), *range(0, kept, ROWS)]:
        place, at = (low_ref, row) if row < kept else (high_ref, row - kept)
        if row == 0:
            copies = [
                pltpu.make_async_copy(high_ref, high_out, sems.at[0]),
                pltpu.make_async_copy(carry_ref, carry_out, sems.at[1]),
            ]
            for copy in copies:
                copy.start()
        for start in range(0, atoms, TILE):
            cos_span = slice(start, start + TILE)
            sin_span = slice(atoms + start, atoms + start + TILE)
            turns = jnp.dot(ka_ref[row : row + ROWS, :], carry_ref[chans:, cos_span], **f32)
            cosv, sinv = phases_of(turns)
            place[at : at + ROWS, cos_span] = cosv.astype(jnp.bfloat16)
            place[at : at + ROWS, sin_span] = sinv.astype(jnp.bfloat16)
            if row == kept:
                carry_ref[:chans, cos_span] = jnp.dot(weight_ref[...], h_ref[:, cos_span], **f32).astype(jnp.bfloat16)
            pending.append((place, at, row, start))
            if len(pending) > 1:
                add_up(*pending.pop(0))
    add_up(*pending.pop(0))
    kept_ref[...] = whole_ref[mine, :]
    sent_ref[...] = whole_ref[theirs, :].astype(jnp.bfloat16)
    for copy in copies:
        copy.wait()


def in_hbm(*arrays):
    return tuple(pltpu.with_memory_space_constraint(array, pltpu.HBM) for array in arrays)


def structure(count, kvec, coords, h, weight, mixing, scale, regions):
    waves, atoms, chans = kvec.shape[1], coords.shape[1], h.shape[0]
    kept = kept_rows(waves)
    return pl.pallas_call(
        functools.partial(structure_kernel, scale, float(regions)),
        out_shape=(
            jax.ShapeDtypeStruct((kept, 2 * atoms), jnp.bfloat16),
            pltpu.HBM((waves - kept, 2 * atoms), jnp.bfloat16),
            jax.ShapeDtypeStruct((waves // 2, 2 * chans), jnp.float32),
            jax.ShapeDtypeStruct((waves // 2, 2 * chans), jnp.bfloat16),
            pltpu.HBM((chans + 24, atoms), jnp.bfloat16),
            jax.ShapeDtypeStruct((waves // 2, 2 * chans), jnp.float32),
            jax.ShapeDtypeStruct(mixing.shape, jnp.float32),
        ),
        in_specs=[SMEM_SPEC] + [HBM_SPEC] * 5,
        out_specs=(VMEM_SPEC, HBM_SPEC, VMEM_SPEC, VMEM_SPEC, HBM_SPEC, VMEM_SPEC, VMEM_SPEC),
        scratch_shapes=[
            pltpu.VMEM(kvec.shape, jnp.int32),
            pltpu.VMEM(coords.shape, jnp.float32),
            pltpu.VMEM(h.shape, jnp.bfloat16),
            pltpu.VMEM(weight.shape, jnp.bfloat16),
            pltpu.VMEM((waves, 24), jnp.bfloat16),
            pltpu.VMEM(h.shape, jnp.bfloat16),
            pltpu.VMEM((waves - kept, 2 * atoms), jnp.bfloat16),
            pltpu.VMEM((chans + 24, atoms), jnp.bfloat16),
            pltpu.VMEM((waves, 2 * chans), jnp.float32),
            pltpu.VMEM((waves, 2 * chans), jnp.float32),
            pltpu.SemaphoreType.DMA((5,)),
            pltpu.SemaphoreType.DMA((2,)),
        ],
        compiler_params=PARAMS,
        name="structure",
    )(count, *in_hbm(kvec, coords, h, weight, mixing))


def spectral_kernel(kept_ref, arrived_ref, gain_ref, mixing_ref, out_ref):
    chans = mixing_ref.shape[0]
    factor = kept_ref[...] + arrived_ref[...].astype(jnp.float32)
    high = dict(precision=lax.Precision.HIGHEST, preferred_element_type=jnp.float32)
    mixing = mixing_ref[...]
    cos_part = jnp.dot(factor[:, :chans], mixing, **high)
    sin_part = jnp.dot(factor[:, chans:], mixing, **high)
    out_ref[...] = (jnp.concatenate([cos_part, sin_part], axis=1) * gain_ref[...]).astype(jnp.bfloat16)


def spectral(kept, arrived, gain, mixing):
    return pl.pallas_call(
        spectral_kernel,
        out_shape=jax.ShapeDtypeStruct(arrived.shape, jnp.bfloat16),
        in_specs=[VMEM_SPEC] * 4,
        out_specs=VMEM_SPEC,
        compiler_params=PARAMS,
        name="spectral",
    )(kept, arrived, gain, mixing)


def potentials_kernel(
    own_ref, other_ref, low_ref, high_in, out_ref, filtered_ref, high_ref, across_ref, sum_ref, sem,
):
    chans = out_ref.shape[1]
    pieces, _, width = out_ref.shape
    atoms = pieces * width
    kept, waves = low_ref.shape[0], filtered_ref.shape[0]
    copy = pltpu.make_async_copy(high_in, high_ref, sem)
    copy.start()
    half = own_ref.shape[0]
    core = jnp.bitwise_and(lax.axis_index("atoms"), 1)
    filtered_ref[pl.ds(pl.multiple_of(core * half, half), half), :] = own_ref[...]
    filtered_ref[pl.ds(pl.multiple_of((1 - core) * half, half), half), :] = other_ref[...]
    across_ref[...] = filtered_ref[...].astype(jnp.float32).T.astype(jnp.bfloat16)

    def term(rows, table, piece):
        cos_span = slice(piece * width, (piece + 1) * width)
        sin_span = slice(atoms + piece * width, atoms + (piece + 1) * width)
        f32 = dict(preferred_element_type=jnp.float32)
        return jnp.dot(across_ref[:chans, rows], table[:, cos_span], **f32) + jnp.dot(
            across_ref[chans:, rows], table[:, sin_span], **f32
        )

    for piece in range(pieces):
        sum_ref[piece] = term(slice(0, kept), low_ref, piece)
    copy.wait()
    for piece in range(pieces):
        whole = sum_ref[piece] + term(slice(kept, waves), high_ref, piece)
        out_ref[piece] = (whole * (1.0 / math.sqrt(K))).astype(jnp.bfloat16)


def potentials(own, other, low, high, pieces):
    chans = own.shape[1] // 2
    waves = 2 * own.shape[0]
    atoms = low.shape[1] // 2
    return pl.pallas_call(
        potentials_kernel,
        out_shape=jax.ShapeDtypeStruct((pieces, chans, atoms // pieces), jnp.bfloat16),
        in_specs=[VMEM_SPEC, VMEM_SPEC, VMEM_SPEC, HBM_SPEC],
        out_specs=VMEM_SPEC,
        scratch_shapes=[
            pltpu.VMEM((waves, 2 * chans), jnp.bfloat16),
            pltpu.VMEM(high.shape, jnp.bfloat16),
            pltpu.VMEM((2 * chans, waves), jnp.bfloat16),
            pltpu.VMEM((pieces, chans, atoms // pieces), jnp.float32),
            pltpu.SemaphoreType.DMA,
        ],
        compiler_params=PARAMS,
        name="potentials",
    )(own, other, low, *in_hbm(high))


def pairs_kernel(
    scale_x, regions, unroll, count_ref, idx_ref, live_ref, prev_in, next_in, own_in, h_in, first_in, second_in,
    inner_ref, share_ref, alive_ref, third_ref, second_ref,
    ext_ref, first_ref, own_ref, pos_ref, weights_ref, near_ref, sum_ref, sems,
):
    chans = h_in.shape[0]
    width = own_in.shape[1]
    nblocks = width // BLOCK
    slots = idx_ref.shape[1]
    count = share_ref.shape[1] // BLOCK
    here = lax.axis_index("atoms")
    first = lax.axis_index("waves") * count
    share = pl.ds(pl.multiple_of(first * BLOCK, BLOCK), count * BLOCK)
    moves = []
    for rows in (pl.ds(chans, ext_ref.shape[0] - chans), pl.ds(0, chans)):
        for at, source in enumerate((prev_in, own_in, next_in)):
            moves.append((source.at[rows, :], ext_ref.at[rows, pl.ds(at * width, width)]))
    moves += [(h_in.at[:, share], share_ref), (first_in, first_ref), (second_in, second_ref)]
    copies = [pltpu.make_async_copy(source, target, sems.at[at]) for at, (source, target) in enumerate(moves)]
    for copy in copies:
        copy.start()
    atom = lax.broadcasted_iota(jnp.int32, alive_ref.shape, 1) + first * BLOCK
    alive_ref[...] = jnp.where(atom < count_ref[0] * BLOCK, 1.0, 0.0)
    for copy in copies[:3]:
        copy.wait()
    f32 = dict(preferred_element_type=jnp.float32)
    column = lax.broadcasted_iota(jnp.int32, (8, 8), 1)
    pick = jnp.where((column >= 3) & (column < 6), 1.0, 0.0).astype(jnp.bfloat16)
    row = lax.broadcasted_iota(jnp.int32, (8, BLOCK), 0)
    lead = jnp.where(row < 3, 1.0, 0.0).astype(jnp.bfloat16)
    for axis in range(3):
        rows = slice(chans + 8 * axis, chans + 8 * axis + 8)
        for start in range(0, 3 * width, 4 * BLOCK):
            span = slice(start, start + 4 * BLOCK)
            pos_ref[axis, :, span] = jnp.dot(pick, ext_ref[rows, span], **f32)
    for block in range(count):
        at = pl.multiple_of((nblocks + first + block) * BLOCK, BLOCK)
        for axis in range(3):
            rows = ext_ref[chans + 8 * axis : chans + 8 * axis + 8, pl.ds(at, BLOCK)].astype(jnp.float32)
            swapped = jnp.concatenate([-rows[3:6], rows[0:3], rows[6:8]], axis=0)
            own_ref[block, axis] = jnp.dot(swapped.T.astype(jnp.bfloat16), lead, **f32)
        sum_ref[block] = jnp.zeros((chans, BLOCK), jnp.float32)
        weights_ref[block] = jnp.zeros(weights_ref.shape[1:], jnp.bfloat16)
        near_ref[block] = jnp.zeros(near_ref.shape[1:], jnp.bfloat16)
    for copy in copies[3:6]:
        copy.wait()
    exponent = -2.0 * math.log2(math.e)
    part_rows = 16

    def add_up(block):
        sum_ref[block] += lax.dot_general(near_ref[block], weights_ref[block], NT, **f32)

    def slots_step(step, carried):
        for block in range(count):
            add_up(block)
        for block in range(count):
            for part in range(unroll):
                slot = step * unroll + part
                entry = idx_ref[first + block, slot]
                where = jnp.bitwise_and(entry + (regions + 1 - here) * nblocks, regions * nblocks - 1)
                span = pl.ds(pl.multiple_of(where * BLOCK, BLOCK), BLOCK)
                to = slice(part * BLOCK, (part + 1) * BLOCK)
                used = live_ref[first + block, slot].astype(jnp.float32)
                mapped = ext_ref[:chans, span].astype(jnp.float32) * used
                near_ref[block, :, to] = mapped.astype(jnp.bfloat16)
                minus = [jnp.tile(pos_ref[axis, :, span], (part_rows // 8, 1)) for axis in range(3)]
                for start in range(0, BLOCK, part_rows):
                    rows = slice(start, start + part_rows)
                    total = None
                    for axis in range(3):
                        diff = own_ref[block, axis, rows, :] + minus[axis]
                        diff = diff - jnp.round(diff)
                        term = diff * diff
                        if axis == 0:
                            term = term * (scale_x * scale_x)
                        total = term if total is None else total + term
                    weights_ref[block, rows, to] = jnp.exp2(total * exponent).astype(jnp.bfloat16)
        return carried

    lax.fori_loop(0, slots // unroll, slots_step, 0)
    for copy in copies[6:]:
        copy.wait()
    outer = first_ref[: 2 * chans, :]
    third_ref[...] = first_ref[2 * chans :, :].astype(jnp.float32).T.astype(jnp.bfloat16)
    for block in range(count):
        add_up(block)
        span = slice(block * BLOCK, (block + 1) * BLOCK)
        msg = (sum_ref[block] * MSG_SCALE).astype(jnp.bfloat16)
        known = jnp.concatenate([share_ref[:, span], msg], axis=0)
        inner_ref[:, span] = lax.dot_general(outer, known, TN, **f32)


def pairs(live_blocks, neighbours, live_slots, prev, own, following, h, first, second, count, regions):
    rows, width = own.shape
    chans = h.shape[0]
    hidden = first.shape[1]
    slots = neighbours.shape[1]
    share = count * BLOCK
    work = slots * share * BLOCK
    unroll = 3 if slots % 3 == 0 else 1
    return pl.pallas_call(
        functools.partial(pairs_kernel, float(regions), regions, unroll),
        out_shape=(
            jax.ShapeDtypeStruct((hidden, share), jnp.float32),
            jax.ShapeDtypeStruct((chans, share), jnp.bfloat16),
            jax.ShapeDtypeStruct((8, share), jnp.float32),
            jax.ShapeDtypeStruct((hidden, chans), jnp.bfloat16),
            jax.ShapeDtypeStruct(second.shape, jnp.bfloat16),
        ),
        in_specs=[SMEM_SPEC] * 3 + [ANY_SPEC] * 2 + [HBM_SPEC] * 4,
        out_specs=(VMEM_SPEC,) * 5,
        scratch_shapes=[
            pltpu.VMEM((rows, 3 * width), jnp.bfloat16),
            pltpu.VMEM(first.shape, jnp.bfloat16),
            pltpu.VMEM((count, 3, BLOCK, BLOCK), jnp.float32),
            pltpu.VMEM((3, 8, 3 * width), jnp.float32),
            pltpu.VMEM((count, BLOCK, unroll * BLOCK), jnp.bfloat16),
            pltpu.VMEM((count, chans, unroll * BLOCK), jnp.bfloat16),
            pltpu.VMEM((count, chans, BLOCK), jnp.float32),
            pltpu.SemaphoreType.DMA((9,)),
        ],
        compiler_params=PARAMS,
        cost_estimate=pl.CostEstimate(
            flops=work * (2 * chans + 20), bytes_accessed=6 * rows * width, transcendentals=work
        ),
        name="pairs",
    )(live_blocks, neighbours, live_slots, prev, following, *in_hbm(own, h, first, second))


def update_kernel(arrived_ref, inner_ref, share_ref, alive_ref, third_ref, second_ref, out_ref):
    potential = arrived_ref[0].astype(jnp.float32)
    for piece in range(1, arrived_ref.shape[0]):
        potential = potential + arrived_ref[piece].astype(jnp.float32)
    f32 = dict(preferred_element_type=jnp.float32)
    inner = inner_ref[...] + jnp.dot(third_ref[...], potential.astype(jnp.bfloat16), **f32)
    hidden = jax.nn.silu(inner).astype(jnp.bfloat16)
    out = share_ref[...].astype(jnp.float32) + jnp.dot(second_ref[...], hidden, **f32)
    new = jnp.where(alive_ref[0:1, :] > 0.0, out, 0.0).astype(jnp.bfloat16)
    for piece in range(out_ref.shape[0]):
        out_ref[piece] = new


def update(arrived, known):
    return pl.pallas_call(
        update_kernel,
        out_shape=jax.ShapeDtypeStruct(arrived.shape, jnp.bfloat16),
        in_specs=[VMEM_SPEC] * 6,
        out_specs=VMEM_SPEC,
        compiler_params=PARAMS,
        name="update",
    )(arrived, *known)


def laid_out(pieces, dim):
    lengths = list(pieces.shape[1:])
    lengths[dim] *= pieces.shape[0]
    return jnp.moveaxis(pieces, 0, dim).reshape(lengths)


def shifted(cells, regions, groups, step):
    pairs_of = []
    for region in range(regions):
        to = region + step
        turned = 0 if 0 <= to < regions else groups // 2
        for group in range(groups):
            pairs_of.append((region * groups + group, to % regions * groups + (group ^ turned)))
    return lax.ppermute(cells, ("atoms", "waves"), pairs_of)


def from_others(pieces, axis):
    return lax.all_to_all(pieces, axis, 0, 0, tiled=True)


def local(
    features,
    coords,
    neighbours,
    live_slots,
    block_count,
    kvec,
    msg_weight,
    filter_weight,
    mlp_in,
    mlp_out,
):
    _, width = features.shape
    nblocks = width // BLOCK
    regions = lax.axis_size("atoms")
    groups_waves = lax.axis_size("waves")
    per_group = nblocks // groups_waves
    total = regions * width
    low, high, factor, sent, carry, gain_rows, mixing = structure(
        block_count, kvec, coords, features, msg_weight[0], filter_weight[0], 1.0 / math.sqrt(total), regions
    )
    exchanges = (1, 2, 6, 8, 16)
    for step, flip in enumerate(exchanges):
        arrived = lax.ppermute(sent, "atoms", [(i, i ^ flip) for i in range(regions)])
        if step + 1 < len(exchanges):
            factor = factor + arrived.astype(jnp.float32)
            sent = factor.astype(jnp.bfloat16)
    prev = shifted(carry, regions, groups_waves, 1)
    following = shifted(carry, regions, groups_waves, -1)
    filtered = spectral(factor, arrived, gain_rows, mixing)
    other = lax.ppermute(filtered, "atoms", [(i, i ^ 1) for i in range(regions)])
    partial_potential = potentials(filtered, other, low, high, groups_waves)
    potential = from_others(partial_potential, "waves")
    known = pairs(
        block_count, neighbours.T, live_slots.T, prev, carry, following,
        features, mlp_in[0].T, mlp_out[0], per_group, regions,
    )
    new = update(potential, known)
    return laid_out(from_others(new, "waves"), 1)


def solution(mesh):
    in_specs = (
        P(None, "atoms"),
        P(None, "atoms"),
        P(None, "atoms"),
        P(None, "atoms"),
        P("atoms"),
        P(None, "waves"),
        P(),
        P(),
        P(),
        P(),
    )
    out_specs = P(None, "atoms")
    return jax.shard_map(local, mesh=mesh, in_specs=in_specs, out_specs=out_specs, check_vma=False)
```

```python
import functools
import math

import jax
import jax.numpy as jnp
from jax import lax
from jax.experimental import pallas as pl
from jax.experimental.pallas import tpu as pltpu
from jax.sharding import PartitionSpec as P


K = 4096
BLOCK = 128

MSG_SCALE = 0.125
GAIN_TOP = 20.0
ALPHA = 8.0**0.25
SIN_COEFS = tuple(ALPHA / math.sqrt(2.0) * c for c in (2.221430356581745, -0.9131746556274619, 0.10983828651966959))
TILE = 256
ROWS = 128
LIMIT = 16 * 2**20
VMEM_SPEC = pl.BlockSpec(memory_space=pltpu.VMEM)
SMEM_SPEC = pl.BlockSpec(memory_space=pltpu.SMEM)
ANY_SPEC = pl.BlockSpec(memory_space=pl.ANY)
HBM_SPEC = pl.BlockSpec(memory_space=pltpu.HBM)
PARAMS = pltpu.CompilerParams(vmem_limit_bytes=LIMIT)
NT = (((1,), (1,)), ((), ()))
TN = (((0,), (0,)), ((), ()))


def kept_rows(waves):
    return waves * 3 // 4


def phases_of(turns):
    r = turns - jnp.round(turns)
    u = r * r
    s = r * ((SIN_COEFS[2] * u + SIN_COEFS[1]) * u + SIN_COEFS[0])
    q = s * s
    w = math.sqrt(8.0) - q
    return 1.0 - q * w, ((s * w) * (math.sqrt(2.0) - q)) * lax.rsqrt(w)


def three_pieces(values):
    first = values.astype(jnp.bfloat16)
    rest = values - first.astype(jnp.float32)
    second = rest.astype(jnp.bfloat16)
    third = (rest - second.astype(jnp.float32)).astype(jnp.bfloat16)
    return first.astype(jnp.float32), second.astype(jnp.float32), third.astype(jnp.float32)


def structure_kernel(
    scale, regions, count_ref, kvec_in, coords_in, h_in, weight_in, mixing_in,
    low_ref, high_out, kept_ref, sent_ref, carry_out, gain_ref, mixing_ref,
    kvec_ref, coords_ref, h_ref, weight_ref, ka_ref, masked_ref, high_ref, carry_ref, whole_ref, gains_ref, in_sems, sems,
):
    waves = kvec_ref.shape[1]
    chans, atoms = h_ref.shape
    kept = low_ref.shape[0]
    half = kept_ref.shape[0]
    core = jnp.bitwise_and(lax.axis_index("atoms"), 1)
    mine = pl.ds(pl.multiple_of(core * half, half), half)
    theirs = pl.ds(pl.multiple_of((1 - core) * half, half), half)
    f32 = dict(preferred_element_type=jnp.float32)
    taken = [
        pltpu.make_async_copy(source, target, in_sems.at[at])
        for at, (source, target) in enumerate(
            (
                (kvec_in, kvec_ref),
                (coords_in, coords_ref),
                (h_in, h_ref),
                (weight_in, weight_ref),
                (mixing_in, mixing_ref),
            )
        )
    ]
    for copy in taken:
        copy.start()
    taken[0].wait()
    kf = kvec_ref[...].astype(jnp.float32)
    ahead, behind = jnp.zeros((3, waves), jnp.float32), jnp.zeros((2, waves), jnp.float32)
    ka = jnp.concatenate([part for axis in range(3) for part in (ahead, *(-kf[axis : axis + 1],) * 3, behind)], axis=0)
    ka_ref[...] = ka.T.astype(jnp.bfloat16)
    kx = kf[0:1] / regions
    gain = GAIN_TOP / (4.0 + kx * kx + kf[1:2] * kf[1:2] + kf[2:3] * kf[2:3])
    columns = jnp.broadcast_to(gain * scale, (8, waves)).T
    gains_ref[...] = jnp.broadcast_to(columns[:, 0:1], gains_ref.shape)
    gain_ref[...] = gains_ref[mine, :]
    taken[1].wait()
    pieces = three_pieces(coords_ref[...])
    ones, gap = jnp.ones((3, atoms), jnp.float32), jnp.zeros((2, atoms), jnp.float32)
    for axis in range(3):
        rows = jnp.concatenate([ones, *(-piece[axis : axis + 1] for piece in pieces), gap], axis=0)
        carry_ref[chans + 8 * axis : chans + 8 * axis + 8, :] = rows.astype(jnp.bfloat16)
    for copy in taken[2:]:
        copy.wait()
    live_atoms = count_ref[0] * BLOCK
    atom = lax.broadcasted_iota(jnp.int32, (chans, atoms), 1)
    masked_ref[...] = jnp.where(atom < live_atoms, h_ref[...].astype(jnp.float32), 0.0).astype(jnp.bfloat16)
    zero = jnp.zeros((chans, TILE), jnp.bfloat16)
    sums = {}

    def add_up(place, at, row, start):
        ht = masked_ref[:, start : start + TILE]
        cosv = place[at : at + ROWS, start : start + TILE]
        sinv = place[at : at + ROWS, atoms + start : atoms + start + TILE]
        term = lax.dot_general(cosv, jnp.concatenate([ht, zero], axis=0), NT, **f32)
        term = term + lax.dot_general(sinv, jnp.concatenate([zero, ht], axis=0), NT, **f32)
        sums[row] = term if start == 0 else sums[row] + term
        if start + TILE == atoms:
            whole_ref[row : row + ROWS, :] = sums.pop(row)

    pending = []
    copies = []
    for row in [*range(kept, waves, ROWS), *range(0, kept, ROWS)]:
        place, at = (low_ref, row) if row < kept else (high_ref, row - kept)
        if row == 0:
            copies = [
                pltpu.make_async_copy(high_ref, high_out, sems.at[0]),
                pltpu.make_async_copy(carry_ref, carry_out, sems.at[1]),
            ]
            for copy in copies:
                copy.start()
        for start in range(0, atoms, TILE):
            cos_span = slice(start, start + TILE)
            sin_span = slice(atoms + start, atoms + start + TILE)
            turns = jnp.dot(ka_ref[row : row + ROWS, :], carry_ref[chans:, cos_span], **f32)
            cosv, sinv = phases_of(turns)
            place[at : at + ROWS, cos_span] = cosv.astype(jnp.bfloat16)
            place[at : at + ROWS, sin_span] = sinv.astype(jnp.bfloat16)
            if row == kept:
                carry_ref[:chans, cos_span] = jnp.dot(weight_ref[...], h_ref[:, cos_span], **f32).astype(jnp.bfloat16)
            pending.append((place, at, row, start))
            if len(pending) > 2:
                add_up(*pending.pop(0))
    for last in pending:
        add_up(*last)
    kept_ref[...] = whole_ref[mine, :]
    sent_ref[...] = whole_ref[theirs, :].astype(jnp.bfloat16)
    for copy in copies:
        copy.wait()


def in_hbm(*arrays):
    return tuple(pltpu.with_memory_space_constraint(array, pltpu.HBM) for array in arrays)


def structure(count, kvec, coords, h, weight, mixing, scale, regions):
    waves, atoms, chans = kvec.shape[1], coords.shape[1], h.shape[0]
    kept = kept_rows(waves)
    return pl.pallas_call(
        functools.partial(structure_kernel, scale, float(regions)),
        out_shape=(
            jax.ShapeDtypeStruct((kept, 2 * atoms), jnp.bfloat16),
            pltpu.HBM((waves - kept, 2 * atoms), jnp.bfloat16),
            jax.ShapeDtypeStruct((waves // 2, 2 * chans), jnp.float32),
            jax.ShapeDtypeStruct((waves // 2, 2 * chans), jnp.bfloat16),
            pltpu.HBM((chans + 24, atoms), jnp.bfloat16),
            jax.ShapeDtypeStruct((waves // 2, 2 * chans), jnp.float32),
            jax.ShapeDtypeStruct(mixing.shape, jnp.float32),
        ),
        in_specs=[SMEM_SPEC] + [HBM_SPEC] * 5,
        out_specs=(VMEM_SPEC, HBM_SPEC, VMEM_SPEC, VMEM_SPEC, HBM_SPEC, VMEM_SPEC, VMEM_SPEC),
        scratch_shapes=[
            pltpu.VMEM(kvec.shape, jnp.int32),
            pltpu.VMEM(coords.shape, jnp.float32),
            pltpu.VMEM(h.shape, jnp.bfloat16),
            pltpu.VMEM(weight.shape, jnp.bfloat16),
            pltpu.VMEM((waves, 24), jnp.bfloat16),
            pltpu.VMEM(h.shape, jnp.bfloat16),
            pltpu.VMEM((waves - kept, 2 * atoms), jnp.bfloat16),
            pltpu.VMEM((chans + 24, atoms), jnp.bfloat16),
            pltpu.VMEM((waves, 2 * chans), jnp.float32),
            pltpu.VMEM((waves, 2 * chans), jnp.float32),
            pltpu.SemaphoreType.DMA((5,)),
            pltpu.SemaphoreType.DMA((2,)),
        ],
        compiler_params=PARAMS,
        name="structure",
    )(count, *in_hbm(kvec, coords, h, weight, mixing))


def spectral_kernel(kept_ref, arrived_ref, gain_ref, mixing_ref, out_ref):
    chans = mixing_ref.shape[0]
    factor = kept_ref[...] + arrived_ref[...].astype(jnp.float32)
    high = dict(precision=lax.Precision.HIGHEST, preferred_element_type=jnp.float32)
    mixing = mixing_ref[...]
    cos_part = jnp.dot(factor[:, :chans], mixing, **high)
    sin_part = jnp.dot(factor[:, chans:], mixing, **high)
    out_ref[...] = (jnp.concatenate([cos_part, sin_part], axis=1) * gain_ref[...]).astype(jnp.bfloat16)


def spectral(kept, arrived, gain, mixing):
    return pl.pallas_call(
        spectral_kernel,
        out_shape=jax.ShapeDtypeStruct(arrived.shape, jnp.bfloat16),
        in_specs=[VMEM_SPEC] * 4,
        out_specs=VMEM_SPEC,
        compiler_params=PARAMS,
        name="spectral",
    )(kept, arrived, gain, mixing)


def potentials_kernel(
    own_ref, other_ref, low_ref, high_in, out_ref, filtered_ref, high_ref, across_ref, sum_ref, sem,
):
    chans = out_ref.shape[1]
    pieces, _, width = out_ref.shape
    atoms = pieces * width
    kept, waves = low_ref.shape[0], filtered_ref.shape[0]
    copy = pltpu.make_async_copy(high_in, high_ref, sem)
    copy.start()
    half = own_ref.shape[0]
    core = jnp.bitwise_and(lax.axis_index("atoms"), 1)
    filtered_ref[pl.ds(pl.multiple_of(core * half, half), half), :] = own_ref[...]
    filtered_ref[pl.ds(pl.multiple_of((1 - core) * half, half), half), :] = other_ref[...]
    across_ref[...] = filtered_ref[...].astype(jnp.float32).T.astype(jnp.bfloat16)

    def term(rows, table, piece):
        cos_span = slice(piece * width, (piece + 1) * width)
        sin_span = slice(atoms + piece * width, atoms + (piece + 1) * width)
        f32 = dict(preferred_element_type=jnp.float32)
        return jnp.dot(across_ref[:chans, rows], table[:, cos_span], **f32) + jnp.dot(
            across_ref[chans:, rows], table[:, sin_span], **f32
        )

    for piece in range(pieces):
        sum_ref[piece] = term(slice(0, kept), low_ref, piece)
    copy.wait()
    for piece in range(pieces):
        whole = sum_ref[piece] + term(slice(kept, waves), high_ref, piece)
        out_ref[piece] = (whole * (1.0 / math.sqrt(K))).astype(jnp.bfloat16)


def potentials(own, other, low, high, pieces):
    chans = own.shape[1] // 2
    waves = 2 * own.shape[0]
    atoms = low.shape[1] // 2
    return pl.pallas_call(
        potentials_kernel,
        out_shape=jax.ShapeDtypeStruct((pieces, chans, atoms // pieces), jnp.bfloat16),
        in_specs=[VMEM_SPEC, VMEM_SPEC, VMEM_SPEC, HBM_SPEC],
        out_specs=VMEM_SPEC,
        scratch_shapes=[
            pltpu.VMEM((waves, 2 * chans), jnp.bfloat16),
            pltpu.VMEM(high.shape, jnp.bfloat16),
            pltpu.VMEM((2 * chans, waves), jnp.bfloat16),
            pltpu.VMEM((pieces, chans, atoms // pieces), jnp.float32),
            pltpu.SemaphoreType.DMA,
        ],
        compiler_params=PARAMS,
        name="potentials",
    )(own, other, low, *in_hbm(high))


def pairs_kernel(
    scale_x, regions, unroll, count_ref, idx_ref, live_ref, prev_in, next_in, own_in, h_in, first_in, second_in,
    inner_ref, share_ref, alive_ref, third_ref, second_ref,
    ext_ref, first_ref, own_ref, pos_ref, weights_ref, near_ref, sum_ref, sems,
):
    chans = h_in.shape[0]
    width = own_in.shape[1]
    nblocks = width // BLOCK
    slots = idx_ref.shape[1]
    count = share_ref.shape[1] // BLOCK
    here = lax.axis_index("atoms")
    first = lax.axis_index("waves") * count
    share = pl.ds(pl.multiple_of(first * BLOCK, BLOCK), count * BLOCK)
    moves = []
    for rows in (pl.ds(chans, ext_ref.shape[0] - chans), pl.ds(0, chans)):
        for at, source in enumerate((prev_in, own_in, next_in)):
            moves.append((source.at[rows, :], ext_ref.at[rows, pl.ds(at * width, width)]))
    moves += [(h_in.at[:, share], share_ref), (first_in, first_ref), (second_in, second_ref)]
    copies = [pltpu.make_async_copy(source, target, sems.at[at]) for at, (source, target) in enumerate(moves)]
    for copy in copies:
        copy.start()
    atom = lax.broadcasted_iota(jnp.int32, alive_ref.shape, 1) + first * BLOCK
    alive_ref[...] = jnp.where(atom < count_ref[0] * BLOCK, 1.0, 0.0)
    for copy in copies[:3]:
        copy.wait()
    f32 = dict(preferred_element_type=jnp.float32)
    column = lax.broadcasted_iota(jnp.int32, (8, 8), 1)
    pick = jnp.where((column >= 3) & (column < 6), 1.0, 0.0).astype(jnp.bfloat16)
    row = lax.broadcasted_iota(jnp.int32, (8, BLOCK), 0)
    lead = jnp.where(row < 3, 1.0, 0.0).astype(jnp.bfloat16)
    for axis in range(3):
        rows = slice(chans + 8 * axis, chans + 8 * axis + 8)
        for start in range(0, 3 * width, 4 * BLOCK):
            span = slice(start, start + 4 * BLOCK)
            pos_ref[axis, :, span] = jnp.dot(pick, ext_ref[rows, span], **f32)
    for block in range(count):
        at = pl.multiple_of((nblocks + first + block) * BLOCK, BLOCK)
        for axis in range(3):
            rows = ext_ref[chans + 8 * axis : chans + 8 * axis + 8, pl.ds(at, BLOCK)].astype(jnp.float32)
            swapped = jnp.concatenate([-rows[3:6], rows[0:3], rows[6:8]], axis=0)
            own_ref[block, axis] = jnp.dot(swapped.T.astype(jnp.bfloat16), lead, **f32)
        sum_ref[block] = jnp.zeros((chans, BLOCK), jnp.float32)
        weights_ref[block] = jnp.zeros(weights_ref.shape[1:], jnp.bfloat16)
        near_ref[block] = jnp.zeros(near_ref.shape[1:], jnp.bfloat16)
    for copy in copies[3:6]:
        copy.wait()
    exponent = -2.0 * math.log2(math.e)
    part_rows = 16

    def add_up(block):
        sum_ref[block] += lax.dot_general(near_ref[block], weights_ref[block], NT, **f32)

    def slots_step(step, carried):
        for block in range(count):
            add_up(block)
        for block in range(count):
            for part in range(unroll):
                slot = step * unroll + part
                entry = idx_ref[first + block, slot]
                where = jnp.bitwise_and(entry + (regions + 1 - here) * nblocks, regions * nblocks - 1)
                span = pl.ds(pl.multiple_of(where * BLOCK, BLOCK), BLOCK)
                to = slice(part * BLOCK, (part + 1) * BLOCK)
                used = live_ref[first + block, slot].astype(jnp.float32)
                mapped = ext_ref[:chans, span].astype(jnp.float32) * used
                near_ref[block, :, to] = mapped.astype(jnp.bfloat16)
                minus = [jnp.tile(pos_ref[axis, :, span], (part_rows // 8, 1)) for axis in range(3)]
                for start in range(0, BLOCK, part_rows):
                    rows = slice(start, start + part_rows)
                    total = None
                    for axis in range(3):
                        diff = own_ref[block, axis, rows, :] + minus[axis]
                        diff = diff - jnp.round(diff)
                        term = diff * diff
                        if axis == 0:
                            term = term * (scale_x * scale_x)
                        total = term if total is None else total + term
                    weights_ref[block, rows, to] = jnp.exp2(total * exponent).astype(jnp.bfloat16)
        return carried

    lax.fori_loop(0, slots // unroll, slots_step, 0)
    for copy in copies[6:]:
        copy.wait()
    outer = first_ref[: 2 * chans, :]
    third_ref[...] = first_ref[2 * chans :, :].astype(jnp.float32).T.astype(jnp.bfloat16)
    for block in range(count):
        add_up(block)
        span = slice(block * BLOCK, (block + 1) * BLOCK)
        msg = (sum_ref[block] * MSG_SCALE).astype(jnp.bfloat16)
        known = jnp.concatenate([share_ref[:, span], msg], axis=0)
        inner_ref[:, span] = lax.dot_general(outer, known, TN, **f32)


def pairs(live_blocks, neighbours, live_slots, prev, own, following, h, first, second, count, regions):
    rows, width = own.shape
    chans = h.shape[0]
    hidden = first.shape[1]
    slots = neighbours.shape[1]
    share = count * BLOCK
    work = slots * share * BLOCK
    unroll = 3 if slots % 3 == 0 else 1
    return pl.pallas_call(
        functools.partial(pairs_kernel, float(regions), regions, unroll),
        out_shape=(
            jax.ShapeDtypeStruct((hidden, share), jnp.float32),
            jax.ShapeDtypeStruct((chans, share), jnp.bfloat16),
            jax.ShapeDtypeStruct((8, share), jnp.float32),
            jax.ShapeDtypeStruct((hidden, chans), jnp.bfloat16),
            jax.ShapeDtypeStruct(second.shape, jnp.bfloat16),
        ),
        in_specs=[SMEM_SPEC] * 3 + [ANY_SPEC] * 2 + [HBM_SPEC] * 4,
        out_specs=(VMEM_SPEC,) * 5,
        scratch_shapes=[
            pltpu.VMEM((rows, 3 * width), jnp.bfloat16),
            pltpu.VMEM(first.shape, jnp.bfloat16),
            pltpu.VMEM((count, 3, BLOCK, BLOCK), jnp.float32),
            pltpu.VMEM((3, 8, 3 * width), jnp.float32),
            pltpu.VMEM((count, BLOCK, unroll * BLOCK), jnp.bfloat16),
            pltpu.VMEM((count, chans, unroll * BLOCK), jnp.bfloat16),
            pltpu.VMEM((count, chans, BLOCK), jnp.float32),
            pltpu.SemaphoreType.DMA((9,)),
        ],
        compiler_params=PARAMS,
        cost_estimate=pl.CostEstimate(
            flops=work * (2 * chans + 20), bytes_accessed=6 * rows * width, transcendentals=work
        ),
        name="pairs",
    )(live_blocks, neighbours, live_slots, prev, following, *in_hbm(own, h, first, second))


def update_kernel(arrived_ref, inner_ref, share_ref, alive_ref, third_ref, second_ref, out_ref):
    potential = arrived_ref[0].astype(jnp.float32)
    for piece in range(1, arrived_ref.shape[0]):
        potential = potential + arrived_ref[piece].astype(jnp.float32)
    f32 = dict(preferred_element_type=jnp.float32)
    inner = inner_ref[...] + jnp.dot(third_ref[...], potential.astype(jnp.bfloat16), **f32)
    hidden = jax.nn.silu(inner).astype(jnp.bfloat16)
    out = share_ref[...].astype(jnp.float32) + jnp.dot(second_ref[...], hidden, **f32)
    new = jnp.where(alive_ref[0:1, :] > 0.0, out, 0.0).astype(jnp.bfloat16)
    for piece in range(out_ref.shape[0]):
        out_ref[piece] = new


def update(arrived, known):
    return pl.pallas_call(
        update_kernel,
        out_shape=jax.ShapeDtypeStruct(arrived.shape, jnp.bfloat16),
        in_specs=[VMEM_SPEC] * 6,
        out_specs=VMEM_SPEC,
        compiler_params=PARAMS,
        name="update",
    )(arrived, *known)


def laid_out(pieces, dim):
    lengths = list(pieces.shape[1:])
    lengths[dim] *= pieces.shape[0]
    return jnp.moveaxis(pieces, 0, dim).reshape(lengths)


def shifted(cells, regions, groups, step):
    pairs_of = []
    for region in range(regions):
        to = region + step
        turned = 0 if 0 <= to < regions else groups // 2
        for group in range(groups):
            pairs_of.append((region * groups + group, to % regions * groups + (group ^ turned)))
    return lax.ppermute(cells, ("atoms", "waves"), pairs_of)


def from_others(pieces, axis):
    return lax.all_to_all(pieces, axis, 0, 0, tiled=True)


def local(
    features,
    coords,
    neighbours,
    live_slots,
    block_count,
    kvec,
    msg_weight,
    filter_weight,
    mlp_in,
    mlp_out,
):
    _, width = features.shape
    nblocks = width // BLOCK
    regions = lax.axis_size("atoms")
    groups_waves = lax.axis_size("waves")
    per_group = nblocks // groups_waves
    total = regions * width
    low, high, factor, sent, carry, gain_rows, mixing = structure(
        block_count, kvec, coords, features, msg_weight[0], filter_weight[0], 1.0 / math.sqrt(total), regions
    )
    exchanges = (1, 2, 6, 8, 24)
    for step, flip in enumerate(exchanges):
        arrived = lax.ppermute(sent, "atoms", [(i, i ^ flip) for i in range(regions)])
        if step + 1 < len(exchanges):
            factor = factor + arrived.astype(jnp.float32)
            sent = factor.astype(jnp.bfloat16)
    prev = shifted(carry, regions, groups_waves, 1)
    following = shifted(carry, regions, groups_waves, -1)
    filtered = spectral(factor, arrived, gain_rows, mixing)
    other = lax.ppermute(filtered, "atoms", [(i, i ^ 1) for i in range(regions)])
    partial_potential = potentials(filtered, other, low, high, groups_waves)
    potential = from_others(partial_potential, "waves")
    known = pairs(
        block_count, neighbours.T, live_slots.T, prev, carry, following,
        features, mlp_in[0].T, mlp_out[0], per_group, regions,
    )
    new = update(potential, known)
    return laid_out(from_others(new, "waves"), 1)


def solution(mesh):
    in_specs = (
        P(None, "atoms"),
        P(None, "atoms"),
        P(None, "atoms"),
        P(None, "atoms"),
        P("atoms"),
        P(None, "waves"),
        P(),
        P(),
        P(),
        P(),
    )
    out_specs = P(None, "atoms")
    return jax.shard_map(local, mesh=mesh, in_specs=in_specs, out_specs=out_specs, check_vma=False)
```
